32 devices in a mesh: orb: 8 (over z, x), slab: 4 (over y, core).
Axes of the slice: x: 2, y: 2, z: 4, core: 2. Of those that a mesh axis runs over, the one named last changes fastest.
Arguments:
- orbitals: bfloat16 [8, 64, 64, 128], P('orb', 'slab'), may hold values from -6 to 6
- pair_table: int32 [64, 3], P('orb'), may hold values from -1 to 7, as said below
Outputs:
- exchange_action: float32 [8, 64, 64, 128], P('orb', 'slab')
The draws below stay inside these ranges and needn't reach their ends.
Inputs may be any that keep to these rules, and one draw needn't show every extreme that they name: `pair_table`: A live slot holds (m, n, s) with m <= n and s in 0, 1; an empty slot holds -1 in all three columns. A block of 8 slots has its live slots first. No (m, n, s) appears twice in the table. Exactly 36 slots are live, and the 8 blocks hold, in some order, k * 1 live slots for k = 1 to 8.
All inputs are finite; a program needn't handle non-finite values.
Results may differ from the reference program's by a relative error of at most 0.0003.
Values may be sent and summed in bfloat16 or wider, within the bound.
A program may use at most 64 MiB of HBM per device.

```python
import math
import jax
import jax.numpy as jnp
from jax import lax

G = 64
CP_DEV = 1
COUPLES = 8
N_ORB = 8


def draw_pair_table(key, part):
    couples = CP_DEV * N_ORB
    capacity = couples
    blocks = N_ORB
    upper_rows, upper_cols = jnp.triu_indices(couples)
    combos = upper_rows.shape[0] * 2
    shuffled = jax.random.permutation(jax.random.fold_in(key, 11), combos)
    ranking = jax.random.permutation(jax.random.fold_in(key, 12), blocks)
    counts = capacity * (ranking + 1) // blocks
    starts = jnp.cumsum(counts) - counts
    slot_index = jnp.arange(blocks * capacity, dtype=jnp.int32)
    block_of = slot_index // capacity
    column = slot_index % capacity
    is_live = column < counts[block_of]
    chosen = shuffled[jnp.where(is_live, starts[block_of] + column, 0)]
    pair_index = chosen // 2
    result_rows = jnp.stack([upper_rows[pair_index], upper_cols[pair_index], chosen % 2], axis=1).astype(jnp.int32)
    return jnp.where(is_live[:, None], result_rows, -1).astype(jnp.int32)


def steps_of(rng, extent, split, least, largest):
    level, own = 1.0, jax.random.fold_in(rng, 6)
    for dim, blocks in split:
        draws = jnp.exp(jax.random.uniform(jax.random.fold_in(own, dim), (blocks,), jnp.float32, least / len(split), largest / len(split)))
        level = level * jnp.repeat(draws, extent[dim] // blocks).reshape([-1 if axis == dim else 1 for axis in range(len(extent))])
    return level


def scatter_about(key, extent, deviation, bound, split=(), kind=jnp.bfloat16):
    gain = steps_of(key, extent, split, -0.22, 0.18) if split else 1.0
    array = jax.random.normal(key, extent, jnp.float32) * deviation * gain
    return jnp.minimum(jnp.maximum(array, -bound), bound).astype(kind)


def setup_inputs(seed: int = 0) -> dict:
    streams_of = jax.random.split(jax.random.key(seed), 3)
    orbitals = scatter_about(streams_of[0], (COUPLES, G, G, 2 * G), 1.0, 6.0, ((0, 8), (1, 4)))
    pair_table = draw_pair_table(jax.random.fold_in(streams_of[2], 71), 0)
    return dict(orbitals=orbitals, pair_table=pair_table)


exchange_fraction = 0.25
cell_ratio = 8.0


def folded(values, grid_len):
    return jnp.minimum(values, grid_len - values)


def kernel_half(grid_len):
    full_axis = folded(jnp.arange(grid_len, dtype=jnp.int32), grid_len).astype(jnp.float32)
    planes_x = cell_ratio * full_axis
    half_axis = jnp.arange(grid_len // 2 + 1, dtype=jnp.int32).astype(jnp.float32)
    scale_k = (2.0 * math.pi / grid_len) * (2.0 * math.pi / grid_len)
    squared = scale_k * (planes_x[:, None, None] * planes_x[:, None, None]
                         + full_axis[None, :, None] * full_axis[None, :, None]
                         + half_axis[None, None, :] * half_axis[None, None, :])
    safe_sq = jnp.where(squared > 0, squared, 1.0)
    return jnp.where(squared > 0, -exchange_fraction / safe_sq, 0.0)


def lane_swap(field_in, grid_len):
    return jnp.concatenate([field_in[..., grid_len:], field_in[..., :grid_len]], axis=-1)


def to_lanes(field_in, grid_len):
    return field_in.reshape(grid_len, grid_len, 2, grid_len).transpose(2, 0, 1, 3)


def from_lanes(field_in, grid_len):
    return field_in.transpose(1, 2, 0, 3).reshape(grid_len, grid_len, 2 * grid_len)


def reference(orbitals, pair_table):
    couples = orbitals.shape[0]
    grid_len = orbitals.shape[1]
    kernel = kernel_half(grid_len)

    def add_slot(totals, row_vals):
        first_id = row_vals[0]
        second_id = row_vals[1]
        left_rows = orbitals[first_id].astype(jnp.float32)
        right_rows = orbitals[second_id].astype(jnp.float32)
        partner = jnp.where(row_vals[2] == 1, lane_swap(right_rows, grid_len), right_rows)
        density = to_lanes(left_rows * partner, grid_len)
        spectrum = jnp.fft.rfftn(density, axes=(1, 2, 3))
        potential = jnp.fft.irfftn(spectrum * kernel[None], s=(grid_len, grid_len, grid_len), axes=(1, 2, 3))
        potential = from_lanes(potential.astype(left_rows.dtype), grid_len)
        first_term = potential * partner
        second_term = potential * left_rows
        second_term = jnp.where(row_vals[2] == 1, lane_swap(second_term, grid_len), second_term)
        totals = totals.at[first_id].add(first_term)
        return totals.at[second_id].add(jnp.where(first_id != second_id, second_term, 0.0))

    def visit(slot_index, totals):
        row_vals = pair_table[slot_index]
        return lax.cond(row_vals[0] >= 0, lambda acc_in: add_slot(acc_in, row_vals), lambda acc_in: acc_in, totals)

    totals = lax.fori_loop(0, pair_table.shape[0], visit, jnp.zeros(orbitals.shape, jnp.float32))
    orbital_count = 2 * couples
    cell_count = grid_len * grid_len * grid_len
    orbital_grid = orbitals.astype(jnp.float32).reshape(couples, grid_len, grid_len, 2, grid_len)
    orbital_grid = orbital_grid.transpose(0, 3, 1, 2, 4).reshape(orbital_count, cell_count)
    actions = totals.reshape(couples, grid_len, grid_len, 2, grid_len)
    actions = actions.transpose(0, 3, 1, 2, 4).reshape(orbital_count, cell_count)
    intersection = lax.dot_general(orbital_grid, actions, (((1,), (1,)), ((), ())), precision=lax.Precision.HIGHEST) / cell_count
    corrected = actions - lax.dot_general(intersection, orbital_grid, (((0,), (0,)), ((), ())), precision=lax.Precision.HIGHEST)
    corrected = corrected.reshape(couples, 2, grid_len, grid_len, grid_len).transpose(0, 2, 3, 1, 4)
    return corrected.reshape(orbitals.shape)
```

```python
import functools
import math

import jax
import jax.numpy as jnp
import numpy as np
from jax import lax
from jax.experimental import pallas as pl
from jax.experimental.pallas import tpu as pltpu
from jax.sharding import PartitionSpec as P

exchange_fraction = 0.25
cell_ratio = 8.0
MESH = pl.DeviceIdType.MESH
VMEM_SPEC = pl.BlockSpec(memory_space=pltpu.VMEM)
ANY_SPEC = pl.BlockSpec(memory_space=pl.ANY)


def folded(values, grid_len):
    return jnp.minimum(values, grid_len - values).astype(jnp.float32)


def hartley(grid_len):
    rows_idx = np.arange(grid_len)
    angles = 2.0 * math.pi / grid_len * (rows_idx[:, None] * rows_idx[None, :] % grid_len)
    return ((np.cos(angles) + np.sin(angles)) / math.sqrt(grid_len)).astype(np.float32)


def split_const(values):
    high = values.astype(jnp.bfloat16)
    return high, (values - high.astype(np.float32)).astype(jnp.bfloat16)


def split(values):
    high = values.astype(jnp.bfloat16)
    low = (values - high.astype(jnp.float32)).astype(jnp.bfloat16)
    return high, low


def coulomb(grid_len, slab_len, slab_index):
    planes_x = cell_ratio * folded(jnp.arange(grid_len, dtype=jnp.int32), grid_len)
    rows_y = folded(slab_index * slab_len + jnp.arange(slab_len, dtype=jnp.int32), grid_len)
    depth_z = folded(jnp.arange(2 * grid_len, dtype=jnp.int32) % grid_len, grid_len)
    scale_k = 2.0 * math.pi / grid_len * (2.0 * math.pi / grid_len)
    squared = scale_k * (
        planes_x[:, None, None] * planes_x[:, None, None]
        + rows_y[None, :, None] * rows_y[None, :, None]
        + depth_z[None, None, :] * depth_z[None, None, :]
    )
    safe_sq = jnp.where(squared > 0, squared, 1.0)
    return jnp.where(squared > 0, -exchange_fraction / safe_sq, 0.0)


def axis_parts(count):
    inner = 1
    while inner * inner * 4 <= count and count % (inner * 2) == 0:
        inner *= 2
    return count // inner, inner


def peer(index):
    return {"orb": index}


def greet_all(count, me):
    barrier = pltpu.get_barrier_semaphore()
    for step in range(1, count):
        pl.semaphore_signal(
            barrier, inc=1, device_id=peer(lax.rem(me + step, count)), device_id_type=MESH
        )
    pl.semaphore_wait(barrier, count - 1)


def table_kernel(count, table_ref, tables_ref, send_sem, recv_sem):
    me = lax.axis_index("orb")
    greet_all(count, me)

    def tab_copy(step):
        return pltpu.make_async_remote_copy(
            src_ref=table_ref, dst_ref=tables_ref.at[me], send_sem=send_sem.at[step - 1],
            recv_sem=recv_sem.at[step - 1], device_id=peer(lax.rem(me + step, count)),
            device_id_type=MESH)

    for step in range(1, count):
        tab_copy(step).start()
    tables_ref[me] = table_ref[...]
    for step in range(1, count):
        tab_copy(step).wait_recv()
    for step in range(1, count):
        tab_copy(step).wait_send()


def gather_tables(table, count):
    dma = pltpu.SemaphoreType.DMA
    return pl.pallas_call(
        functools.partial(table_kernel, count),
        out_shape=jax.ShapeDtypeStruct((count,) + table.shape, table.dtype),
        in_specs=[VMEM_SPEC],
        out_specs=VMEM_SPEC,
        scratch_shapes=[dma((count - 1,)), dma((count - 1,))],
        compiler_params=pltpu.CompilerParams(collective_id=0, has_side_effects=True),
    )(table)


def depth_turn(rows, depth_ref):
    width = rows.shape[1]
    high, low = split(rows)
    both = jnp.dot(jnp.concatenate([high, low], axis=1), depth_ref[...],
                   preferred_element_type=jnp.float32)
    return both[:, :width] + both[:, width:]


def pair_turn(first, second, left_ref):
    high, low = split(jnp.concatenate([first, second], axis=1))
    return jnp.dot(left_ref[...], jnp.concatenate([high, low, high], axis=0),
                   preferred_element_type=jnp.float32)


def greet_both(n_orb, n_slab, me, me_slab):
    barrier = pltpu.get_barrier_semaphore()
    for step in range(1, n_orb):
        pl.semaphore_signal(barrier, inc=1, device_id=peer(lax.rem(me + step, n_orb)),
                            device_id_type=MESH)
    for step in range(1, n_slab):
        pl.semaphore_signal(barrier, inc=1, device_id={"slab": lax.rem(me_slab + step, n_slab)},
                            device_id_type=MESH)
    pl.semaphore_wait(barrier, n_orb + n_slab - 2)


def chunk_count(slab_len, most):
    return max(1, min(most, slab_len // 2))


def advance_kernel(n_orb, n_slab, chunks, grid_len, ids_ref, own_ref, depth_ref, turn_ref,
                   basis_ref, out_ref, *scratch):
    held = scratch[:chunks]
    (spectra, keep_sem, stay_sem, up_send, up_recv, down_send, down_recv, side_send, side_recv,
     cross_send, cross_recv) = scratch[chunks:]
    outer, inner = axis_parts(n_orb)
    me, me_slab = lax.axis_index("orb"), lax.axis_index("slab")
    z_pos, x_pos = me // inner, me % inner
    couples_own = own_ref.shape[0]
    slots, _, slab_len, width = out_ref.shape
    planes = slab_len // chunks
    rows = planes * grid_len
    greet_both(n_orb, n_slab, me, me_slab)

    def mine(chunk):
        return own_ref.at[:, pl.ds(chunk * rows, rows)]

    def place(chunk, z_at):
        return held[chunk].at[pl.ds((z_at * inner + x_pos) * couples_own, couples_own)]

    def up_copy(chunk, step, src):
        return pltpu.make_async_remote_copy(
            src_ref=src, dst_ref=place(chunk, z_pos - step), send_sem=up_send.at[chunk, step],
            recv_sem=up_recv.at[chunk, step], device_id=peer((z_pos + 1) * inner + x_pos),
            device_id_type=MESH)

    def down_copy(chunk, step, src):
        return pltpu.make_async_remote_copy(
            src_ref=src, dst_ref=place(chunk, z_pos + step), send_sem=down_send.at[chunk, step],
            recv_sem=down_recv.at[chunk, step], device_id=peer((z_pos - 1) * inner + x_pos),
            device_id_type=MESH)

    def side_copy(chunk, hop, z_at, src):
        return pltpu.make_async_remote_copy(
            src_ref=src, dst_ref=place(chunk, z_at), send_sem=side_send.at[chunk, hop - 1, z_at],
            recv_sem=side_recv.at[chunk, hop - 1, z_at],
            device_id=peer(z_pos * inner + lax.rem(x_pos + hop, inner)), device_id_type=MESH)

    def keep_copy(chunk):
        return pltpu.make_async_copy(mine(chunk), place(chunk, z_pos), keep_sem.at[chunk])

    def cross_copy(chunk, hop):
        to = lax.rem(me_slab + hop, n_slab)
        return pltpu.make_async_remote_copy(
            src_ref=spectra.at[chunk, :, :,
                               pl.ds(pl.multiple_of(to * slab_len, slab_len), slab_len)],
            dst_ref=out_ref.at[:, pl.ds(me_slab * slab_len + chunk * planes, planes)],
            send_sem=cross_send.at[chunk, hop - 1], recv_sem=cross_recv.at[chunk, hop - 1],
            device_id={"slab": to}, device_id_type=MESH)

    def stay_copy(chunk):
        return pltpu.make_async_copy(
            spectra.at[chunk, :, :,
                       pl.ds(pl.multiple_of(me_slab * slab_len, slab_len), slab_len)],
            out_ref.at[:, pl.ds(me_slab * slab_len + chunk * planes, planes)],
            stay_sem.at[chunk])

    has_up, has_down = z_pos + 1 < outer, z_pos >= 1

    for chunk in range(chunks):
        @pl.when(has_up)
        def _():
            up_copy(chunk, 0, mine(chunk)).start()

        @pl.when(has_down)
        def _():
            down_copy(chunk, 0, mine(chunk)).start()

        for hop in range(1, inner):
            side_copy(chunk, hop, z_pos, mine(chunk)).start()
        keep_copy(chunk).start()

    def relay(chunk, step):
        @pl.when(z_pos - step >= 0)
        def _():
            got = place(chunk, z_pos - step)
            up_copy(chunk, step - 1, got).wait_recv()

            @pl.when(has_up)
            def _():
                up_copy(chunk, step, got).start()

            for hop in range(1, inner):
                side_copy(chunk, hop, z_pos - step, got).start()

        @pl.when(z_pos + step < outer)
        def _():
            got = place(chunk, z_pos + step)
            down_copy(chunk, step - 1, got).wait_recv()

            @pl.when(has_down)
            def _():
                down_copy(chunk, step, got).start()

            for hop in range(1, inner):
                side_copy(chunk, hop, z_pos + step, got).start()

    def compute(chunk):
        keep_copy(chunk).wait()
        for hop in range(1, inner):
            for z_at in range(outer):
                side_copy(chunk, hop, z_at, mine(chunk)).wait_recv()

        @pl.loop(0, slots)
        def _(slot):
            left = held[chunk][ids_ref[slot, 0]].astype(jnp.float32)
            right = held[chunk][ids_ref[slot, 1]].astype(jnp.float32)
            flipped = ids_ref[slot, 2] == 1
            partner = jnp.where(flipped, pltpu.roll(right, grid_len, 1), right)
            density = jnp.where(ids_ref[slot, 3] == 1, left * partner, 0.0)
            flat = depth_turn(density, depth_ref)
            for x_at in range(0, planes, 2):
                low, mid, high = x_at * grid_len, (x_at + 1) * grid_len, (x_at + 2) * grid_len
                done = pair_turn(flat[low:mid], flat[mid:high], turn_ref)
                spectra[chunk, slot, x_at] = done[:, :width]
                spectra[chunk, slot, x_at + 1] = done[:, width:]

        for hop in range(1, n_slab):
            cross_copy(chunk, hop).start()
        stay_copy(chunk).start()
        basis_ref[:, chunk * rows:(chunk + 1) * rows] = held[chunk][...]

    for wave in range(1, chunks + outer - 1):
        for step in range(outer - 1, 0, -1):
            if 0 <= wave - step < chunks:
                relay(wave - step, step)
        if wave - (outer - 1) >= 0:
            compute(wave - (outer - 1))

    for chunk in range(chunks):
        stay_copy(chunk).wait()
        for hop in range(1, n_slab):
            cross_copy(chunk, hop).wait_recv()
            cross_copy(chunk, hop).wait_send()
        for hop in range(1, inner):
            for z_at in range(outer):
                side_copy(chunk, hop, z_at, mine(chunk)).wait_send()
        for step in range(outer):
            @pl.when(has_up & (z_pos - step >= 0))
            def _():
                up_copy(chunk, step, mine(chunk)).wait_send()

            @pl.when(has_down & (z_pos + step < outer))
            def _():
                down_copy(chunk, step, mine(chunk)).wait_send()


def advance(ids, own, depth_mat, turn_mat, grid_len, n_orb, n_slab):
    outer, inner = axis_parts(n_orb)
    slots = ids.shape[0]
    couples_own, all_rows, width = own.shape
    slab_len = all_rows // grid_len
    chunks = chunk_count(slab_len, 4)
    planes = slab_len // chunks
    rows = planes * grid_len
    sides, slabs = max(inner - 1, 1), max(n_slab - 1, 1)
    dma, vmem, f32 = pltpu.SemaphoreType.DMA, pltpu.VMEM, jnp.float32
    return pl.pallas_call(
        functools.partial(advance_kernel, n_orb, n_slab, chunks, grid_len),
        out_shape=(jax.ShapeDtypeStruct((n_orb * couples_own, all_rows, width), own.dtype),
                   jax.ShapeDtypeStruct((slots, grid_len, slab_len, width), f32)),
        in_specs=[pl.BlockSpec(memory_space=pltpu.SMEM)] + [VMEM_SPEC] * 3,
        out_specs=(VMEM_SPEC, VMEM_SPEC),
        scratch_shapes=[vmem((n_orb * couples_own, rows, width), own.dtype)] * chunks + [
            vmem((chunks, slots, planes, grid_len, width), f32),
            dma((chunks,)), dma((chunks,)),
            dma((chunks, outer)), dma((chunks, outer)), dma((chunks, outer)), dma((chunks, outer)),
            dma((chunks, sides, outer)), dma((chunks, sides, outer)),
            dma((chunks, slabs)), dma((chunks, slabs)),
        ],
        compiler_params=pltpu.CompilerParams(collective_id=2, has_side_effects=True),
    )(ids, own, depth_mat, turn_mat)


def middle_kernel(grid_len, slab_len, in_ref, kernel_ref, turn_ref, out_ref):
    width = in_ref.shape[2]
    for row in range(0, slab_len, 2):
        one = pl.ds(row, grid_len, stride=slab_len)
        two = pl.ds(row + 1, grid_len, stride=slab_len)
        done = pair_turn(in_ref[0, one, :], in_ref[0, two, :], turn_ref)
        back = pair_turn(done[:, :width] * kernel_ref[one, :], done[:, width:] * kernel_ref[two, :],
                         turn_ref)
        out_ref[0, one, :] = back[:, :width]
        out_ref[0, two, :] = back[:, width:]


def return_kernel(n_orb, n_slab, chunks, couples_own, ids_ref, weights_ref, solved_ref, basis_ref,
                  depth_ref, turn_ref, out_ref, back, terms, flat_ref, parts, side_in, line_in, sums,
                  keep_sem, back_send, back_recv, side_send, side_recv, line_send, line_recv):
    outer, inner = axis_parts(n_orb)
    me, me_slab = lax.axis_index("orb"), lax.axis_index("slab")
    z_pos, x_pos = me // inner, me % inner
    slots, grid_len, slab_len, width = solved_ref.shape
    planes = slab_len // chunks
    rows = planes * grid_len

    greet_both(n_orb, n_slab, me, me_slab)
    own_rows = pl.ds(pl.multiple_of(me_slab * slab_len, slab_len), slab_len)

    def back_copy(chunk, hop):
        to = lax.rem(me_slab + hop, n_slab)
        return pltpu.make_async_remote_copy(
            src_ref=solved_ref.at[:, pl.ds(to * slab_len + chunk * planes, planes)],
            dst_ref=back.at[chunk, :, :, own_rows],
            send_sem=back_send.at[chunk, hop - 1], recv_sem=back_recv.at[chunk, hop - 1],
            device_id={"slab": to}, device_id_type=MESH)

    def keep_copy(chunk):
        return pltpu.make_async_copy(
            solved_ref.at[:, pl.ds(me_slab * slab_len + chunk * planes, planes)],
            back.at[chunk, :, :, own_rows], keep_sem.at[chunk])

    def side_copy(chunk, hop, turn):
        z_at = lax.rem(z_pos + turn, outer)
        x_to = lax.rem(x_pos + hop, inner)
        return pltpu.make_async_remote_copy(
            src_ref=parts.at[chunk, z_at * inner + x_to], dst_ref=side_in.at[chunk, hop - 1, turn],
            send_sem=side_send.at[chunk, hop - 1, turn], recv_sem=side_recv.at[chunk, hop - 1, turn],
            device_id=peer(z_pos * inner + x_to), device_id_type=MESH)

    def line_copy(chunk, turn):
        z_at = lax.rem(z_pos + turn, outer)
        return pltpu.make_async_remote_copy(
            src_ref=sums.at[chunk, turn], dst_ref=line_in.at[chunk, turn - 1],
            send_sem=line_send.at[chunk, turn - 1], recv_sem=line_recv.at[chunk, turn - 1],
            device_id=peer(z_at * inner + x_pos), device_id_type=MESH)

    order = list(range(1, outer)) + [0]

    def compute(chunk):
        keep_copy(chunk).wait()
        for hop in range(1, n_slab):
            back_copy(chunk, hop).wait_recv()

        @pl.loop(0, slots)
        def _(slot):
            for x_at in range(0, planes, 2):
                done = pair_turn(back[chunk, slot, x_at], back[chunk, slot, x_at + 1], turn_ref)
                flat_ref[x_at * grid_len:(x_at + 1) * grid_len] = done[:, :width]
                flat_ref[(x_at + 1) * grid_len:(x_at + 2) * grid_len] = done[:, width:]
            potential = depth_turn(flat_ref[...], depth_ref)
            flipped = ids_ref[slot, 2] == 1
            span = pl.ds(chunk * rows, rows)
            right = basis_ref[ids_ref[slot, 1], span].astype(jnp.float32)
            left = basis_ref[ids_ref[slot, 0], span].astype(jnp.float32)
            terms[2 * slot] = potential * jnp.where(flipped, pltpu.roll(right, grid_len, 1), right)
            second = potential * left
            terms[2 * slot + 1] = jnp.where(flipped, pltpu.roll(second, grid_len, 1), second)

        tile = 32

        @pl.loop(0, rows // tile)
        def _(at):
            here = pl.ds(pl.multiple_of(at * tile, tile), tile)

            @pl.loop(0, n_orb)
            def _(owner):
                for k in range(couples_own):
                    total = jnp.zeros((tile, width), jnp.float32)
                    for term in range(2 * slots):
                        total += weights_ref[owner * couples_own + k, term] * terms[term, here]
                    parts[chunk, owner, k, here] = total

        for turn in order:
            for hop in range(1, inner):
                side_copy(chunk, hop, turn).start()

    def forward(chunk):
        for turn in order:
            merged = parts[chunk, lax.rem(z_pos + turn, outer) * inner + x_pos]
            for hop in range(1, inner):
                side_copy(chunk, hop, turn).wait_recv()
                merged = merged + side_in[chunk, hop - 1, turn]
            sums[chunk, turn] = merged
            if turn:
                line_copy(chunk, turn).start()

    for chunk in range(chunks):
        for hop in range(1, n_slab):
            back_copy(chunk, hop).start()
        keep_copy(chunk).start()
    for chunk in range(chunks):
        compute(chunk)
        if chunk:
            forward(chunk - 1)
    forward(chunks - 1)
    for chunk in range(chunks):
        total = sums[chunk, 0]
        for turn in range(1, outer):
            line_copy(chunk, turn).wait_recv()
            total = total + line_in[chunk, turn - 1]
        out_ref[:, chunk * rows:(chunk + 1) * rows] = total
    for chunk in range(chunks):
        for hop in range(1, n_slab):
            back_copy(chunk, hop).wait_send()
        for turn in range(outer):
            for hop in range(1, inner):
                side_copy(chunk, hop, turn).wait_send()
            if turn:
                line_copy(chunk, turn).wait_send()


def return_sum(ids, weights, solved, basis, depth_mat, turn_mat, n_orb, n_slab):
    outer, inner = axis_parts(n_orb)
    slots, grid_len, slab_len, width = solved.shape
    couples_own = basis.shape[0] // n_orb
    chunks = chunk_count(slab_len, 8)
    planes = slab_len // chunks
    rows = planes * grid_len
    sides, lines = max(inner - 1, 1), max(outer - 1, 1)
    dma, vmem, f32 = pltpu.SemaphoreType.DMA, pltpu.VMEM, jnp.float32
    smem = pl.BlockSpec(memory_space=pltpu.SMEM)
    block = (couples_own, rows, width)
    return pl.pallas_call(
        functools.partial(return_kernel, n_orb, n_slab, chunks, couples_own),
        out_shape=jax.ShapeDtypeStruct((couples_own, slab_len * grid_len, width), f32),
        in_specs=[smem, smem] + [VMEM_SPEC] * 4,
        out_specs=VMEM_SPEC,
        scratch_shapes=[
            vmem((chunks, slots, planes, grid_len, width), f32),
            vmem((2 * slots, rows, width), f32),
            vmem((rows, width), f32),
            vmem((chunks, n_orb) + block, f32),
            vmem((chunks, sides, outer) + block, f32),
            vmem((chunks, lines) + block, f32),
            vmem((chunks, outer) + block, f32),
            dma((chunks,)),
            dma((chunks, max(n_slab - 1, 1))), dma((chunks, max(n_slab - 1, 1))),
            dma((chunks, sides, outer)), dma((chunks, sides, outer)),
            dma((chunks, lines)), dma((chunks, lines)),
        ],
        compiler_params=pltpu.CompilerParams(collective_id=1, has_side_effects=True),
    )(ids, weights, solved, basis, depth_mat, turn_mat)


def local(orbitals, pair_table, n_orb, n_slab):
    couples_own, slab_len, grid_len, width = orbitals.shape
    rows = slab_len * grid_len
    capacity = pair_table.shape[0]
    couples = couples_own * n_orb
    padded = jnp.pad(pair_table, ((0, 0), (0, 128 - pair_table.shape[1])), constant_values=-1)
    tables = gather_tables(padded, n_orb)
    table = tables.reshape(n_orb * capacity, 128)[:, :3]

    live_total = sum(capacity * (k + 1) // n_orb for k in range(n_orb))
    per_device = -(-live_total // n_orb)
    is_live = table[:, 0] >= 0
    places = jnp.arange(n_orb * capacity, dtype=jnp.int32)
    ahead = (places[None, :] < places[:, None]) & is_live[None, :]
    rank = jnp.sum(ahead.astype(jnp.int32), axis=1)
    wanted = jnp.arange(per_device, dtype=jnp.int32) * n_orb + lax.axis_index("orb")
    hits = (rank[None, :] == wanted[:, None]) & is_live[None, :]
    picked = jnp.sum(jnp.where(hits[:, :, None], table[None], 0), axis=1)
    used = jnp.any(hits, axis=1).astype(jnp.int32)
    ids = jnp.concatenate([picked, used[:, None]], axis=1)

    mat = hartley(grid_len)
    mat_high, mat_low = split_const(mat)
    turn_mat = jnp.asarray(np.concatenate([mat_high, mat_high, mat_low], axis=1))
    deep_high, deep_low = split_const(np.kron(np.eye(2, dtype=np.float32), mat))
    depth_mat = jnp.asarray(np.block([[deep_high, deep_low],
                                      [deep_high, np.zeros_like(deep_low)]]))
    kernel = coulomb(grid_len, slab_len, lax.axis_index("slab")).reshape(grid_len * slab_len, width)

    def whole(shape):
        return pl.BlockSpec(shape, lambda j, *ids: (0,) * len(shape))

    slot_spec = pl.BlockSpec((1, rows, width), lambda j, *ids: (j, 0, 0))
    slots_shape = jax.ShapeDtypeStruct((per_device, rows, width), jnp.float32)

    gathered, crossed = advance(ids, orbitals.reshape(couples_own, rows, width), depth_mat,
                                turn_mat, grid_len, n_orb, n_slab)
    solved = pl.pallas_call(
        functools.partial(middle_kernel, grid_len, slab_len),
        out_shape=slots_shape,
        grid=(per_device,),
        in_specs=[slot_spec, whole(kernel.shape), whole(turn_mat.shape)],
        out_specs=slot_spec,
    )(crossed.reshape(per_device, rows, width), kernel, turn_mat)
    couple_ids = jnp.arange(couples, dtype=jnp.int32)[:, None]
    first_on = (couple_ids == ids[None, :, 0]) & (ids[None, :, 3] == 1)
    second_on = (couple_ids == ids[None, :, 1]) & (ids[None, :, 3] == 1) & (
        ids[None, :, 0] != ids[None, :, 1])
    weights = jnp.stack([first_on, second_on], axis=2).reshape(couples, 2 * per_device)
    own = return_sum(ids, weights.astype(jnp.float32),
                     solved.reshape(per_device, grid_len, slab_len, width),
                     gathered, depth_mat, turn_mat, n_orb, n_slab)
    own = own.reshape(couples_own, rows, width)
    cell_count = grid_len * grid_len * grid_len

    def swap(values):
        return jnp.concatenate([values[..., grid_len:], values[..., :grid_len]], axis=-1)

    def lanes(values):
        summed = values.reshape(values.shape[:-1] + (2, grid_len)).sum(axis=-1)
        return jnp.repeat(summed, grid_len, axis=-1)

    basis = gathered.astype(jnp.float32)
    turned = swap(own)
    straight = jnp.sum(basis[None] * own[:, None], axis=2)
    across = jnp.sum(basis[None] * turned[:, None], axis=2)
    both = lax.psum(lanes(jnp.stack([straight, across])) / cell_count, "slab")
    kept = jnp.sum(both[0][:, :, None, :] * basis[None], axis=1)
    moved = jnp.sum(both[1][:, :, None, :] * basis[None], axis=1)
    return (own - kept - swap(moved)).reshape(orbitals.shape)


def solution(mesh):
    placed = (P("orb", "slab", None, None), P("orb", None))
    return jax.shard_map(
        functools.partial(local, n_orb=mesh.shape["orb"], n_slab=mesh.shape["slab"]),
        mesh=mesh, in_specs=placed, out_specs=P("orb", "slab", None, None), check_vma=False
    )
```

```python
import functools
import math

import jax
import jax.numpy as jnp
import numpy as np
from jax import lax
from jax.experimental import pallas as pl
from jax.experimental.pallas import tpu as pltpu
from jax.sharding import PartitionSpec as P

exchange_fraction = 0.25
cell_ratio = 8.0
lines_own = 8
code_peak = 32760.0
MESH = pl.DeviceIdType.MESH
VMEM_SPEC = pl.BlockSpec(memory_space=pltpu.VMEM)
f32 = jnp.float32


def hartley(grid_len):
    rows_idx = np.arange(grid_len)
    angles = 2.0 * math.pi / grid_len * (rows_idx[:, None] * rows_idx[None, :] % grid_len)
    return ((np.cos(angles) + np.sin(angles)) / math.sqrt(grid_len)).astype(np.float32)


def split_const(values):
    high = values.astype(jnp.bfloat16)
    return high, (values - high.astype(np.float32)).astype(jnp.bfloat16)


def split(values):
    high = values.astype(jnp.bfloat16)
    low = (values - high.astype(f32)).astype(jnp.bfloat16)
    return high, low


def depth_turn(rows, depth_ref):
    width = rows.shape[1]
    high, low = split(rows)
    both = jnp.dot(jnp.concatenate([high, low], axis=1), depth_ref[...],
                   preferred_element_type=f32)
    return both[:, :width] + both[:, width:]


def pair_turn(first, second, left_ref):
    high, low = split(jnp.concatenate([first, second], axis=1))
    return jnp.dot(left_ref[...], jnp.concatenate([high, low, high], axis=0),
                   preferred_element_type=f32)


def encode(block):
    peak = jnp.max(jnp.abs(block), axis=0, keepdims=True)
    inverse = jnp.where(peak > 1e-34, code_peak / jnp.maximum(peak, 1e-34), 0.0)
    return jnp.round(block * inverse).astype(jnp.int32).astype(jnp.int16), peak * (1.0 / code_peak)


def decode(code, unit):
    return code.astype(jnp.int32).astype(f32) * unit


def remote(src, dst, send_sem, recv_sem, device):
    return pltpu.make_async_remote_copy(src_ref=src, dst_ref=dst, send_sem=send_sem, recv_sem=recv_sem,
                                        device_id=device, device_id_type=MESH)


def action_kernel(n_orb, n_slab, half, slots, chunks, grid_len, table_ref, own_ref, depth_ref,
                  turn_ref, out_ref, *scratch):
    held = scratch[:chunks]
    (tab_own, tables, tab_s, starts, ids, chosen, gain, kern, fsend, funit, frecv, frunit, work, turned,
     bsend, bunit, brecv, brunit, terms, parts, rsend, runit, rrecv, rrunit, sums, overlap, overlap_in,
     coef, ysend,
     tab_sem, tab_send, tab_recv, own_sem, g_send, g_recv, stay_sem, f_send, f_recv, keep_sem, b_send,
     b_recv, r_send, r_recv, p_send, p_recv, y_send, y_recv) = scratch[chunks:]
    me, me_slab = lax.axis_index("orb"), lax.axis_index("slab")
    group, part = me // half, me % half
    groups, members = n_orb // half, n_slab * half
    place = me_slab * half + part
    own_couples, _, width = own_ref.shape
    couples = n_orb * own_couples
    shared = half * own_couples
    capacity = table_ref.shape[1]
    lines = grid_len // members
    planes = grid_len // members // chunks
    rows = planes * grid_len
    tile = planes * lines

    def line_peer(step):
        return {"orb": lax.rem(me + step, n_orb)}

    def member(step):
        to = lax.rem(place + step, members)
        return to, {"orb": group * half + to % half, "slab": to // half}

    barrier = pltpu.get_barrier_semaphore()
    for step in range(1, n_orb):
        pl.semaphore_signal(barrier, inc=1, device_id=line_peer(step), device_id_type=MESH)
    for slab_step in range(1, n_slab):
        for other in range(half):
            pl.semaphore_signal(
                barrier, inc=1, device_id={"orb": group * half + other,
                                           "slab": lax.rem(me_slab + slab_step, n_slab)},
                device_id_type=MESH)
    pl.semaphore_wait(barrier, n_orb - 1 + (n_slab - 1) * half)

    def plane_rows(which, chunk):
        return pl.ds(pl.multiple_of((which * chunks + chunk) * rows, rows), rows)

    def tab_copy(step):
        return remote(tab_own, tables.at[me], tab_send.at[step - 1], tab_recv.at[step - 1],
                      line_peer(step))

    def gather_copy(chunk, step):
        to = lax.rem(me + step, n_orb)
        return remote(own_ref.at[:, plane_rows(to % half, chunk)],
                      held[chunk].at[pl.ds(me * own_couples, own_couples)],
                      g_send.at[chunk, step - 1], g_recv.at[chunk, step - 1], line_peer(step))

    def own_copy(chunk):
        return pltpu.make_async_copy(own_ref.at[:, plane_rows(part, chunk)],
                                     held[chunk].at[pl.ds(me * own_couples, own_couples)],
                                     own_sem.at[chunk])

    def fwd_copies(chunk, step):
        to, device = member(step)
        return (remote(fsend.at[chunk, to], frecv.at[:, place, chunk], f_send.at[0, chunk, step - 1],
                       f_recv.at[0, chunk, step - 1], device),
                remote(funit.at[chunk, to], frunit.at[place, chunk], f_send.at[1, chunk, step - 1],
                       f_recv.at[1, chunk, step - 1], device))

    def fwd_stay(chunk):
        return (pltpu.make_async_copy(fsend.at[chunk, place], frecv.at[:, place, chunk],
                                      stay_sem.at[0, chunk]),
                pltpu.make_async_copy(funit.at[chunk, place], frunit.at[place, chunk],
                                      stay_sem.at[1, chunk]))

    def back_copies(chunk, step):
        to, device = member(step)
        return (remote(bsend.at[chunk, to], brecv.at[chunk, place], b_send.at[0, chunk, step - 1],
                       b_recv.at[0, chunk, step - 1], device),
                remote(bunit.at[chunk, to], brunit.at[chunk, place], b_send.at[1, chunk, step - 1],
                       b_recv.at[1, chunk, step - 1], device))

    def back_stay(chunk):
        return (pltpu.make_async_copy(bsend.at[chunk, place], brecv.at[chunk, place],
                                      keep_sem.at[0, chunk]),
                pltpu.make_async_copy(bunit.at[chunk, place], brunit.at[chunk, place],
                                      keep_sem.at[1, chunk]))

    def sum_copies(chunk, step):
        to = lax.rem(group + step, groups)
        theirs = pl.ds(to * shared, shared)
        device = {"orb": to * half + part}
        return (remote(rsend.at[chunk, theirs], rrecv.at[chunk, step - 1], r_send.at[0, chunk, step - 1],
                       r_recv.at[0, chunk, step - 1], device),
                remote(runit.at[chunk, theirs], rrunit.at[chunk, step - 1], r_send.at[1, chunk, step - 1],
                       r_recv.at[1, chunk, step - 1], device))

    def overlap_copy(step):
        return remote(overlap, overlap_in.at[step - 1], p_send.at[step - 1], p_recv.at[step - 1],
                      member(step)[1])

    def result_copy(chunk, hop):
        to = lax.rem(part + hop, half)
        return remote(ysend.at[chunk, pl.ds(to * own_couples, own_couples)],
                      out_ref.at[:, plane_rows(part, chunk)], y_send.at[chunk, hop - 1],
                      y_recv.at[chunk, hop - 1], {"orb": group * half + to})

    tab_own[...] = jnp.full(tab_own.shape, -1, jnp.int32)
    tab_own[0:3, 0:capacity] = table_ref[...]
    for step in range(1, n_orb):
        tab_copy(step).start()
    for chunk in range(chunks):
        for step in range(1, n_orb):
            gather_copy(chunk, step).start()
        own_copy(chunk).start()
    tables[me] = tab_own[...]

    kz = lax.broadcasted_iota(jnp.int32, (grid_len, width), 1) % grid_len
    fz = jnp.minimum(kz, grid_len - kz).astype(f32)
    ky = lax.broadcasted_iota(jnp.int32, (grid_len, width), 0)
    fy = jnp.minimum(ky, grid_len - ky).astype(f32)
    plane_sq = fy * fy + fz * fz
    deep = cell_ratio * cell_ratio
    gain[...] = 1.0 / jnp.where(plane_sq > 0, plane_sq, deep)
    fx = cell_ratio * fy
    scale_k = (2.0 * math.pi / grid_len) * (2.0 * math.pi / grid_len)
    for line in range(lines):
        at = place * lines + line
        fl = jnp.minimum(at, grid_len - at).astype(f32)
        plane = fl * fl + fz * fz
        whole = fx * fx + plane
        level = jnp.where(plane > 0, plane, deep)
        kern[line * grid_len:(line + 1) * grid_len] = jnp.where(
            whole > 0, (-exchange_fraction / scale_k) * level / jnp.where(whole > 0, whole, 1.0), 0.0)
    terms[2 * slots] = jnp.zeros(terms.shape[1:], f32)
    overlap[...] = jnp.zeros(overlap.shape, f32)
    for chunk in range(chunks):
        for ref in (funit, bunit):
            ref[chunk] = jnp.zeros(ref.shape[1:], f32)

    for step in range(1, n_orb):
        tab_copy(step).wait_recv()
    to_scalars = pltpu.make_async_copy(tables, tab_s, tab_sem)
    to_scalars.start()
    to_scalars.wait()

    def count_block(block, total):
        starts[block] = total
        return lax.fori_loop(
            0, capacity, lambda k, sum_in: sum_in + (tab_s[block, 0, k] >= 0).astype(jnp.int32), total)

    live = lax.fori_loop(0, n_orb, count_block, jnp.int32(0))

    @pl.loop(0, slots)
    def _(slot):
        wanted = slot * groups + group
        used = wanted < live
        block = lax.fori_loop(
            1, n_orb, lambda b, sum_in: sum_in + (starts[b] <= wanted).astype(jnp.int32), jnp.int32(0))
        column = jnp.clip(wanted - starts[block], 0, capacity - 1)
        for k in range(3):
            ids[slot, k] = jnp.maximum(tab_s[block, k, column], 0)
        first = jnp.where(used, tab_s[block, 0, column], -1)
        second = jnp.where(used, tab_s[block, 1, column], -1)

        @pl.loop(0, couples)
        def _(couple):
            chosen[couple, slot] = jnp.where(
                first == couple, 2 * slot, jnp.where(second == couple, 2 * slot + 1, 2 * slots))

    def pair_of(chunk, slot):
        left = held[chunk][ids[slot, 0]].astype(f32)
        right = held[chunk][ids[slot, 1]].astype(f32)
        flipped = ids[slot, 2] == 1
        return left, jnp.where(flipped, pltpu.roll(right, grid_len, 1), right), flipped

    def advance(chunk):
        own_copy(chunk).wait()
        for step in range(1, n_orb):
            gather_copy(chunk, step).wait_recv()

        @pl.loop(0, slots)
        def _(slot):
            left, partner, _ = pair_of(chunk, slot)
            flat = depth_turn(left * partner, depth_ref)
            done = pair_turn(flat[:grid_len], flat[grid_len:], turn_ref)
            one, two = done[:, :width] * gain[...], done[:, width:] * gain[...]
            for to in range(members):
                span = slice(to * lines, (to + 1) * lines)
                code, unit = encode(jnp.concatenate([one[span], two[span]], axis=0))
                fsend[chunk, to, slot] = code
                funit[chunk, to, pl.ds(slot, 1)] = unit

        for step in range(1, members):
            for copy in fwd_copies(chunk, step):
                copy.start()
        for copy in fwd_stay(chunk):
            copy.start()

    for chunk in range(chunks):
        advance(chunk)

    for chunk in range(chunks):
        for copy in fwd_stay(chunk):
            copy.wait()
        for step in range(1, members):
            for copy in fwd_copies(chunk, step):
                copy.wait_recv()

    @pl.loop(0, slots)
    def _(slot):
        for src in range(members):
            for chunk in range(chunks):
                at = (src * chunks + chunk) * tile
                work[at:at + tile] = decode(frecv[slot, src, chunk], frunit[src, chunk, pl.ds(slot, 1)])
        for line in range(0, lines, 2):
            one, two = pl.ds(line, grid_len, stride=lines), pl.ds(line + 1, grid_len, stride=lines)
            low, mid, high = line * grid_len, (line + 1) * grid_len, (line + 2) * grid_len
            done = pair_turn(work[one, :], work[two, :], turn_ref)
            back = pair_turn(done[:, :width] * kern[low:mid], done[:, width:] * kern[mid:high], turn_ref)
            turned[one, :] = back[:, :width]
            turned[two, :] = back[:, width:]
        for to in range(members):
            for chunk in range(chunks):
                at = (to * chunks + chunk) * tile
                code, unit = encode(turned[at:at + tile])
                bsend[chunk, to, slot] = code
                bunit[chunk, to, pl.ds(slot, 1)] = unit

    for chunk in range(chunks):
        for step in range(1, members):
            for copy in back_copies(chunk, step):
                copy.start()
        for copy in back_stay(chunk):
            copy.start()

    def retreat(chunk):
        for copy in back_stay(chunk):
            copy.wait()
        for step in range(1, members):
            for copy in back_copies(chunk, step):
                copy.wait_recv()

        @pl.loop(0, slots)
        def _(slot):
            blocks = [decode(brecv[chunk, src, slot], brunit[chunk, src, pl.ds(slot, 1)])
                      for src in range(members)]
            done = pair_turn(jnp.concatenate([block[:lines] for block in blocks], axis=0),
                             jnp.concatenate([block[lines:] for block in blocks], axis=0), turn_ref)
            potential = depth_turn(jnp.concatenate([done[:, :width], done[:, width:]], axis=0), depth_ref)
            left, partner, flipped = pair_of(chunk, slot)
            terms[2 * slot] = potential * partner
            second = potential * left
            terms[2 * slot + 1] = jnp.where(flipped, pltpu.roll(second, grid_len, 1), second)

        @pl.loop(0, couples)
        def _(couple):
            total = terms[chosen[couple, 0]]
            for slot in range(1, slots):
                total = total + terms[chosen[couple, slot]]
            parts[chunk, couple] = total
            code, unit = encode(total)
            rsend[chunk, couple] = code
            runit[chunk, couple] = jnp.broadcast_to(unit, runit.shape[2:])

        for step in range(1, groups):
            for copy in sum_copies(chunk, step):
                copy.start()

    def collect(chunk):
        for step in range(1, groups):
            for copy in sum_copies(chunk, step):
                copy.wait_recv()
        for k in range(shared):
            total = parts[chunk, group * shared + k]
            for step in range(1, groups):
                total = total + decode(rrecv[chunk, step - 1, k], rrunit[chunk, step - 1, k, 0:1])
            sums[chunk, k] = total
            across = pltpu.roll(total, grid_len, 1)

            @pl.loop(0, couples)
            def _(couple):
                basis = held[chunk][couple].astype(f32)
                for kind, field in enumerate((total, across)):
                    at = pl.ds((kind * shared + k) * couples + couple, 1)
                    overlap[at] += jnp.sum(basis * field, axis=0, keepdims=True)

    for chunk in range(chunks):
        retreat(chunk)
        if chunk:
            collect(chunk - 1)
    collect(chunks - 1)

    for step in range(1, members):
        overlap_copy(step).start()
    total = overlap[...]
    for step in range(1, members):
        overlap_copy(step).wait_recv()
        total = total + overlap_in[step - 1]
    total = total * (1.0 / (grid_len * grid_len * grid_len))
    lane = lax.broadcasted_iota(jnp.int32, total.shape, 1)
    lower = jnp.sum(jnp.where(lane < grid_len, total, 0.0), axis=1, keepdims=True)
    upper = jnp.sum(jnp.where(lane < grid_len, 0.0, total), axis=1, keepdims=True)
    coef[...] = jnp.where(lane < grid_len, lower, upper)

    strip = rows // 4
    for chunk in range(chunks):
        @pl.loop(0, rows // strip)
        def _(at):
            here = pl.ds(pl.multiple_of(at * strip, strip), strip)
            kept = [jnp.zeros((strip, width), f32) for _ in range(2 * shared)]
            for couple in range(couples):
                basis = held[chunk][couple, here].astype(f32)
                for k in range(2 * shared):
                    row = k * couples + couple
                    kept[k] = kept[k] + coef[row:row + 1] * basis
            for k in range(shared):
                ysend[chunk, k, here] = (sums[chunk, k, here] - kept[k]
                                         - pltpu.roll(kept[shared + k], grid_len, 1))

        for hop in range(1, half):
            result_copy(chunk, hop).start()
        out_ref[:, plane_rows(part, chunk)] = ysend[chunk, pl.ds(part * own_couples, own_couples)]

    for chunk in range(chunks):
        for hop in range(1, half):
            result_copy(chunk, hop).wait()
        for step in range(1, members):
            for copy in fwd_copies(chunk, step) + back_copies(chunk, step):
                copy.wait_send()
        for step in range(1, groups):
            for copy in sum_copies(chunk, step):
                copy.wait_send()
        for step in range(1, n_orb):
            gather_copy(chunk, step).wait_send()
    for step in range(1, members):
        overlap_copy(step).wait_send()
    for step in range(1, n_orb):
        tab_copy(step).wait_send()


def local(orbitals, pair_table, n_orb, n_slab):
    own_couples, slab_len, grid_len, width = orbitals.shape
    capacity = pair_table.shape[0]
    half = max(1, grid_len // (lines_own * n_slab))
    members = n_slab * half
    groups = n_orb // half
    live_total = sum(capacity * (k + 1) // n_orb for k in range(n_orb))
    slots = -(-live_total // groups)
    couples, shared = n_orb * own_couples, half * own_couples
    lines = grid_len // members
    chunks = lines // 2
    rows, tile = 2 * grid_len, 2 * lines
    slots_pad = -(-slots // 8) * 8
    tab_lanes = -(-capacity // 128) * 128

    mat = hartley(grid_len)
    mat_high, mat_low = split_const(mat)
    turn_mat = jnp.asarray(np.concatenate([mat_high, mat_high, mat_low], axis=1))
    deep_high, deep_low = split_const(np.kron(np.eye(2, dtype=np.float32), mat))
    depth_mat = jnp.asarray(np.block([[deep_high, deep_low], [deep_high, np.zeros_like(deep_low)]]))

    dma, vmem, smem = pltpu.SemaphoreType.DMA, pltpu.VMEM, pltpu.SMEM
    i32, i16 = jnp.int32, jnp.int16
    coded = vmem((chunks, members, slots, tile, width), i16)
    units = vmem((chunks, members, slots_pad, width), f32)
    lines_sem = dma((chunks, n_orb - 1))
    cross_sem = dma((2, chunks, members - 1))
    steps = max(groups - 1, 1)
    sum_sem = dma((2, chunks, steps))
    hops = max(half - 1, 1)
    out = pl.pallas_call(
        functools.partial(action_kernel, n_orb, n_slab, half, slots, chunks, grid_len),
        out_shape=jax.ShapeDtypeStruct((own_couples, slab_len * grid_len, width), f32),
        in_specs=[VMEM_SPEC] * 4,
        out_specs=VMEM_SPEC,
        scratch_shapes=[vmem((couples, rows, width), orbitals.dtype)] * chunks + [
            vmem((8, tab_lanes), i32), vmem((n_orb, 8, tab_lanes), i32), smem((n_orb, 8, tab_lanes), i32),
            smem((n_orb,), i32), smem((slots, 3), i32), smem((couples, slots), i32),
            vmem((grid_len, width), f32), vmem((lines * grid_len, width), f32),
            coded, units,
            vmem((slots, members, chunks, tile, width), i16), vmem((members, chunks, slots_pad, width), f32),
            vmem((lines * grid_len, width), f32), vmem((lines * grid_len, width), f32),
            coded, units, coded, units,
            vmem((2 * slots + 1, rows, width), f32),
            vmem((chunks, couples, rows, width), f32),
            vmem((chunks, couples, rows, width), i16), vmem((chunks, couples, 8, width), f32),
            vmem((chunks, steps, shared, rows, width), i16), vmem((chunks, steps, shared, 8, width), f32),
            vmem((chunks, shared, rows, width), f32),
            vmem((2 * shared * couples, width), f32),
            vmem((members - 1, 2 * shared * couples, width), f32),
            vmem((2 * shared * couples, width), f32),
            vmem((chunks, shared, rows, width), f32),
            dma, dma((n_orb - 1,)), dma((n_orb - 1,)), dma((chunks,)), lines_sem, lines_sem,
            dma((2, chunks)), cross_sem, cross_sem, dma((2, chunks)), cross_sem, cross_sem,
            sum_sem, sum_sem, dma((members - 1,)), dma((members - 1,)),
            dma((chunks, hops)), dma((chunks, hops)),
        ],
        compiler_params=pltpu.CompilerParams(collective_id=0, has_side_effects=True,
                                             vmem_limit_bytes=56 << 20),
    )(pair_table.T, orbitals.reshape(own_couples, slab_len * grid_len, width), depth_mat, turn_mat)
    return out.reshape(orbitals.shape)


def solution(mesh):
    placed = (P("orb", "slab", None, None), P("orb", None))
    return jax.shard_map(
        functools.partial(local, n_orb=mesh.shape["orb"], n_slab=mesh.shape["slab"]),
        mesh=mesh, in_specs=placed, out_specs=P("orb", "slab", None, None), check_vma=False
    )
```

```python
import functools
import math

import jax
import jax.numpy as jnp
import numpy as np
from jax import lax
from jax.experimental import pallas as pl
from jax.experimental.pallas import tpu as pltpu
from jax.sharding import PartitionSpec as P

exchange_fraction = 0.25
cell_ratio = 8.0
lines_own = 8
cube = 16
batch = 3
code_peak = 32760.0
MESH = pl.DeviceIdType.MESH
VMEM_SPEC = pl.BlockSpec(memory_space=pltpu.VMEM)
f32 = jnp.float32


def hartley(grid_len):
    rows_idx = np.arange(grid_len)
    angles = 2.0 * math.pi / grid_len * (rows_idx[:, None] * rows_idx[None, :] % grid_len)
    return ((np.cos(angles) + np.sin(angles)) / math.sqrt(grid_len)).astype(np.float32)


def split_const(values):
    high = values.astype(jnp.bfloat16)
    return high, (values - high.astype(np.float32)).astype(jnp.bfloat16)


def split(values):
    high = values.astype(jnp.bfloat16)
    low = (values - high.astype(f32)).astype(jnp.bfloat16)
    return high, low


def depth_turn(rows, depth_ref):
    width = rows.shape[1]
    high, low = split(rows)
    both = jnp.dot(jnp.concatenate([high, low], axis=1), depth_ref[...],
                   preferred_element_type=f32)
    return both[:, :width] + both[:, width:]


def left_turn(fields, left_ref):
    high, low = split(jnp.concatenate(fields, axis=1))
    return jnp.dot(left_ref[...], jnp.concatenate([high, low, high], axis=0),
                   preferred_element_type=f32)


def encode(block):
    peak = jnp.max(jnp.abs(block), axis=0, keepdims=True)
    unit = (jnp.maximum(peak, 1e-30) * (1.004 / code_peak)).astype(jnp.bfloat16).astype(f32)
    return jnp.round(block * (1.0 / unit)).astype(jnp.int32).astype(jnp.int16), unit


def decode(code, unit):
    return code.astype(jnp.int32).astype(f32) * unit


def remote(src, dst, send_sem, recv_sem, device):
    return pltpu.make_async_remote_copy(src_ref=src, dst_ref=dst, send_sem=send_sem, recv_sem=recv_sem,
                                        device_id=device, device_id_type=MESH)


def action_kernel(n_orb, n_slab, half, quota, chunks, grid_len, table_ref, own_ref, depth_ref,
                  turn_ref, out_ref, *scratch):
    held = scratch[:chunks]
    (tab_own, tables, tab_s, starts, ids, chosen, gain, kern, units, fsend, funit, frecv, frunit, frunit_f, work,
     turned, bsend, bunit, bunit_f, brecv, brunit, terms, parts, rsend, runit, rrecv, rrunit, sums, overlap, packed,
     packed_in, coef, ysend,
     tab_sem, tab_send, tab_recv, own_sem, g_send, g_recv, stay_sem, f_send, f_recv, keep_sem, b_send,
     b_recv, r_send, r_recv, p_send, p_recv, y_send, y_recv) = scratch[chunks:]
    me, me_slab = lax.axis_index("orb"), lax.axis_index("slab")
    group, part = me // half, me % half
    groups, members = n_orb // half, n_slab * half
    place = me_slab * half + part
    own_couples, _, width = own_ref.shape
    couples = n_orb * own_couples
    shared = half * own_couples
    capacity = table_ref.shape[1]
    lines = lines_own
    bands = grid_len // lines
    sets = members // bands
    slots = sets * quota
    planes = grid_len // members // chunks
    rows = planes * grid_len
    tile = planes * lines

    def taker(which, band):
        return (band // half * sets + which) * half + band % half

    my_band = me_slab // sets * half + part

    def line_peer(step):
        return {"orb": lax.rem(me + step, n_orb)}

    def member(step):
        to = lax.rem(place + step, members)
        return to, {"orb": group * half + to % half, "slab": to // half}

    barrier = pltpu.get_barrier_semaphore()
    for step in range(1, n_orb):
        pl.semaphore_signal(barrier, inc=1, device_id=line_peer(step), device_id_type=MESH)
    for slab_step in range(1, n_slab):
        for other in range(half):
            pl.semaphore_signal(
                barrier, inc=1, device_id={"orb": group * half + other,
                                           "slab": lax.rem(me_slab + slab_step, n_slab)},
                device_id_type=MESH)
    pl.semaphore_wait(barrier, n_orb - 1 + (n_slab - 1) * half)

    def plane_rows(which, chunk):
        return pl.ds(pl.multiple_of((which * chunks + chunk) * rows, rows), rows)

    def tab_copy(step):
        return remote(tab_own, tables.at[me], tab_send.at[step - 1], tab_recv.at[step - 1],
                      line_peer(step))

    def gather_copy(chunk, step):
        to = lax.rem(me + step, n_orb)
        return remote(own_ref.at[:, plane_rows(to % half, chunk)],
                      held[chunk].at[pl.ds(me * own_couples, own_couples)],
                      g_send.at[chunk, step - 1], g_recv.at[chunk, step - 1], line_peer(step))

    def own_copy(chunk):
        return pltpu.make_async_copy(own_ref.at[:, plane_rows(part, chunk)],
                                     held[chunk].at[pl.ds(me * own_couples, own_couples)],
                                     own_sem.at[chunk])

    def fwd_copies(chunk, step):
        to, device = member(step)
        return (remote(fsend.at[chunk, to], frecv.at[:, place, chunk], f_send.at[0, chunk, step - 1],
                       f_recv.at[0, chunk, step - 1], device),
                remote(funit.at[chunk, to], frunit.at[place, chunk], f_send.at[1, chunk, step - 1],
                       f_recv.at[1, chunk, step - 1], device))

    def fwd_stay(chunk):
        return (pltpu.make_async_copy(fsend.at[chunk, place], frecv.at[:, place, chunk],
                                      stay_sem.at[0, chunk]),
                pltpu.make_async_copy(funit.at[chunk, place], frunit.at[place, chunk],
                                      stay_sem.at[1, chunk]))

    def back_copies(chunk, step):
        to, device = member(step)
        return (remote(bsend.at[chunk, to], brecv.at[chunk, place], b_send.at[0, chunk, step - 1],
                       b_recv.at[0, chunk, step - 1], device),
                remote(bunit.at[chunk, to], brunit.at[chunk, place], b_send.at[1, chunk, step - 1],
                       b_recv.at[1, chunk, step - 1], device))

    def back_stay(chunk):
        return (pltpu.make_async_copy(bsend.at[chunk, place], brecv.at[chunk, place],
                                      keep_sem.at[0, chunk]),
                pltpu.make_async_copy(bunit.at[chunk, place], brunit.at[chunk, place],
                                      keep_sem.at[1, chunk]))

    def sum_copies(chunk, step):
        to = lax.rem(group + step, groups)
        theirs = pl.ds(to * shared, shared)
        device = {"orb": to * half + part}
        return (remote(rsend.at[chunk, theirs], rrecv.at[chunk, step - 1], r_send.at[0, chunk, step - 1],
                       r_recv.at[0, chunk, step - 1], device),
                remote(runit.at[chunk, to], rrunit.at[chunk, step - 1], r_send.at[1, chunk, step - 1],
                       r_recv.at[1, chunk, step - 1], device))

    def overlap_copy(step):
        return remote(packed, packed_in.at[step - 1], p_send.at[step - 1], p_recv.at[step - 1],
                      member(step)[1])

    def result_copy(chunk, hop):
        to = lax.rem(part + hop, half)
        return remote(ysend.at[chunk, pl.ds(to * own_couples, own_couples)],
                      out_ref.at[:, plane_rows(part, chunk)], y_send.at[chunk, hop - 1],
                      y_recv.at[chunk, hop - 1], {"orb": group * half + to})

    tab_own[...] = jnp.full(tab_own.shape, -1, jnp.int32)
    tab_own[0:3, 0:capacity] = table_ref[...]
    for step in range(1, n_orb):
        tab_copy(step).start()
    for chunk in range(chunks):
        for step in range(1, n_orb):
            gather_copy(chunk, step).start()
        own_copy(chunk).start()
    tables[me] = tab_own[...]

    kz = lax.broadcasted_iota(jnp.int32, (grid_len, width), 1) % grid_len
    fz = jnp.minimum(kz, grid_len - kz).astype(f32)
    ky = lax.broadcasted_iota(jnp.int32, (grid_len, width), 0)
    fy = jnp.minimum(ky, grid_len - ky).astype(f32)
    plane_sq = fy * fy + fz * fz
    deep = cell_ratio * cell_ratio
    gain[...] = 1.0 / jnp.where(plane_sq > 0, plane_sq, deep)
    fx = cell_ratio * fy
    scale_k = (2.0 * math.pi / grid_len) * (2.0 * math.pi / grid_len)
    for line in range(lines):
        at = my_band * lines + line
        fl = jnp.minimum(at, grid_len - at).astype(f32)
        plane = fl * fl + fz * fz
        whole = fx * fx + plane
        level = jnp.where(plane > 0, plane, deep)
        kern[:, line * width:(line + 1) * width] = jnp.where(
            whole > 0, (-exchange_fraction / scale_k) * level / jnp.where(whole > 0, whole, 1.0), 0.0)
    terms[2 * slots] = jnp.zeros(terms.shape[1:], f32)
    overlap[...] = jnp.zeros(overlap.shape, f32)
    units[...] = jnp.zeros(units.shape, f32)
    runit[...] = jnp.zeros(runit.shape, f32)

    for step in range(1, n_orb):
        tab_copy(step).wait_recv()
    to_scalars = pltpu.make_async_copy(tables, tab_s, tab_sem)
    to_scalars.start()
    to_scalars.wait()

    def count_block(block, total):
        starts[block] = total
        return lax.fori_loop(
            0, capacity, lambda k, sum_in: sum_in + (tab_s[block, 0, k] >= 0).astype(jnp.int32), total)

    live = lax.fori_loop(0, n_orb, count_block, jnp.int32(0))

    @pl.loop(0, slots)
    def _(slot):
        wanted = slot * groups + group
        used = wanted < live
        block = lax.fori_loop(
            1, n_orb, lambda b, sum_in: sum_in + (starts[b] <= wanted).astype(jnp.int32), jnp.int32(0))
        column = jnp.clip(wanted - starts[block], 0, capacity - 1)
        for k in range(3):
            ids[slot, k] = jnp.maximum(tab_s[block, k, column], 0)
        first = jnp.where(used, tab_s[block, 0, column], -1)
        second = jnp.where(used, tab_s[block, 1, column], -1)

        @pl.loop(0, couples)
        def _(couple):
            chosen[couple, slot] = jnp.where(
                first == couple, 2 * slot, jnp.where(second == couple, 2 * slot + 1, 2 * slots))

    def pair_of(chunk, slot):
        left = held[chunk][ids[slot, 0]].astype(f32)
        right = held[chunk][ids[slot, 1]].astype(f32)
        flipped = ids[slot, 2] == 1
        return left, jnp.where(flipped, pltpu.roll(right, grid_len, 1), right), flipped

    def advance(chunk):
        own_copy(chunk).wait()
        for step in range(1, n_orb):
            gather_copy(chunk, step).wait_recv()

        for which in range(sets):
            @pl.loop(0, quota, step=batch)
            def _(base):
                pairs = [pair_of(chunk, which * quota + base + k) for k in range(batch)]
                flat = depth_turn(jnp.concatenate([left * partner for left, partner, _ in pairs], axis=0),
                                  depth_ref)
                done = left_turn([flat[k * grid_len:(k + 1) * grid_len] for k in range(2 * batch)], turn_ref)
                for k in range(batch):
                    one = done[:, 2 * k * width:(2 * k + 1) * width] * gain[...]
                    two = done[:, (2 * k + 1) * width:(2 * k + 2) * width] * gain[...]
                    for band in range(bands):
                        to = taker(which, band)
                        span = slice(band * lines, (band + 1) * lines)
                        code, unit = encode(jnp.concatenate([one[span], two[span]], axis=0))
                        fsend[chunk, to, base + k] = code
                        units[to, pl.ds(base + k, 1)] = unit

        funit[chunk] = units[...].astype(funit.dtype)
        for step in range(1, members):
            for copy in fwd_copies(chunk, step):
                copy.start()
        for copy in fwd_stay(chunk):
            copy.start()

    for chunk in range(chunks):
        advance(chunk)

    for chunk in range(chunks):
        for copy in fwd_stay(chunk):
            copy.wait()
        for step in range(1, members):
            for copy in fwd_copies(chunk, step):
                copy.wait_recv()

    for chunk in range(chunks):
        frunit_f[:, chunk] = frunit[:, chunk].astype(f32)

    @pl.loop(0, quota, step=batch)
    def _(base):
        for k in range(batch):
            for src in range(members):
                for chunk in range(chunks):
                    at = (src * chunks + chunk) * tile
                    work[k, at:at + tile] = decode(frecv[base + k, src, chunk],
                                                   frunit_f[src, chunk, pl.ds(base + k, 1)])
            done = left_turn([work[k, pl.ds(line, grid_len, stride=lines), :] for line in range(lines)],
                             turn_ref)
            done = done * kern[...]
            back = left_turn([done[:, line * width:(line + 1) * width] for line in range(lines)], turn_ref)
            for line in range(lines):
                turned[k, pl.ds(line, grid_len, stride=lines), :] = back[:, line * width:(line + 1) * width]
            for to in range(members):
                for chunk in range(chunks):
                    at = (to * chunks + chunk) * tile
                    code, unit = encode(turned[k, at:at + tile])
                    bsend[chunk, to, base + k] = code
                    bunit_f[chunk, to, pl.ds(base + k, 1)] = unit

    bunit[...] = bunit_f[...].astype(bunit.dtype)
    for chunk in range(chunks):
        for step in range(1, members):
            for copy in back_copies(chunk, step):
                copy.start()
        for copy in back_stay(chunk):
            copy.start()

    def retreat(chunk):
        for copy in back_stay(chunk):
            copy.wait()
        for step in range(1, members):
            for copy in back_copies(chunk, step):
                copy.wait_recv()

        units[...] = brunit[chunk].astype(f32)

        for which in range(sets):
            @pl.loop(0, quota, step=batch)
            def _(base):
                fields = []
                for k in range(batch):
                    blocks = [decode(brecv[chunk, taker(which, band), base + k],
                                     units[taker(which, band), pl.ds(base + k, 1)])
                              for band in range(bands)]
                    fields.append(jnp.concatenate([block[:lines] for block in blocks], axis=0))
                    fields.append(jnp.concatenate([block[lines:] for block in blocks], axis=0))
                done = left_turn(fields, turn_ref)
                potentials = depth_turn(jnp.concatenate(
                    [done[:, k * width:(k + 1) * width] for k in range(2 * batch)], axis=0), depth_ref)
                for k in range(batch):
                    slot = which * quota + base + k
                    potential = potentials[k * rows:(k + 1) * rows]
                    left, partner, flipped = pair_of(chunk, slot)
                    terms[2 * slot] = potential * partner
                    second = potential * left
                    terms[2 * slot + 1] = jnp.where(flipped, pltpu.roll(second, grid_len, 1), second)

        @pl.loop(0, couples)
        def _(couple):
            total = terms[chosen[couple, 0]]
            for slot in range(1, slots):
                total = total + terms[chosen[couple, slot]]
            parts[chunk, couple] = total
            code, unit = encode(total)
            rsend[chunk, couple] = code
            runit[chunk, couple // shared, pl.ds(couple % shared, 1)] = unit

        for step in range(1, groups):
            for copy in sum_copies(chunk, step):
                copy.start()

    def collect(chunk):
        for step in range(1, groups):
            for copy in sum_copies(chunk, step):
                copy.wait_recv()
        for k in range(shared):
            total = parts[chunk, group * shared + k]
            for step in range(1, groups):
                total = total + decode(rrecv[chunk, step - 1, k], rrunit[chunk, step - 1, k:k + 1])
            sums[chunk, k] = total
            across = pltpu.roll(total, grid_len, 1)

            @pl.loop(0, couples)
            def _(couple):
                basis = held[chunk][couple].astype(f32)
                for kind, field in enumerate((total, across)):
                    at = pl.ds((kind * shared + k) * couples + couple, 1)
                    overlap[at] += jnp.sum(basis * field, axis=0, keepdims=True)

    for chunk in range(chunks):
        retreat(chunk)
        if chunk:
            collect(chunk - 1)
    collect(chunks - 1)

    lane = lax.broadcasted_iota(jnp.int32, (8, width), 1)
    halves = ((lane // grid_len) == lax.broadcasted_iota(jnp.int32, (8, width), 0)).astype(jnp.bfloat16)

    def thirds(values):
        high = values.astype(jnp.bfloat16)
        rest = values - high.astype(f32)
        mid = rest.astype(jnp.bfloat16)
        return high, mid, (rest - mid.astype(f32)).astype(jnp.bfloat16)

    packed[...] = sum(lax.dot_general(halves, third, (((1,), (1,)), ((), ())), preferred_element_type=f32)
                      for third in thirds(overlap[...]))
    for step in range(1, members):
        overlap_copy(step).start()
    total = packed[...]
    for step in range(1, members):
        overlap_copy(step).wait_recv()
        total = total + packed_in[step - 1]
    total = total * (1.0 / (grid_len * grid_len * grid_len))
    coef[...] = sum(lax.dot_general(third, halves, (((0,), (0,)), ((), ())), preferred_element_type=f32)
                    for third in thirds(total))

    strip = rows // 4
    for chunk in range(chunks):
        @pl.loop(0, rows // strip)
        def _(at):
            here = pl.ds(pl.multiple_of(at * strip, strip), strip)
            kept = [jnp.zeros((strip, width), f32) for _ in range(2 * shared)]
            for couple in range(couples):
                basis = held[chunk][couple, here].astype(f32)
                for k in range(2 * shared):
                    row = k * couples + couple
                    kept[k] = kept[k] + coef[row:row + 1] * basis
            for k in range(shared):
                ysend[chunk, k, here] = (sums[chunk, k, here] - kept[k]
                                         - pltpu.roll(kept[shared + k], grid_len, 1))

        for hop in range(1, half):
            result_copy(chunk, hop).start()
        out_ref[:, plane_rows(part, chunk)] = ysend[chunk, pl.ds(part * own_couples, own_couples)]

    for chunk in range(chunks):
        for hop in range(1, half):
            result_copy(chunk, hop).wait()
        for step in range(1, members):
            for copy in fwd_copies(chunk, step) + back_copies(chunk, step):
                copy.wait_send()
        for step in range(1, groups):
            for copy in sum_copies(chunk, step):
                copy.wait_send()
        for step in range(1, n_orb):
            gather_copy(chunk, step).wait_send()
    for step in range(1, members):
        overlap_copy(step).wait_send()
    for step in range(1, n_orb):
        tab_copy(step).wait_send()


def local(orbitals, pair_table, n_orb, n_slab):
    own_couples, slab_len, grid_len, width = orbitals.shape
    capacity = pair_table.shape[0]
    half = max(1, cube // n_slab)
    members = n_slab * half
    groups = n_orb // half
    bands = grid_len // lines_own
    sets = members // bands
    live_total = sum(capacity * (k + 1) // n_orb for k in range(n_orb))
    quota = -(-live_total // (groups * sets * batch)) * batch
    slots = sets * quota
    couples, shared = n_orb * own_couples, half * own_couples
    planes = grid_len // members
    chunks = planes // 2
    rows, tile = 2 * grid_len, 2 * lines_own
    quota_pad = -(-quota // 16) * 16
    shared_pad = -(-shared // 8) * 8
    overlap_rows = -(-2 * shared * couples // 128) * 128
    tab_lanes = -(-capacity // 128) * 128

    mat = hartley(grid_len)
    mat_high, mat_low = split_const(mat)
    turn_mat = jnp.asarray(np.concatenate([mat_high, mat_high, mat_low], axis=1))
    deep_high, deep_low = split_const(np.kron(np.eye(2, dtype=np.float32), mat))
    depth_mat = jnp.asarray(np.block([[deep_high, deep_low], [deep_high, np.zeros_like(deep_low)]]))

    dma, vmem, smem = pltpu.SemaphoreType.DMA, pltpu.VMEM, pltpu.SMEM
    i32, i16 = jnp.int32, jnp.int16
    bf16 = orbitals.dtype
    coded = vmem((chunks, members, quota, tile, width), i16)
    sent_units = vmem((chunks, members, quota_pad, width), bf16)
    lines_sem = dma((chunks, n_orb - 1))
    cross_sem = dma((2, chunks, members - 1))
    steps = max(groups - 1, 1)
    sum_sem = dma((2, chunks, steps))
    hops = max(half - 1, 1)
    out = pl.pallas_call(
        functools.partial(action_kernel, n_orb, n_slab, half, quota, chunks, grid_len),
        out_shape=jax.ShapeDtypeStruct((own_couples, slab_len * grid_len, width), f32),
        in_specs=[VMEM_SPEC] * 4,
        out_specs=VMEM_SPEC,
        scratch_shapes=[vmem((couples, rows, width), orbitals.dtype)] * chunks + [
            vmem((8, tab_lanes), i32), vmem((n_orb, 8, tab_lanes), i32), smem((n_orb, 8, tab_lanes), i32),
            smem((n_orb,), i32), smem((slots, 3), i32), smem((couples, slots), i32),
            vmem((grid_len, width), f32), vmem((grid_len, lines_own * width), f32),
            vmem((members, quota_pad, width), f32), coded, sent_units,
            vmem((quota, members, chunks, tile, width), i16), vmem((members, chunks, quota_pad, width), bf16),
            vmem((members, chunks, quota_pad, width), f32),
            vmem((batch, lines_own * grid_len, width), f32), vmem((batch, lines_own * grid_len, width), f32),
            coded, sent_units, vmem((chunks, members, quota_pad, width), f32), coded, sent_units,
            vmem((2 * slots + 1, rows, width), f32),
            vmem((chunks, couples, rows, width), f32),
            vmem((chunks, couples, rows, width), i16), vmem((chunks, groups, shared_pad, width), f32),
            vmem((chunks, steps, shared, rows, width), i16), vmem((chunks, steps, shared_pad, width), f32),
            vmem((chunks, shared, rows, width), f32),
            vmem((overlap_rows, width), f32), vmem((8, overlap_rows), f32),
            vmem((members - 1, 8, overlap_rows), f32), vmem((overlap_rows, width), f32),
            vmem((chunks, shared, rows, width), f32),
            dma, dma((n_orb - 1,)), dma((n_orb - 1,)), dma((chunks,)), lines_sem, lines_sem,
            dma((2, chunks)), cross_sem, cross_sem, dma((2, chunks)), cross_sem, cross_sem,
            sum_sem, sum_sem, dma((members - 1,)), dma((members - 1,)),
            dma((chunks, hops)), dma((chunks, hops)),
        ],
        compiler_params=pltpu.CompilerParams(collective_id=0, has_side_effects=True,
                                             vmem_limit_bytes=56 << 20),
    )(pair_table.T, orbitals.reshape(own_couples, slab_len * grid_len, width), depth_mat, turn_mat)
    return out.reshape(orbitals.shape)


def solution(mesh):
    placed = (P("orb", "slab", None, None), P("orb", None))
    return jax.shard_map(
        functools.partial(local, n_orb=mesh.shape["orb"], n_slab=mesh.shape["slab"]),
        mesh=mesh, in_specs=placed, out_specs=P("orb", "slab", None, None), check_vma=False
    )
```

```python
import functools
import math

import jax
import jax.numpy as jnp
import numpy as np
from jax import lax
from jax.experimental import pallas as pl
from jax.experimental.pallas import tpu as pltpu
from jax.sharding import PartitionSpec as P

exchange_fraction = 0.25
cell_ratio = 8.0
lines_own = 8
cube = 16
batch = 3
code_peak = 32760.0
MESH = pl.DeviceIdType.MESH
VMEM_SPEC = pl.BlockSpec(memory_space=pltpu.VMEM)
f32 = jnp.float32


def hartley(grid_len):
    rows_idx = np.arange(grid_len)
    angles = 2.0 * math.pi / grid_len * (rows_idx[:, None] * rows_idx[None, :] % grid_len)
    return ((np.cos(angles) + np.sin(angles)) / math.sqrt(grid_len)).astype(np.float32)


def split_const(values):
    high = values.astype(jnp.bfloat16)
    return high, (values - high.astype(np.float32)).astype(jnp.bfloat16)


def split(values):
    high = values.astype(jnp.bfloat16)
    low = (values - high.astype(f32)).astype(jnp.bfloat16)
    return high, low


def depth_turn(rows, depth_ref):
    width = rows.shape[1]
    high, low = split(rows)
    both = jnp.dot(jnp.concatenate([high, low], axis=1), depth_ref[...],
                   preferred_element_type=f32)
    return both[:, :width] + both[:, width:]


def left_turn(fields, left_ref):
    high, low = split(jnp.concatenate(fields, axis=1))
    return jnp.dot(left_ref[...], jnp.concatenate([high, low, high], axis=0),
                   preferred_element_type=f32)


def encode(block):
    peak = jnp.max(jnp.abs(block), axis=0, keepdims=True)
    unit = (jnp.maximum(peak, 1e-30) * (1.004 / code_peak)).astype(jnp.bfloat16).astype(f32)
    return jnp.round(block * (1.0 / unit)).astype(jnp.int32).astype(jnp.int16), unit


def decode(code, unit):
    return code.astype(jnp.int32).astype(f32) * unit


def remote(src, dst, send_sem, recv_sem, device):
    return pltpu.make_async_remote_copy(src_ref=src, dst_ref=dst, send_sem=send_sem, recv_sem=recv_sem,
                                        device_id=device, device_id_type=MESH)


def action_kernel(n_orb, n_slab, half, quota, chunks, grid_len, table_ref, own_ref, depth_ref,
                  turn_ref, out_ref, unit_ref, *scratch):
    held = scratch[:chunks]
    (tab_own, tables, tab_s, starts, ids, chosen, gain, kern, units, fsend, funit, frecv, frunit, frunit_f, work,
     turned, bsend, bunit, bunit_f, brecv, brunit, terms, parts, rsend, runit, rrecv, rrunit, overlap, packed,
     packed_in, merged, merged_in, coef, result, ysend, yunit,
     tab_sem, tab_send, tab_recv, own_sem, g_send, g_recv, stay_sem, f_send, f_recv, keep_sem, b_send,
     b_recv, r_send, r_recv, o_send, o_recv, p_send, p_recv, y_send, y_recv) = scratch[chunks:]
    me, me_slab = lax.axis_index("orb"), lax.axis_index("slab")
    group, part = me // half, me % half
    groups, members = n_orb // half, n_slab * half
    place = me_slab * half + part
    own_couples, _, width = own_ref.shape
    couples = n_orb * own_couples
    shared = half * own_couples
    capacity = table_ref.shape[1]
    lines = lines_own
    bands = grid_len // lines
    sets = members // bands
    slots = sets * quota
    runs = quota // batch
    planes = grid_len // members // chunks
    rows = planes * grid_len
    tile = planes * lines

    def taker(which, band):
        return (band // half * sets + which) * half + band % half

    my_band = me_slab // sets * half + part

    def line_peer(step):
        return {"orb": lax.rem(me + step, n_orb)}

    def member(step):
        to = lax.rem(place + step, members)
        return to, {"orb": group * half + to % half, "slab": to // half}

    barrier = pltpu.get_barrier_semaphore()
    for step in range(1, n_orb):
        pl.semaphore_signal(barrier, inc=1, device_id=line_peer(step), device_id_type=MESH)
    for slab_step in range(1, n_slab):
        for other in range(half):
            pl.semaphore_signal(
                barrier, inc=1, device_id={"orb": group * half + other,
                                           "slab": lax.rem(me_slab + slab_step, n_slab)},
                device_id_type=MESH)

    def plane_rows(which, chunk):
        return pl.ds(pl.multiple_of((which * chunks + chunk) * rows, rows), rows)

    def tab_copy(step):
        return remote(tab_own, tables.at[me], tab_send.at[step - 1], tab_recv.at[step - 1],
                      line_peer(step))

    def gather_copy(chunk, step):
        to = lax.rem(me + step, n_orb)
        return remote(own_ref.at[:, plane_rows(to % half, chunk)],
                      held[chunk].at[pl.ds(me * own_couples, own_couples)],
                      g_send.at[chunk, step - 1], g_recv.at[chunk, step - 1], line_peer(step))

    def own_copy(chunk):
        return pltpu.make_async_copy(own_ref.at[:, plane_rows(part, chunk)],
                                     held[chunk].at[pl.ds(me * own_couples, own_couples)],
                                     own_sem.at[chunk])

    def fwd_copy(chunk, step):
        to, device = member(step)
        return remote(fsend.at[chunk, to], frecv.at[:, place, chunk], f_send.at[0, chunk, step - 1],
                      f_recv.at[0, chunk, step - 1], device)

    def fwd_unit(chunk, step):
        to, device = member(step)
        return remote(funit.at[chunk, to], frunit.at[place, chunk], f_send.at[1, chunk, step - 1],
                      f_recv.at[1, chunk, step - 1], device)

    def fwd_stay(chunk):
        return (pltpu.make_async_copy(fsend.at[chunk, place], frecv.at[:, place, chunk],
                                      stay_sem.at[0, chunk]),
                pltpu.make_async_copy(funit.at[chunk, place], frunit.at[place, chunk],
                                      stay_sem.at[1, chunk]))

    def back_copy(chunk, step, run):
        to, device = member(step)
        some = pl.ds(run * batch, batch)
        return remote(bsend.at[chunk, to, some], brecv.at[chunk, place, some],
                      b_send.at[run, chunk, step - 1], b_recv.at[run, chunk, step - 1], device)

    def back_unit(chunk, step):
        to, device = member(step)
        return remote(bunit.at[chunk, to], brunit.at[chunk, place], b_send.at[runs, chunk, step - 1],
                      b_recv.at[runs, chunk, step - 1], device)

    def back_stay(chunk):
        return (pltpu.make_async_copy(bsend.at[chunk, place], brecv.at[chunk, place],
                                      keep_sem.at[0, chunk]),
                pltpu.make_async_copy(bunit.at[chunk, place], brunit.at[chunk, place],
                                      keep_sem.at[1, chunk]))

    def sum_copies(chunk, step):
        to = lax.rem(group + step, groups)
        theirs = pl.ds(to * shared, shared)
        device = {"orb": to * half + part}
        return (remote(rsend.at[chunk, theirs], rrecv.at[chunk, step - 1], r_send.at[0, chunk, step - 1],
                       r_recv.at[0, chunk, step - 1], device),
                remote(runit.at[chunk, to], rrunit.at[chunk, step - 1], r_send.at[1, chunk, step - 1],
                       r_recv.at[1, chunk, step - 1], device))

    def overlap_copy(step):
        to = lax.rem(group + step, groups)
        return remote(packed.at[to], packed_in.at[step - 1], o_send.at[step - 1], o_recv.at[step - 1],
                      {"orb": to * half + part})

    def merged_copy(step):
        return remote(merged, merged_in.at[step - 1], p_send.at[step - 1], p_recv.at[step - 1],
                      member(step)[1])

    def result_copies(chunk, hop):
        to = lax.rem(part + hop, half)
        theirs, device = pl.ds(to * own_couples, own_couples), {"orb": group * half + to}
        return (remote(ysend.at[chunk, theirs], out_ref.at[:, plane_rows(part, chunk)],
                       y_send.at[0, chunk, hop - 1], y_recv.at[0, chunk, hop - 1], device),
                remote(yunit.at[chunk, theirs], unit_ref.at[:, part * chunks + chunk],
                       y_send.at[1, chunk, hop - 1], y_recv.at[1, chunk, hop - 1], device))

    tab_own[...] = jnp.full(tab_own.shape, -1, jnp.int32)
    tab_own[0:3, 0:capacity] = table_ref[...]
    kz = lax.broadcasted_iota(jnp.int32, (grid_len, width), 1) % grid_len
    fz = jnp.minimum(kz, grid_len - kz).astype(f32)
    ky = lax.broadcasted_iota(jnp.int32, (grid_len, width), 0)
    fy = jnp.minimum(ky, grid_len - ky).astype(f32)
    plane_sq = fy * fy + fz * fz
    deep = cell_ratio * cell_ratio
    gain[...] = 1.0 / jnp.where(plane_sq > 0, plane_sq, deep)
    fx = cell_ratio * fy
    scale_k = (2.0 * math.pi / grid_len) * (2.0 * math.pi / grid_len)
    for line in range(lines):
        at = my_band * lines + line
        fl = jnp.minimum(at, grid_len - at).astype(f32)
        plane = fl * fl + fz * fz
        whole = fx * fx + plane
        level = jnp.where(plane > 0, plane, deep)
        kern[:, line * width:(line + 1) * width] = jnp.where(
            whole > 0, (-exchange_fraction / scale_k) * level / jnp.where(whole > 0, whole, 1.0), 0.0)
    terms[2 * slots] = jnp.zeros(terms.shape[1:], f32)
    overlap[...] = jnp.zeros(overlap.shape, f32)
    units[...] = jnp.zeros(units.shape, f32)
    runit[...] = jnp.zeros(runit.shape, f32)

    pl.semaphore_wait(barrier, n_orb - 1 + (n_slab - 1) * half)
    for step in range(1, n_orb):
        tab_copy(step).start()
    for chunk in range(chunks):
        for step in range(1, n_orb):
            gather_copy(chunk, step).start()
        own_copy(chunk).start()
    tables[me] = tab_own[...]

    for step in range(1, n_orb):
        tab_copy(step).wait_recv()
    to_scalars = pltpu.make_async_copy(tables, tab_s, tab_sem)
    to_scalars.start()
    to_scalars.wait()

    def count_block(block, total):
        starts[block] = total
        return lax.fori_loop(
            0, capacity, lambda k, sum_in: sum_in + (tab_s[block, 0, k] >= 0).astype(jnp.int32), total)

    live = lax.fori_loop(0, n_orb, count_block, jnp.int32(0))

    @pl.loop(0, slots)
    def _(slot):
        wanted = slot * groups + group
        used = wanted < live
        block = lax.fori_loop(
            1, n_orb, lambda b, sum_in: sum_in + (starts[b] <= wanted).astype(jnp.int32), jnp.int32(0))
        column = jnp.clip(wanted - starts[block], 0, capacity - 1)
        for k in range(3):
            ids[slot, k] = jnp.maximum(tab_s[block, k, column], 0)
        first = jnp.where(used, tab_s[block, 0, column], -1)
        second = jnp.where(used, tab_s[block, 1, column], -1)

        @pl.loop(0, couples)
        def _(couple):
            chosen[couple, slot] = jnp.where(
                first == couple, 2 * slot, jnp.where(second == couple, 2 * slot + 1, 2 * slots))

    def pair_of(chunk, slot):
        left = held[chunk][ids[slot, 0]].astype(f32)
        right = held[chunk][ids[slot, 1]].astype(f32)
        flipped = ids[slot, 2] == 1
        return left, jnp.where(flipped, pltpu.roll(right, grid_len, 1), right), flipped

    def advance(chunk):
        own_copy(chunk).wait()
        for step in range(1, n_orb):
            gather_copy(chunk, step).wait_recv()

        for which in range(sets):
            @pl.loop(0, quota, step=batch)
            def _(base):
                pairs = [pair_of(chunk, which * quota + base + k) for k in range(batch)]
                flat = depth_turn(jnp.concatenate([left * partner for left, partner, _ in pairs], axis=0),
                                  depth_ref)
                done = left_turn([flat[k * grid_len:(k + 1) * grid_len] for k in range(2 * batch)], turn_ref)
                for k in range(batch):
                    one = done[:, 2 * k * width:(2 * k + 1) * width] * gain[...]
                    two = done[:, (2 * k + 1) * width:(2 * k + 2) * width] * gain[...]
                    for band in range(bands):
                        to = taker(which, band)
                        span = slice(band * lines, (band + 1) * lines)
                        code, unit = encode(jnp.concatenate([one[span], two[span]], axis=0))
                        fsend[chunk, to, base + k] = code
                        units[to, pl.ds(base + k, 1)] = unit

            for step in range(1, members):
                to = member(step)[0]

                @pl.when(to // half % sets == which)
                def _():
                    fwd_copy(chunk, step).start()

        funit[chunk] = units[...].astype(funit.dtype)
        for step in range(1, members):
            fwd_unit(chunk, step).start()
        for copy in fwd_stay(chunk):
            copy.start()

    for chunk in range(chunks):
        advance(chunk)

    for chunk in range(chunks):
        for copy in fwd_stay(chunk):
            copy.wait()
        for step in range(1, members):
            fwd_copy(chunk, step).wait_recv()
            fwd_unit(chunk, step).wait_recv()

    for chunk in range(chunks):
        frunit_f[:, chunk] = frunit[:, chunk].astype(f32)

    @pl.loop(0, quota, step=batch)
    def _(base):
        for k in range(batch):
            for src in range(members):
                for chunk in range(chunks):
                    at = (src * chunks + chunk) * tile
                    work[k, at:at + tile] = decode(frecv[base + k, src, chunk],
                                                   frunit_f[src, chunk, pl.ds(base + k, 1)])
            done = left_turn([work[k, pl.ds(line, grid_len, stride=lines), :] for line in range(lines)],
                             turn_ref)
            done = done * kern[...]
            back = left_turn([done[:, line * width:(line + 1) * width] for line in range(lines)], turn_ref)
            for line in range(lines):
                turned[k, pl.ds(line, grid_len, stride=lines), :] = back[:, line * width:(line + 1) * width]
            for to in range(members):
                for chunk in range(chunks):
                    at = (to * chunks + chunk) * tile
                    code, unit = encode(turned[k, at:at + tile])
                    bsend[chunk, to, base + k] = code
                    bunit_f[chunk, to, pl.ds(base + k, 1)] = unit
        for step in range(1, members):
            back_copy(0, step, base // batch).start()

    bunit[...] = bunit_f[...].astype(bunit.dtype)
    for chunk in range(chunks):
        for step in range(1, members):
            back_unit(chunk, step).start()
        if chunk:
            for run in range(runs):
                for step in range(1, members):
                    back_copy(chunk, step, run).start()
        for copy in back_stay(chunk):
            copy.start()

    def retreat(chunk):
        for copy in back_stay(chunk):
            copy.wait()
        for step in range(1, members):
            for run in range(runs):
                back_copy(chunk, step, run).wait_recv()
            back_unit(chunk, step).wait_recv()

        units[...] = brunit[chunk].astype(f32)

        for which in range(sets):
            @pl.loop(0, quota, step=batch)
            def _(base):
                fields = []
                for k in range(batch):
                    blocks = [decode(brecv[chunk, taker(which, band), base + k],
                                     units[taker(which, band), pl.ds(base + k, 1)])
                              for band in range(bands)]
                    fields.append(jnp.concatenate([block[:lines] for block in blocks], axis=0))
                    fields.append(jnp.concatenate([block[lines:] for block in blocks], axis=0))
                done = left_turn(fields, turn_ref)
                potentials = depth_turn(jnp.concatenate(
                    [done[:, k * width:(k + 1) * width] for k in range(2 * batch)], axis=0), depth_ref)
                for k in range(batch):
                    slot = which * quota + base + k
                    potential = potentials[k * rows:(k + 1) * rows]
                    left, partner, flipped = pair_of(chunk, slot)
                    terms[2 * slot] = potential * partner
                    second = potential * left
                    terms[2 * slot + 1] = jnp.where(flipped, pltpu.roll(second, grid_len, 1), second)

        @pl.loop(0, couples)
        def _(couple):
            total = terms[chosen[couple, 0]]
            for slot in range(1, slots):
                total = total + terms[chosen[couple, slot]]
            parts[chunk, couple] = total
            code, unit = encode(total)
            rsend[chunk, couple] = code
            runit[chunk, couple // shared, pl.ds(couple % shared, 1)] = unit
            across = pltpu.roll(total, grid_len, 1)
            at = couple % shared * couples
            for other in range(couples):
                basis = held[chunk][other].astype(f32)
                for kind, field in enumerate((total, across)):
                    row = pl.ds(at + kind * shared * couples + other, 1)
                    overlap[couple // shared, row] += jnp.sum(basis * field, axis=0, keepdims=True)


    for chunk in range(chunks - 1):
        retreat(chunk)
        for step in range(1, groups):
            for copy in sum_copies(chunk, step):
                copy.start()
    retreat(chunks - 1)

    lane = lax.broadcasted_iota(jnp.int32, (8, width), 1)
    halves = ((lane // grid_len) == lax.broadcasted_iota(jnp.int32, (8, width), 0)).astype(jnp.bfloat16)

    def thirds(values):
        high = values.astype(jnp.bfloat16)
        rest = values - high.astype(f32)
        mid = rest.astype(jnp.bfloat16)
        return high, mid, (rest - mid.astype(f32)).astype(jnp.bfloat16)

    for which in range(groups):
        packed[which] = sum(lax.dot_general(halves, third, (((1,), (1,)), ((), ())),
                                            preferred_element_type=f32)
                            for third in thirds(overlap[which]))
    for step in range(1, groups):
        overlap_copy(step).start()
    for step in range(1, groups):
        for copy in sum_copies(chunks - 1, step):
            copy.start()
    total = packed[group]
    for step in range(1, groups):
        overlap_copy(step).wait_recv()
        total = total + packed_in[step - 1]
    merged[...] = total
    for step in range(1, members):
        merged_copy(step).start()
    for step in range(1, members):
        merged_copy(step).wait_recv()
        total = total + merged_in[step - 1]
    total = total * (1.0 / (grid_len * grid_len * grid_len))
    coef[...] = sum(lax.dot_general(third, halves, (((0,), (0,)), ((), ())), preferred_element_type=f32)
                    for third in thirds(total))

    strip = rows // 4
    for chunk in range(chunks):
        for step in range(1, groups):
            for copy in sum_copies(chunk, step):
                copy.wait_recv()

        @pl.loop(0, rows // strip)
        def _(at):
            here = pl.ds(pl.multiple_of(at * strip, strip), strip)
            kept = [jnp.zeros((strip, width), f32) for _ in range(2 * shared)]
            for couple in range(couples):
                basis = held[chunk][couple, here].astype(f32)
                for k in range(2 * shared):
                    row = k * couples + couple
                    kept[k] = kept[k] + coef[row:row + 1] * basis
            for k in range(shared):
                total = parts[chunk, group * shared + k, here]
                for step in range(1, groups):
                    total = total + decode(rrecv[chunk, step - 1, k, here],
                                           rrunit[chunk, step - 1, k:k + 1])
                result[k, here] = total - kept[k] - pltpu.roll(kept[shared + k], grid_len, 1)

        for k in range(shared):
            code, unit = encode(result[k])
            ysend[chunk, k] = code
            yunit[chunk, k] = jnp.broadcast_to(unit, yunit.shape[2:])
        for hop in range(1, half):
            for copy in result_copies(chunk, hop):
                copy.start()
        mine = pl.ds(part * own_couples, own_couples)
        out_ref[:, plane_rows(part, chunk)] = ysend[chunk, mine]
        unit_ref[:, part * chunks + chunk] = yunit[chunk, mine]

    for chunk in range(chunks):
        for hop in range(1, half):
            for copy in result_copies(chunk, hop):
                copy.wait()
        for step in range(1, members):
            fwd_copy(chunk, step).wait_send()
            fwd_unit(chunk, step).wait_send()
            for run in range(runs):
                back_copy(chunk, step, run).wait_send()
            back_unit(chunk, step).wait_send()
        for step in range(1, groups):
            for copy in sum_copies(chunk, step):
                copy.wait_send()
        for step in range(1, n_orb):
            gather_copy(chunk, step).wait_send()
    for step in range(1, groups):
        overlap_copy(step).wait_send()
    for step in range(1, members):
        merged_copy(step).wait_send()
    for step in range(1, n_orb):
        tab_copy(step).wait_send()


def local(orbitals, pair_table, n_orb, n_slab):
    own_couples, slab_len, grid_len, width = orbitals.shape
    capacity = pair_table.shape[0]
    half = max(1, cube // n_slab)
    members = n_slab * half
    groups = n_orb // half
    bands = grid_len // lines_own
    sets = members // bands
    live_total = sum(capacity * (k + 1) // n_orb for k in range(n_orb))
    quota = -(-live_total // (groups * sets * batch)) * batch
    slots = sets * quota
    couples, shared = n_orb * own_couples, half * own_couples
    planes = grid_len // members
    chunks = planes // 2
    rows, tile = 2 * grid_len, 2 * lines_own
    quota_pad = -(-quota // 16) * 16
    shared_pad = -(-shared // 8) * 8
    overlap_rows = -(-2 * shared * couples // 128) * 128
    tab_lanes = -(-capacity // 128) * 128

    mat = hartley(grid_len)
    mat_high, mat_low = split_const(mat)
    turn_mat = jnp.asarray(np.concatenate([mat_high, mat_high, mat_low], axis=1))
    deep_high, deep_low = split_const(np.kron(np.eye(2, dtype=np.float32), mat))
    depth_mat = jnp.asarray(np.block([[deep_high, deep_low], [deep_high, np.zeros_like(deep_low)]]))

    dma, vmem, smem = pltpu.SemaphoreType.DMA, pltpu.VMEM, pltpu.SMEM
    i32, i16 = jnp.int32, jnp.int16
    bf16 = orbitals.dtype
    coded = vmem((chunks, members, quota, tile, width), i16)
    sent_units = vmem((chunks, members, quota_pad, width), bf16)
    lines_sem = dma((chunks, n_orb - 1))
    cross_sem = dma((2, chunks, members - 1))
    back_sem = dma((quota // batch + 1, chunks, members - 1))
    steps = max(groups - 1, 1)
    sum_sem = dma((2, chunks, steps))
    hops = max(half - 1, 1)
    blocks = slab_len * grid_len // rows
    code, unit = pl.pallas_call(
        functools.partial(action_kernel, n_orb, n_slab, half, quota, chunks, grid_len),
        out_shape=(jax.ShapeDtypeStruct((own_couples, slab_len * grid_len, width), i16),
                   jax.ShapeDtypeStruct((own_couples, blocks, 8, width), f32)),
        in_specs=[VMEM_SPEC] * 4,
        out_specs=(VMEM_SPEC, VMEM_SPEC),
        scratch_shapes=[vmem((couples, rows, width), orbitals.dtype)] * chunks + [
            vmem((8, tab_lanes), i32), vmem((n_orb, 8, tab_lanes), i32), smem((n_orb, 8, tab_lanes), i32),
            smem((n_orb,), i32), smem((slots, 3), i32), smem((couples, slots), i32),
            vmem((grid_len, width), f32), vmem((grid_len, lines_own * width), f32),
            vmem((members, quota_pad, width), f32), coded, sent_units,
            vmem((quota, members, chunks, tile, width), i16), vmem((members, chunks, quota_pad, width), bf16),
            vmem((members, chunks, quota_pad, width), f32),
            vmem((batch, lines_own * grid_len, width), f32), vmem((batch, lines_own * grid_len, width), f32),
            coded, sent_units, vmem((chunks, members, quota_pad, width), f32), coded, sent_units,
            vmem((2 * slots + 1, rows, width), f32),
            vmem((chunks, couples, rows, width), f32),
            vmem((chunks, couples, rows, width), i16), vmem((chunks, groups, shared_pad, width), f32),
            vmem((chunks, steps, shared, rows, width), i16), vmem((chunks, steps, shared_pad, width), f32),
            vmem((groups, overlap_rows, width), f32), vmem((groups, 8, overlap_rows), f32),
            vmem((steps, 8, overlap_rows), f32), vmem((8, overlap_rows), f32),
            vmem((members - 1, 8, overlap_rows), f32), vmem((overlap_rows, width), f32),
            vmem((shared, rows, width), f32),
            vmem((chunks, shared, rows, width), i16), vmem((chunks, shared, 8, width), f32),
            dma, dma((n_orb - 1,)), dma((n_orb - 1,)), dma((chunks,)), lines_sem, lines_sem,
            dma((2, chunks)), cross_sem, cross_sem, dma((2, chunks)), back_sem, back_sem,
            sum_sem, sum_sem, dma((steps,)), dma((steps,)), dma((members - 1,)), dma((members - 1,)),
            dma((2, chunks, hops)), dma((2, chunks, hops)),
        ],
        compiler_params=pltpu.CompilerParams(collective_id=0, has_side_effects=True,
                                             vmem_limit_bytes=56 << 20),
    )(pair_table.T, orbitals.reshape(own_couples, slab_len * grid_len, width), depth_mat, turn_mat)
    pieces = code.reshape(own_couples, blocks, rows, width).astype(f32)
    return (pieces * unit[:, :, :1]).reshape(orbitals.shape)


def solution(mesh):
    placed = (P("orb", "slab", None, None), P("orb", None))
    return jax.shard_map(
        functools.partial(local, n_orb=mesh.shape["orb"], n_slab=mesh.shape["slab"]),
        mesh=mesh, in_specs=placed, out_specs=P("orb", "slab", None, None), check_vma=False
    )
```

```python
import functools
import math

import jax
import jax.numpy as jnp
import numpy as np
from jax import lax
from jax.experimental import pallas as pl
from jax.experimental.pallas import tpu as pltpu
from jax.sharding import PartitionSpec as P

exchange_fraction = 0.25
cell_ratio = 8.0
lines_own = 8
cube = 16
batch = 3
code_peak = 32700.0
MESH = pl.DeviceIdType.MESH
HBM_SPEC = pl.BlockSpec(memory_space=pltpu.HBM)
f32 = jnp.float32


def hartley(grid_len):
    rows_idx = np.arange(grid_len)
    angles = 2.0 * math.pi / grid_len * (rows_idx[:, None] * rows_idx[None, :] % grid_len)
    return ((np.cos(angles) + np.sin(angles)) / math.sqrt(grid_len)).astype(np.float32)


def split_const(values):
    high = values.astype(jnp.bfloat16)
    return high, (values - high.astype(np.float32)).astype(jnp.bfloat16)


def split(values):
    high = values.astype(jnp.bfloat16)
    low = (values - high.astype(f32)).astype(jnp.bfloat16)
    return high, low


def depth_turn(rows, depth_ref):
    width = rows.shape[1]
    high, low = split(rows)
    both = jnp.dot(jnp.concatenate([high, low], axis=1), depth_ref[...],
                   preferred_element_type=f32)
    return both[:, :width] + both[:, width:]


def left_turn(fields, left_ref):
    high, low = split(jnp.concatenate(fields, axis=1))
    return jnp.dot(left_ref[...], jnp.concatenate([high, low, high], axis=0),
                   preferred_element_type=f32)


def unit_of(level):
    return jnp.exp2(level * (1.0 / 64.0))


def encode(block):
    peak = jnp.max(jnp.abs(block), axis=0, keepdims=True)
    level = jnp.ceil(jnp.log2(jnp.maximum(peak, 1e-30) * (1.0 / code_peak)) * 64.0)
    return whole(block * unit_of(-level)), level


def whole(values):
    return jnp.round(values).astype(jnp.int32).astype(jnp.int16)


def plain(code):
    return code.astype(jnp.int32).astype(f32)


def decode(code, unit):
    return plain(code) * unit


def remote(src, dst, send_sem, recv_sem, device):
    return pltpu.make_async_remote_copy(src_ref=src, dst_ref=dst, send_sem=send_sem, recv_sem=recv_sem,
                                        device_id=device, device_id_type=MESH)


def flipped(index, bits):
    turned, bit = index, 1
    while bit <= bits:
        if bits & bit:
            turned = turned + bit - 2 * bit * (index // bit % 2)
        bit *= 2
    return turned


def spread_order(members, half):
    core = half
    plain = sorted((b for b in range(1, members) if not b & core), key=lambda b: (bin(b).count("1"), b))
    order, left = [], list(plain)
    while left:
        first = left.pop(0)
        order.append(first)
        rest = (max(members - 1 - core, 0)) ^ first
        if rest in left:
            left.remove(rest)
            order.append(rest)
    return order + [b | core for b in order] + [core] if members > core else order


def action_kernel(n_orb, n_slab, half, quota, chunks, grid_len, table_hbm, own_ref, depth_hbm,
                  turn_hbm, out_ref, unit_ref, *scratch):
    held = scratch[:chunks]
    (table_ref, depth_ref, turn_ref, tab_own, tables, tab_s, starts, ids, chosen, gain, kern, levels, fsend, frecv, units, work,
     turned, bsend, brecv, terms, parts, rsend, runit, rrecv, rrunit, overlap, packed,
     packed_in, merged, merged_in, coef, result, ysend, yunit,
     load_sem, out_sem, tab_sem, tab_send, tab_recv, own_sem, g_send, g_recv, stay_sem, f_send, f_recv, keep_sem, b_send,
     b_recv, r_send, r_recv, o_send, o_recv, p_send, p_recv, y_send, y_recv) = scratch[chunks:]
    me, me_slab = lax.axis_index("orb"), lax.axis_index("slab")
    group, part = me // half, me % half
    groups, members = n_orb // half, n_slab * half
    place = me_slab * half + part
    own_couples, _, width = own_ref.shape
    couples = n_orb * own_couples
    shared = half * own_couples
    capacity = table_ref.shape[1]
    lines = lines_own
    bands = grid_len // lines
    sets = members // bands
    slots = sets * quota
    runs = quota // batch
    own_planes = grid_len // members
    planes = own_planes // chunks
    rows = planes * grid_len
    tile = planes * lines
    slot_tiles = fsend.shape[2]
    stride = quota if quota <= 12 else batch

    def taker(which, band):
        return (band // half * sets + which) * half + band % half

    my_band = me_slab // sets * half + part

    near = spread_order(members, half)

    def line_to(step):
        return flipped(me, n_orb - step)

    def line_peer(step):
        return {"orb": line_to(step)}

    def member(step):
        to = flipped(place, near[step - 1])
        return to, {"orb": group * half + to % half, "slab": to // half}

    loads = [pltpu.make_async_copy(src, dst, load_sem.at[k]) for k, (src, dst) in enumerate(
        ((table_hbm, table_ref), (depth_hbm, depth_ref), (turn_hbm, turn_ref)))]

    barrier = pltpu.get_barrier_semaphore()
    for step in range(1, n_orb):
        pl.semaphore_signal(barrier, inc=1, device_id=line_peer(step), device_id_type=MESH)
    for slab_step in range(1, n_slab):
        for other in range(half):
            pl.semaphore_signal(
                barrier, inc=1, device_id={"orb": group * half + other,
                                           "slab": lax.rem(me_slab + slab_step, n_slab)},
                device_id_type=MESH)

    def plane_rows(which, chunk):
        return pl.ds(pl.multiple_of((which * chunks + chunk) * rows, rows), rows)

    def tab_copy(step):
        return remote(tab_own, tables.at[me], tab_send.at[step - 1], tab_recv.at[step - 1],
                      line_peer(step))

    def plane_row(which, plane):
        return pl.ds(pl.multiple_of((which * own_planes + plane) * grid_len, grid_len), grid_len)

    def gather_copy(chunk, step):
        to = line_to(step)
        return remote(own_ref.at[:, plane_rows(to % half, chunk)],
                      held[chunk].at[pl.ds(me * own_couples, own_couples)],
                      g_send.at[chunk, step - 1], g_recv.at[chunk, step - 1], line_peer(step))

    def own_copy(chunk):
        return pltpu.make_async_copy(own_ref.at[:, plane_rows(part, chunk)],
                                     held[chunk].at[pl.ds(me * own_couples, own_couples)],
                                     own_sem.at[chunk])

    def fwd_copy(chunk, step):
        to, device = member(step)
        return remote(fsend.at[chunk, to], frecv.at[chunk, place], f_send.at[chunk, step - 1],
                      f_recv.at[chunk, step - 1], device)

    def fwd_stay(chunk):
        return pltpu.make_async_copy(fsend.at[chunk, place], frecv.at[chunk, place], stay_sem.at[chunk])

    def back_copy(chunk, step, run=0):
        to, device = member(step)
        some, at = pl.ds(0, slot_tiles), runs - 1 + chunk
        if chunk == 0:
            some, at = pl.ds(run * batch, batch), run
            if isinstance(run, int) and run == runs - 1:
                some = pl.ds(run * batch, slot_tiles - run * batch)
        return remote(bsend.at[chunk, to, some], brecv.at[chunk, place, some], b_send.at[at, step - 1],
                      b_recv.at[at, step - 1], device)

    def back_parts(chunk, step):
        return [back_copy(chunk, step, run) for run in range(runs if chunk == 0 else 1)]

    def back_stay(chunk):
        return pltpu.make_async_copy(bsend.at[chunk, place], brecv.at[chunk, place], keep_sem.at[chunk])

    def sum_copies(plane, step):
        to = lax.rem(group + step, groups)
        theirs = pl.ds(to * shared, shared)
        device = {"orb": to * half + part}
        return (remote(rsend.at[plane, theirs], rrecv.at[plane, step - 1], r_send.at[0, plane, step - 1],
                       r_recv.at[0, plane, step - 1], device),
                remote(runit.at[plane, theirs], rrunit.at[plane, step - 1], r_send.at[1, plane, step - 1],
                       r_recv.at[1, plane, step - 1], device))

    def overlap_copy(step):
        to = lax.rem(group + step, groups)
        return remote(packed.at[to], packed_in.at[step - 1], o_send.at[step - 1], o_recv.at[step - 1],
                      {"orb": to * half + part})

    def merged_copy(step):
        return remote(merged, merged_in.at[step - 1], p_send.at[step - 1], p_recv.at[step - 1],
                      member(step)[1])

    def result_stay(plane):
        mine = pl.ds(part * own_couples, own_couples)
        return (pltpu.make_async_copy(ysend.at[plane, mine], out_ref.at[:, plane_row(part, plane)],
                                      out_sem.at[0, plane]),
                pltpu.make_async_copy(yunit.at[plane, mine], unit_ref.at[:, part * own_planes + plane],
                                      out_sem.at[1, plane]))

    def result_copies(plane, hop):
        to = flipped(part, hop)
        theirs, device = pl.ds(to * own_couples, own_couples), {"orb": group * half + to}
        return (remote(ysend.at[plane, theirs], out_ref.at[:, plane_row(part, plane)],
                       y_send.at[0, plane, hop - 1], y_recv.at[0, plane, hop - 1], device),
                remote(yunit.at[plane, theirs], unit_ref.at[:, part * own_planes + plane],
                       y_send.at[1, plane, hop - 1], y_recv.at[1, plane, hop - 1], device))

    for load in loads:
        load.start()
    tab_own[...] = jnp.full(tab_own.shape, -1, jnp.int32)
    loads[0].wait()
    tab_own[0:3, 0:capacity] = table_ref[...]
    kz = lax.broadcasted_iota(jnp.int32, (grid_len, width), 1) % grid_len
    fz = jnp.minimum(kz, grid_len - kz).astype(f32)
    ky = lax.broadcasted_iota(jnp.int32, (grid_len, width), 0)
    fy = jnp.minimum(ky, grid_len - ky).astype(f32)
    plane_sq = fy * fy + fz * fz
    deep = cell_ratio * cell_ratio
    gain[...] = 1.0 / jnp.where(plane_sq > 0, plane_sq, deep)
    fx = cell_ratio * fy
    scale_k = (2.0 * math.pi / grid_len) * (2.0 * math.pi / grid_len)
    for line in range(lines):
        at = my_band * lines + line
        fl = jnp.minimum(at, grid_len - at).astype(f32)
        plane = fl * fl + fz * fz
        full = fx * fx + plane
        level = jnp.where(plane > 0, plane, deep)
        kern[:, line * width:(line + 1) * width] = jnp.where(
            full > 0, (-exchange_fraction / scale_k) * level / jnp.where(full > 0, full, 1.0), 0.0)
    terms[2 * slots] = jnp.zeros(terms.shape[1:], f32)
    overlap[...] = jnp.zeros(overlap.shape, f32)
    levels[...] = jnp.zeros(levels.shape, f32)

    pl.semaphore_wait(barrier, n_orb - 1 + (n_slab - 1) * half)
    for step in range(1, n_orb):
        tab_copy(step).start()
    for chunk in range(chunks):
        for step in range(1, n_orb):
            gather_copy(chunk, step).start()
        own_copy(chunk).start()
    tables[me] = tab_own[...]

    for step in range(1, n_orb):
        tab_copy(step).wait_recv()
    to_scalars = pltpu.make_async_copy(tables, tab_s, tab_sem)
    to_scalars.start()
    to_scalars.wait()

    def count_block(block, total):
        starts[block] = total
        return lax.fori_loop(
            0, capacity, lambda k, sum_in: sum_in + (tab_s[block, 0, k] >= 0).astype(jnp.int32), total)

    live = lax.fori_loop(0, n_orb, count_block, jnp.int32(0))

    @pl.loop(0, slots)
    def _(slot):
        wanted = slot * groups + group
        used = wanted < live
        block = lax.fori_loop(
            1, n_orb, lambda b, sum_in: sum_in + (starts[b] <= wanted).astype(jnp.int32), jnp.int32(0))
        column = jnp.clip(wanted - starts[block], 0, capacity - 1)
        for k in range(3):
            ids[slot, k] = jnp.maximum(tab_s[block, k, column], 0)
        for k in range(2):
            ids[slot, 3 + k] = jnp.where(used, tab_s[block, k, column], -1)

    def pair_of(chunk, slot, span):
        left = held[chunk][ids[slot, 0], span].astype(f32)
        right = held[chunk][ids[slot, 1], span].astype(f32)
        crossed = ids[slot, 2] == 1
        return left, jnp.where(crossed, pltpu.roll(right, grid_len, 1), right), crossed

    def put_levels(ref, chunk, to):
        for k in range(slot_tiles - quota):
            ref[chunk, to, quota + k] = whole(levels[chunk, to, k * tile:(k + 1) * tile])

    def take_units(ref, chunk):
        for src in range(members):
            for k in range(slot_tiles - quota):
                units[chunk, src, k * tile:(k + 1) * tile] = unit_of(plain(ref[chunk, src, quota + k]))

    def advance(chunk):
        own_copy(chunk).wait()
        for step in range(1, n_orb):
            gather_copy(chunk, step).wait_recv()

        for which in range(sets):
            @pl.loop(0, quota, step=batch)
            def _(base):
                pairs = [pair_of(chunk, which * quota + base + k, slice(None)) for k in range(batch)]
                flat = depth_turn(jnp.concatenate([left * partner for left, partner, _ in pairs], axis=0),
                                  depth_ref)
                done = left_turn([flat[k * grid_len:(k + 1) * grid_len] for k in range(2 * batch)], turn_ref)
                for k in range(batch):
                    one = done[:, 2 * k * width:(2 * k + 1) * width] * gain[...]
                    two = done[:, (2 * k + 1) * width:(2 * k + 2) * width] * gain[...]
                    for band in range(bands):
                        to = taker(which, band)
                        span = slice(band * lines, (band + 1) * lines)
                        code, level = encode(jnp.concatenate([one[span], two[span]], axis=0))
                        fsend[chunk, to, base + k] = code
                        levels[chunk, to, pl.ds(base + k, 1)] = level

            for band in range(bands):
                put_levels(fsend, chunk, taker(which, band))
            for step in range(1, members):
                to = member(step)[0]

                @pl.when(to // half % sets == which)
                def _():
                    fwd_copy(chunk, step).start()

        fwd_stay(chunk).start()

    for load in loads[1:]:
        load.wait()
    for chunk in range(chunks):
        advance(chunk)

    @pl.loop(0, slots)
    def _(slot):
        @pl.loop(0, couples)
        def _(couple):
            chosen[couple, slot] = jnp.where(
                ids[slot, 3] == couple, 2 * slot, jnp.where(ids[slot, 4] == couple, 2 * slot + 1, 2 * slots))

    for chunk in range(chunks):
        fwd_stay(chunk).wait()
        for step in range(1, members):
            fwd_copy(chunk, step).wait_recv()

        take_units(frecv, chunk)

    @pl.loop(0, quota, step=batch)
    def _(base):
        for k in range(batch):
            for src in range(members):
                for chunk in range(chunks):
                    at = (src * chunks + chunk) * tile
                    work[k, at:at + tile] = decode(frecv[chunk, src, base + k],
                                                   units[chunk, src, pl.ds(base + k, 1)])
            done = left_turn([work[k, pl.ds(line, grid_len, stride=lines), :] for line in range(lines)],
                             turn_ref)
            done = done * kern[...]
            back = left_turn([done[:, line * width:(line + 1) * width] for line in range(lines)], turn_ref)
            for line in range(lines):
                turned[k, pl.ds(line, grid_len, stride=lines), :] = back[:, line * width:(line + 1) * width]
            for to in range(members):
                for chunk in range(chunks):
                    at = (to * chunks + chunk) * tile
                    code, level = encode(turned[k, at:at + tile])
                    bsend[chunk, to, base + k] = code
                    levels[chunk, to, pl.ds(base + k, 1)] = level

        @pl.when(base < quota - batch)
        def _():
            for step in range(1, members):
                back_copy(0, step, base // batch).start()

    for chunk in range(chunks):
        for to in range(members):
            put_levels(bsend, chunk, to)
        for step in range(1, members):
            back_copy(chunk, step, 0 if chunk else runs - 1).start()
        back_stay(chunk).start()

    def retreat(plane):
        chunk, sub = plane // planes, plane % planes
        if sub == 0:
            back_stay(chunk).wait()
            for step in range(1, members):
                for copy in back_parts(chunk, step):
                    copy.wait_recv()
            take_units(brecv, chunk)
        near_rows, span = slice(sub * lines, (sub + 1) * lines), slice(sub * grid_len, (sub + 1) * grid_len)

        for which in range(sets):
            @pl.loop(0, quota, step=stride)
            def _(base):
                fields = [
                    jnp.concatenate([decode(brecv[chunk, taker(which, band), base + k, near_rows],
                                            units[chunk, taker(which, band), pl.ds(base + k, 1)])
                                     for band in range(bands)], axis=0)
                    for k in range(stride)]
                done = left_turn(fields, turn_ref)
                potentials = depth_turn(jnp.concatenate(
                    [done[:, k * width:(k + 1) * width] for k in range(stride)], axis=0), depth_ref)
                for k in range(stride):
                    slot = which * quota + base + k
                    potential = potentials[k * grid_len:(k + 1) * grid_len]
                    left, partner, crossed = pair_of(chunk, slot, span)
                    terms[2 * slot] = potential * partner
                    second = potential * left
                    terms[2 * slot + 1] = jnp.where(crossed, pltpu.roll(second, grid_len, 1), second)

        @pl.loop(0, couples)
        def _(couple):
            total = terms[chosen[couple, 0]]
            for slot in range(1, slots):
                total = total + terms[chosen[couple, slot]]
            parts[plane, couple] = total
            code, level = encode(total)
            rsend[plane, couple] = code
            runit[plane, couple] = unit_of(level)
            across = pltpu.roll(total, grid_len, 1)
            at = couple % shared * couples
            for other in range(couples):
                basis = held[chunk][other, span].astype(f32)
                for kind, field in enumerate((total, across)):
                    row = pl.ds(at + kind * shared * couples + other, 1)
                    overlap[couple // shared, row] += jnp.sum(basis * field, axis=0, keepdims=True)

    for plane in range(own_planes - 1):
        retreat(plane)
        for step in range(1, groups):
            for copy in sum_copies(plane, step):
                copy.start()
    retreat(own_planes - 1)

    lane = lax.broadcasted_iota(jnp.int32, (8, width), 1)
    halves = ((lane // grid_len) == lax.broadcasted_iota(jnp.int32, (8, width), 0)).astype(jnp.bfloat16)

    def thirds(values):
        high = values.astype(jnp.bfloat16)
        rest = values - high.astype(f32)
        mid = rest.astype(jnp.bfloat16)
        return high, mid, (rest - mid.astype(f32)).astype(jnp.bfloat16)

    for which in range(groups):
        packed[which] = sum(lax.dot_general(halves, third, (((1,), (1,)), ((), ())),
                                            preferred_element_type=f32)
                            for third in thirds(overlap[which]))
    for step in range(1, groups):
        overlap_copy(step).start()
    for step in range(1, groups):
        for copy in sum_copies(own_planes - 1, step):
            copy.start()
    total = packed[group]
    for step in range(1, groups):
        overlap_copy(step).wait_recv()
        total = total + packed_in[step - 1]
    merged[...] = total
    for step in range(1, members):
        merged_copy(step).start()
    for step in range(1, members):
        merged_copy(step).wait_recv()
        total = total + merged_in[step - 1]
    total = total * (1.0 / (grid_len * grid_len * grid_len))
    coef[...] = sum(lax.dot_general(third, halves, (((0,), (0,)), ((), ())), preferred_element_type=f32)
                    for third in thirds(total))

    strip = grid_len // 2
    for plane in range(own_planes):
        chunk, first = plane // planes, plane % planes * grid_len
        for step in range(1, groups):
            for copy in sum_copies(plane, step):
                copy.wait_recv()

        @pl.loop(0, grid_len // strip)
        def _(at):
            here = pl.ds(pl.multiple_of(at * strip, strip), strip)
            there = pl.ds(pl.multiple_of(first + at * strip, strip), strip)
            kept = [jnp.zeros((strip, width), f32) for _ in range(2 * shared)]
            for couple in range(couples):
                basis = held[chunk][couple, there].astype(f32)
                for k in range(2 * shared):
                    row = k * couples + couple
                    kept[k] = kept[k] + coef[row:row + 1] * basis
            for k in range(shared):
                total = parts[plane, group * shared + k, here]
                for step in range(1, groups):
                    total = total + decode(rrecv[plane, step - 1, k, here], rrunit[plane, step - 1, k])
                result[k, here] = total - kept[k] - pltpu.roll(kept[shared + k], grid_len, 1)

        for k in range(shared):
            code, level = encode(result[k])
            ysend[plane, k] = code
            yunit[plane, k] = unit_of(level)
        for hop in range(1, half):
            for copy in result_copies(plane, hop):
                copy.start()
        for copy in result_stay(plane):
            copy.start()

    for plane in range(own_planes):
        for copy in result_stay(plane):
            copy.wait()
        for hop in range(1, half):
            for copy in result_copies(plane, hop):
                copy.wait()
        for step in range(1, groups):
            for copy in sum_copies(plane, step):
                copy.wait_send()
    for chunk in range(chunks):
        for step in range(1, members):
            fwd_copy(chunk, step).wait_send()
            for copy in back_parts(chunk, step):
                copy.wait_send()
        for step in range(1, n_orb):
            gather_copy(chunk, step).wait_send()
    for step in range(1, groups):
        overlap_copy(step).wait_send()
    for step in range(1, members):
        merged_copy(step).wait_send()
    for step in range(1, n_orb):
        tab_copy(step).wait_send()


def local(orbitals, pair_table, n_orb, n_slab):
    own_couples, slab_len, grid_len, width = orbitals.shape
    capacity = pair_table.shape[0]
    half = max(1, cube // n_slab)
    members = n_slab * half
    groups = n_orb // half
    bands = grid_len // lines_own
    sets = members // bands
    live_total = sum(capacity * (k + 1) // n_orb for k in range(n_orb))
    quota = -(-live_total // (groups * sets * batch)) * batch
    slots = sets * quota
    couples, shared = n_orb * own_couples, half * own_couples
    planes = grid_len // members
    chunks = planes // 2
    rows, tile = 2 * grid_len, 2 * lines_own
    level_tiles = -(-quota // tile)
    overlap_rows = -(-2 * shared * couples // 128) * 128
    tab_lanes = -(-capacity // 128) * 128

    mat = hartley(grid_len)
    mat_high, mat_low = split_const(mat)
    turn_mat = jnp.asarray(np.concatenate([mat_high, mat_high, mat_low], axis=1))
    deep_high, deep_low = split_const(np.kron(np.eye(2, dtype=np.float32), mat))
    depth_mat = jnp.asarray(np.block([[deep_high, deep_low], [deep_high, np.zeros_like(deep_low)]]))

    dma, vmem, smem = pltpu.SemaphoreType.DMA, pltpu.VMEM, pltpu.SMEM
    i32, i16 = jnp.int32, jnp.int16
    bf16 = orbitals.dtype
    coded = vmem((chunks, members, quota + level_tiles, tile, width), i16)
    per_slot = vmem((chunks, members, level_tiles * tile, width), f32)
    lines_sem = dma((chunks, n_orb - 1))
    cross_sem = dma((chunks, members - 1))
    back_sem = dma((quota // batch + chunks - 1, members - 1))
    steps = max(groups - 1, 1)
    sum_sem = dma((2, planes, steps))
    hops = max(half - 1, 1)
    code, unit = pl.pallas_call(
        functools.partial(action_kernel, n_orb, n_slab, half, quota, chunks, grid_len),
        out_shape=(jax.ShapeDtypeStruct((own_couples, slab_len * grid_len, width), i16),
                   jax.ShapeDtypeStruct((own_couples, slab_len, 1, width), f32)),
        in_specs=[HBM_SPEC] * 4,
        out_specs=(HBM_SPEC, HBM_SPEC),
        scratch_shapes=[vmem((couples, rows, width), orbitals.dtype)] * chunks + [
            vmem((3, capacity), i32), vmem(depth_mat.shape, bf16), vmem(turn_mat.shape, bf16),
            vmem((8, tab_lanes), i32), vmem((n_orb, 8, tab_lanes), i32), smem((n_orb, 8, tab_lanes), i32),
            smem((n_orb,), i32), smem((slots, 5), i32), smem((couples, slots), i32),
            vmem((grid_len, width), f32), vmem((grid_len, lines_own * width), f32),
            per_slot, coded, coded, per_slot,
            vmem((batch, lines_own * grid_len, width), f32), vmem((batch, lines_own * grid_len, width), f32),
            coded, coded,
            vmem((2 * slots + 1, grid_len, width), f32),
            vmem((planes, couples, grid_len, width), f32),
            vmem((planes, couples, grid_len, width), i16), vmem((planes, couples, 1, width), f32),
            vmem((planes, steps, shared, grid_len, width), i16), vmem((planes, steps, shared, 1, width), f32),
            vmem((groups, overlap_rows, width), f32), vmem((groups, 8, overlap_rows), f32),
            vmem((steps, 8, overlap_rows), f32), vmem((8, overlap_rows), f32),
            vmem((members - 1, 8, overlap_rows), f32), vmem((overlap_rows, width), f32),
            vmem((shared, grid_len, width), f32),
            vmem((planes, shared, grid_len, width), i16), vmem((planes, shared, 1, width), f32),
            dma((3,)), dma((2, planes)), dma, dma((n_orb - 1,)), dma((n_orb - 1,)), dma((chunks,)), lines_sem, lines_sem,
            dma((chunks,)), cross_sem, cross_sem, dma((chunks,)), back_sem, back_sem,
            sum_sem, sum_sem, dma((steps,)), dma((steps,)), dma((members - 1,)), dma((members - 1,)),
            dma((2, planes, hops)), dma((2, planes, hops)),
        ],
        compiler_params=pltpu.CompilerParams(collective_id=0, has_side_effects=True,
                                             vmem_limit_bytes=56 << 20),
    )(pair_table.T, orbitals.reshape(own_couples, slab_len * grid_len, width), depth_mat, turn_mat)
    return code.reshape(orbitals.shape).astype(f32) * unit


def solution(mesh):
    placed = (P("orb", "slab", None, None), P("orb", None))
    return jax.shard_map(
        functools.partial(local, n_orb=mesh.shape["orb"], n_slab=mesh.shape["slab"]),
        mesh=mesh, in_specs=placed, out_specs=P("orb", "slab", None, None), check_vma=False
    )
```

```python
import functools
import math

import jax
import jax.numpy as jnp
import numpy as np
from jax import lax
from jax.experimental import pallas as pl
from jax.experimental.pallas import tpu as pltpu
from jax.sharding import PartitionSpec as P

exchange_fraction = 0.25
cell_ratio = 8.0
lines_own = 8
cube = 16
batch = 3
code_peak = 32700.0
MESH = pl.DeviceIdType.MESH
HBM_SPEC = pl.BlockSpec(memory_space=pltpu.HBM)
f32 = jnp.float32


def hartley(grid_len):
    rows_idx = np.arange(grid_len)
    angles = 2.0 * math.pi / grid_len * (rows_idx[:, None] * rows_idx[None, :] % grid_len)
    return ((np.cos(angles) + np.sin(angles)) / math.sqrt(grid_len)).astype(np.float32)


def split_const(values):
    high = values.astype(jnp.bfloat16)
    return high, (values - high.astype(np.float32)).astype(jnp.bfloat16)


def split(values):
    high = values.astype(jnp.bfloat16)
    low = (values - high.astype(f32)).astype(jnp.bfloat16)
    return high, low


def depth_turn(rows, depth_ref):
    width = rows.shape[1]
    high, low = split(rows)
    both = jnp.dot(jnp.concatenate([high, low], axis=1), depth_ref[...],
                   preferred_element_type=f32)
    return both[:, :width] + both[:, width:]


def left_turn(fields, left_ref):
    high, low = split(jnp.concatenate(fields, axis=1))
    return jnp.dot(left_ref[...], jnp.concatenate([high, low, high], axis=0),
                   preferred_element_type=f32)


def unit_of(level):
    return jnp.exp2(level * (1.0 / 64.0))


def encode(block):
    peak = jnp.max(jnp.abs(block), axis=0, keepdims=True)
    level = jnp.ceil(jnp.log2(jnp.maximum(peak, 1e-30) * (1.0 / code_peak)) * 64.0)
    return whole(block * unit_of(-level)), level


def whole(values):
    return jnp.round(values).astype(jnp.int32).astype(jnp.int16)


def plain(code):
    return code.astype(jnp.int32).astype(f32)


def decode(code, unit):
    return plain(code) * unit


def remote(src, dst, send_sem, recv_sem, device):
    return pltpu.make_async_remote_copy(src_ref=src, dst_ref=dst, send_sem=send_sem, recv_sem=recv_sem,
                                        device_id=device, device_id_type=MESH)


def flipped(index, bits):
    turned, bit = index, 1
    while bit <= bits:
        if bits & bit:
            turned = turned + bit - 2 * bit * (index // bit % 2)
        bit *= 2
    return turned


def spread_order(members, half):
    core = half
    plain = sorted((b for b in range(1, members) if not b & core), key=lambda b: (bin(b).count("1"), b))
    order, left = [], list(plain)
    while left:
        first = left.pop(0)
        order.append(first)
        rest = (max(members - 1 - core, 0)) ^ first
        if rest in left:
            left.remove(rest)
            order.append(rest)
    return order + [b | core for b in order] + [core] if members > core else order


def action_kernel(n_orb, n_slab, half, quota, chunks, grid_len, table_hbm, own_ref, depth_hbm,
                  turn_hbm, out_ref, unit_ref, *scratch):
    held = scratch[:chunks]
    (table_ref, depth_ref, turn_ref, tab_own, tables, tab_s, starts, ids, chosen, gain, kern, levels, fsend, frecv, funit, funit_in, units, work,
     turned, bsend, brecv, terms, parts, rsend, runit, rrecv, rrunit, overlap, packed,
     packed_in, merged, merged_in, coef, result, ysend, yunit,
     load_sem, out_sem, tab_sem, tab_send, tab_recv, own_sem, g_send, g_recv, stay_sem, f_send, f_recv, s_send, s_recv, keep_sem, b_send,
     b_recv, r_send, r_recv, o_send, o_recv, p_send, p_recv, y_send, y_recv) = scratch[chunks:]
    me, me_slab = lax.axis_index("orb"), lax.axis_index("slab")
    group, part = me // half, me % half
    groups, members = n_orb // half, n_slab * half
    place = me_slab * half + part
    own_couples, _, width = own_ref.shape
    couples = n_orb * own_couples
    shared = half * own_couples
    capacity = table_ref.shape[1]
    lines = lines_own
    bands = grid_len // lines
    sets = members // bands
    slots = sets * quota
    runs = quota // batch
    own_planes = grid_len // members
    planes = own_planes // chunks
    rows = planes * grid_len
    tile = planes * lines
    slot_tiles = fsend.shape[2]

    def taker(which, band):
        return (band // half * sets + which) * half + band % half

    my_band = me_slab // sets * half + part

    near = spread_order(members, half)

    def line_to(step):
        return flipped(me, n_orb - step)

    def line_peer(step):
        return {"orb": line_to(step)}

    def member(step):
        to = flipped(place, near[step - 1])
        return to, {"orb": group * half + to % half, "slab": to // half}

    loads = [pltpu.make_async_copy(src, dst, load_sem.at[k]) for k, (src, dst) in enumerate(
        ((table_hbm, table_ref), (depth_hbm, depth_ref), (turn_hbm, turn_ref)))]

    barrier = pltpu.get_barrier_semaphore()
    for step in range(1, n_orb):
        pl.semaphore_signal(barrier, inc=1, device_id=line_peer(step), device_id_type=MESH)
    for slab_step in range(1, n_slab):
        for other in range(half):
            pl.semaphore_signal(
                barrier, inc=1, device_id={"orb": group * half + other,
                                           "slab": lax.rem(me_slab + slab_step, n_slab)},
                device_id_type=MESH)

    def plane_rows(which, chunk):
        return pl.ds(pl.multiple_of((which * chunks + chunk) * rows, rows), rows)

    def tab_copy(step):
        return remote(tab_own, tables.at[me], tab_send, tab_recv, line_peer(step))

    def tab_all():
        every = tables.at[pl.ds(0, n_orb - 1)]
        return remote(every, every, tab_send, tab_recv, line_peer(1))

    def plane_row(which, plane):
        return pl.ds(pl.multiple_of((which * own_planes + plane) * grid_len, grid_len), grid_len)

    def gather_copy(chunk, step):
        to = line_to(step)
        return remote(own_ref.at[:, plane_rows(to % half, chunk)],
                      held[chunk].at[pl.ds(me * own_couples, own_couples)],
                      g_send.at[chunk], g_recv.at[chunk], line_peer(step))

    def gather_all(chunk):
        every = held[chunk].at[pl.ds(0, couples - own_couples)]
        return remote(every, every, g_send.at[chunk], g_recv.at[chunk], line_peer(1))

    def own_copy(chunk):
        return pltpu.make_async_copy(own_ref.at[:, plane_rows(part, chunk)],
                                     held[chunk].at[pl.ds(me * own_couples, own_couples)],
                                     own_sem.at[chunk])

    last = chunks - 1

    def fwd_copy(chunk, step):
        to, device = member(step)
        return remote(fsend.at[chunk, to], frecv.at[chunk, place], f_send.at[chunk], f_recv.at[chunk], device)

    others = pl.ds(0, members - 1)

    def fwd_all(chunk):
        return remote(fsend.at[chunk, others], frecv.at[chunk, others], f_send.at[chunk], f_recv.at[chunk],
                      member(1)[1])

    def fwd_stay(chunk):
        return pltpu.make_async_copy(fsend.at[chunk, place], frecv.at[chunk, place], stay_sem.at[chunk])

    def fwd_run(step, run):
        to, device = member(step)
        some = pl.ds(run * batch, batch)
        at = last + run
        return (remote(fsend.at[last, to, some], frecv.at[last, place, some], f_send.at[at], f_recv.at[at],
                       device),
                remote(funit.at[to, run], funit_in.at[place, run], s_send.at[run], s_recv.at[run], device))

    def fwd_run_all(run):
        some = pl.ds(run * batch, batch)
        at = last + run
        return (remote(fsend.at[last, others, some], frecv.at[last, others, some], f_send.at[at],
                       f_recv.at[at], member(1)[1]),
                remote(funit.at[others, run], funit_in.at[others, run], s_send.at[run], s_recv.at[run],
                       member(1)[1]))

    def fwd_stay_run(run):
        some = pl.ds(run * batch, batch)
        return (pltpu.make_async_copy(fsend.at[last, place, some], frecv.at[last, place, some],
                                      stay_sem.at[last + run]),
                pltpu.make_async_copy(funit.at[place, run], funit_in.at[place, run],
                                      stay_sem.at[last + runs + run]))

    def slot_at(chunk, slot):
        return slot + (slot_tiles - quota if chunk == last else 0)

    def back_run(chunk, run):
        some, at = pl.ds(slot_at(chunk, run * batch), batch), chunk * runs + run
        if isinstance(run, int):
            if chunk == last and run == 0:
                some = pl.ds(0, slot_tiles - quota + batch)
            elif chunk < last and run == runs - 1:
                some = pl.ds(run * batch, slot_tiles - run * batch)
        return some, at

    def back_copy(chunk, step, run):
        to, device = member(step)
        some, at = back_run(chunk, run)
        return remote(bsend.at[chunk, to, some], brecv.at[chunk, place, some], b_send.at[at], b_recv.at[at],
                      device)

    def back_all(chunk, run):
        some, at = back_run(chunk, run)
        return remote(bsend.at[chunk, others, some], brecv.at[chunk, others, some], b_send.at[at],
                      b_recv.at[at], member(1)[1])

    def back_stay(chunk):
        return pltpu.make_async_copy(bsend.at[chunk, place], brecv.at[chunk, place], keep_sem.at[chunk])

    def sum_copies(plane, step):
        to = lax.rem(group + step, groups)
        theirs = pl.ds(to * shared, shared)
        device = {"orb": to * half + part}
        return (remote(rsend.at[plane, theirs], rrecv.at[plane, step - 1], r_send.at[0, plane],
                       r_recv.at[0, plane], device),
                remote(runit.at[plane, theirs], rrunit.at[plane, step - 1], r_send.at[1, plane],
                       r_recv.at[1, plane], device))

    def sum_all(plane):
        device = {"orb": lax.rem(group + 1, groups) * half + part}
        return [remote(ref.at[plane], ref.at[plane], r_send.at[k, plane], r_recv.at[k, plane], device)
                for k, ref in enumerate((rrecv, rrunit))]

    def overlap_copy(step):
        to = lax.rem(group + step, groups)
        return remote(packed.at[to], packed_in.at[step - 1], o_send, o_recv,
                      {"orb": to * half + part})

    def overlap_all():
        return remote(packed_in, packed_in, o_send, o_recv, {"orb": lax.rem(group + 1, groups) * half + part})

    def merged_copy(step):
        return remote(merged, merged_in.at[step - 1], p_send, p_recv, member(step)[1])

    def merged_all():
        return remote(merged_in, merged_in, p_send, p_recv, member(1)[1])

    def result_stay(plane):
        mine = pl.ds(part * own_couples, own_couples)
        return (pltpu.make_async_copy(ysend.at[plane, mine], out_ref.at[:, plane_row(part, plane)],
                                      out_sem.at[0, plane]),
                pltpu.make_async_copy(yunit.at[plane, mine], unit_ref.at[:, part * own_planes + plane],
                                      out_sem.at[1, plane]))

    def result_copies(plane, hop):
        to = flipped(part, hop)
        theirs, device = pl.ds(to * own_couples, own_couples), {"orb": group * half + to}
        return (remote(ysend.at[plane, theirs], out_ref.at[:, plane_row(part, plane)],
                       y_send.at[0], y_recv.at[0], device),
                remote(yunit.at[plane, theirs], unit_ref.at[:, part * own_planes + plane],
                       y_send.at[1], y_recv.at[1], device))

    def result_all():
        theirs = pl.ds(0, shared - own_couples)
        device = {"orb": group * half + flipped(part, 1)}
        return [remote(ref.at[:, theirs], ref.at[:, theirs], y_send.at[k], y_recv.at[k], device)
                for k, ref in enumerate((ysend, yunit))]

    for load in loads:
        load.start()
    tab_own[...] = jnp.full(tab_own.shape, -1, jnp.int32)
    loads[0].wait()
    tab_own[0:3, 0:capacity] = table_ref[...]
    kz = lax.broadcasted_iota(jnp.int32, (grid_len, width), 1) % grid_len
    fz = jnp.minimum(kz, grid_len - kz).astype(f32)
    ky = lax.broadcasted_iota(jnp.int32, (grid_len, width), 0)
    fy = jnp.minimum(ky, grid_len - ky).astype(f32)
    plane_sq = fy * fy + fz * fz
    deep = cell_ratio * cell_ratio
    gain[...] = 1.0 / jnp.where(plane_sq > 0, plane_sq, deep)
    fx = cell_ratio * fy
    scale_k = (2.0 * math.pi / grid_len) * (2.0 * math.pi / grid_len)
    for line in range(lines):
        at = my_band * lines + line
        fl = jnp.minimum(at, grid_len - at).astype(f32)
        plane = fl * fl + fz * fz
        full = fx * fx + plane
        level = jnp.where(plane > 0, plane, deep)
        kern[:, line * width:(line + 1) * width] = jnp.where(
            full > 0, (-exchange_fraction / scale_k) * level / jnp.where(full > 0, full, 1.0), 0.0)
    terms[2 * slots] = jnp.zeros(terms.shape[1:], f32)
    overlap[...] = jnp.zeros(overlap.shape, f32)
    levels[...] = jnp.zeros(levels.shape, f32)

    pl.semaphore_wait(barrier, n_orb - 1 + (n_slab - 1) * half)
    for step in range(1, n_orb):
        tab_copy(step).start()
    for chunk in range(chunks):
        for step in range(1, n_orb):
            gather_copy(chunk, step).start()
        own_copy(chunk).start()
    tables[me] = tab_own[...]

    tab_all().wait_recv()
    to_scalars = pltpu.make_async_copy(tables, tab_s, tab_sem)
    to_scalars.start()
    to_scalars.wait()

    def count_block(block, total):
        starts[block] = total
        return lax.fori_loop(
            0, capacity, lambda k, sum_in: sum_in + (tab_s[block, 0, k] >= 0).astype(jnp.int32), total)

    live = lax.fori_loop(0, n_orb, count_block, jnp.int32(0))

    @pl.loop(0, slots)
    def _(slot):
        wanted = slot * groups + group
        used = wanted < live
        block = lax.fori_loop(
            1, n_orb, lambda b, sum_in: sum_in + (starts[b] <= wanted).astype(jnp.int32), jnp.int32(0))
        column = jnp.clip(wanted - starts[block], 0, capacity - 1)
        for k in range(3):
            ids[slot, k] = jnp.maximum(tab_s[block, k, column], 0)
        for k in range(2):
            ids[slot, 3 + k] = jnp.where(used, tab_s[block, k, column], -1)

    def pair_of(chunk, slot, span):
        left = held[chunk][ids[slot, 0], span].astype(f32)
        right = held[chunk][ids[slot, 1], span].astype(f32)
        crossed = ids[slot, 2] == 1
        return left, jnp.where(crossed, pltpu.roll(right, grid_len, 1), right), crossed

    def put_levels(ref, chunk, to, first):
        for k in range(slot_tiles - quota):
            ref[chunk, to, first + k] = whole(levels[chunk, to, k * tile:(k + 1) * tile])

    def take_units(ref, chunk, first):
        for src in range(members):
            for k in range(slot_tiles - quota):
                units[chunk, src, k * tile:(k + 1) * tile] = unit_of(plain(ref[chunk, src, first + k]))

    def advance(chunk):
        own_copy(chunk).wait()
        gather_all(chunk).wait_recv()

        def densities(which, base, keep):
            pairs = [pair_of(chunk, which * quota + base + k, slice(None)) for k in range(batch)]
            flat = depth_turn(jnp.concatenate([left * partner for left, partner, _ in pairs], axis=0),
                              depth_ref)
            done = left_turn([flat[k * grid_len:(k + 1) * grid_len] for k in range(2 * batch)], turn_ref)
            for k in range(batch):
                one = done[:, 2 * k * width:(2 * k + 1) * width] * gain[...]
                two = done[:, (2 * k + 1) * width:(2 * k + 2) * width] * gain[...]
                for band in range(bands):
                    to = taker(which, band)
                    span = slice(band * lines, (band + 1) * lines)
                    code, level = encode(jnp.concatenate([one[span], two[span]], axis=0))
                    fsend[chunk, to, base + k] = code
                    keep(to, base, k, level)

        def keep_level(to, base, k, level):
            levels[chunk, to, pl.ds(base + k, 1)] = level

        def keep_unit(to, base, k, level):
            funit[to, base // batch, k] = unit_of(level)

        if chunk < last:
            for which in range(sets):
                @pl.loop(0, quota, step=batch)
                def _(base):
                    densities(which, base, keep_level)

                for band in range(bands):
                    put_levels(fsend, chunk, taker(which, band), quota)
                for step in range(1, members):
                    to = member(step)[0]

                    @pl.when(to // half % sets == which)
                    def _():
                        fwd_copy(chunk, step).start()

            fwd_stay(chunk).start()
        else:
            for run in range(runs):
                for which in range(sets):
                    densities(which, run * batch, keep_unit)
                for step in range(1, members):
                    for copy in fwd_run(step, run):
                        copy.start()
                for copy in fwd_stay_run(run):
                    copy.start()

    for load in loads[1:]:
        load.wait()
    for chunk in range(chunks):
        advance(chunk)

    @pl.loop(0, slots)
    def _(slot):
        @pl.loop(0, couples)
        def _(couple):
            chosen[couple, slot] = jnp.where(
                ids[slot, 3] == couple, 2 * slot, jnp.where(ids[slot, 4] == couple, 2 * slot + 1, 2 * slots))

    for chunk in range(last):
        fwd_stay(chunk).wait()
        fwd_all(chunk).wait_recv()
        take_units(frecv, chunk, quota)

    for run in range(runs):
        base = run * batch
        for copy in fwd_stay_run(run):
            copy.wait()
        for copy in fwd_run_all(run):
            copy.wait_recv()
        for k in range(batch):
            for src in range(members):
                for chunk in range(chunks):
                    at = (src * chunks + chunk) * tile
                    unit = (units[chunk, src, pl.ds(base + k, 1)] if chunk < last
                            else funit_in[src, run, k])
                    work[k, at:at + tile] = decode(frecv[chunk, src, base + k], unit)
            done = left_turn([work[k, pl.ds(line, grid_len, stride=lines), :] for line in range(lines)],
                             turn_ref)
            done = done * kern[...]
            back = left_turn([done[:, line * width:(line + 1) * width] for line in range(lines)], turn_ref)
            for line in range(lines):
                turned[k, pl.ds(line, grid_len, stride=lines), :] = back[:, line * width:(line + 1) * width]
            for to in range(members):
                for chunk in range(chunks):
                    at = (to * chunks + chunk) * tile
                    code, level = encode(turned[k, at:at + tile])
                    bsend[chunk, to, slot_at(chunk, base + k)] = code
                    levels[chunk, to, pl.ds(base + k, 1)] = level

        if run < runs - 1:
            for chunk in range(last):
                for step in range(1, members):
                    back_copy(chunk, step, run).start()

    for chunk in range(chunks):
        for to in range(members):
            put_levels(bsend, chunk, to, 0 if chunk == last else quota)
        for run in range(0 if chunk == last else runs - 1, runs):
            for step in range(1, members):
                back_copy(chunk, step, run).start()
        back_stay(chunk).start()

    def retreat(chunk):
        def potentials_of(base):
            slots_at = [(which, base + k) for which in range(sets) for k in range(batch)]
            fields = []
            for which, slot in slots_at:
                blocks = [decode(brecv[chunk, taker(which, band), slot_at(chunk, slot)],
                                 units[chunk, taker(which, band), pl.ds(slot, 1)])
                          for band in range(bands)]
                for k in range(planes):
                    fields.append(jnp.concatenate([block[k * lines:(k + 1) * lines] for block in blocks],
                                                  axis=0))
            done = left_turn(fields, turn_ref)
            deep = depth_turn(jnp.concatenate(
                [done[:, k * width:(k + 1) * width] for k in range(len(fields))], axis=0), depth_ref)
            for k, (which, place_in) in enumerate(slots_at):
                slot = which * quota + place_in
                potential = deep[k * rows:(k + 1) * rows]
                left, partner, crossed = pair_of(chunk, slot, slice(None))
                terms[2 * slot] = potential * partner
                second = potential * left
                terms[2 * slot + 1] = jnp.where(crossed, pltpu.roll(second, grid_len, 1), second)

        back_stay(chunk).wait()
        if chunk < last:
            for run in range(runs):
                back_all(chunk, run).wait_recv()
            take_units(brecv, chunk, quota)

            @pl.loop(0, quota, step=batch)
            def _(base):
                potentials_of(base)
        else:
            back_all(chunk, 0).wait_recv()
            take_units(brecv, chunk, 0)
            potentials_of(0)

            for run in range(1, runs):
                back_all(chunk, run).wait_recv()
                potentials_of(run * batch)

    def finish(plane):
        chunk = plane // planes
        span = slice(plane % planes * grid_len, (plane % planes + 1) * grid_len)

        @pl.loop(0, couples)
        def _(couple):
            total = terms[chosen[couple, 0], span]
            for slot in range(1, slots):
                total = total + terms[chosen[couple, slot], span]
            parts[plane, couple] = total
            code, level = encode(total)
            rsend[plane, couple] = code
            runit[plane, couple] = unit_of(level)
            across = pltpu.roll(total, grid_len, 1)
            at = couple % shared * couples
            for other in range(couples):
                basis = held[chunk][other, span].astype(f32)
                for kind, field in enumerate((total, across)):
                    row = pl.ds(at + kind * shared * couples + other, 1)
                    overlap[couple // shared, row] += jnp.sum(basis * field, axis=0, keepdims=True)

    for plane in range(own_planes):
        if plane % planes == 0:
            retreat(plane // planes)
        finish(plane)
        if plane < own_planes - 1:
            for step in range(1, groups):
                for copy in sum_copies(plane, step):
                    copy.start()

    lane = lax.broadcasted_iota(jnp.int32, (8, width), 1)
    halves = ((lane // grid_len) == lax.broadcasted_iota(jnp.int32, (8, width), 0)).astype(jnp.bfloat16)

    def thirds(values):
        high = values.astype(jnp.bfloat16)
        rest = values - high.astype(f32)
        mid = rest.astype(jnp.bfloat16)
        return high, mid, (rest - mid.astype(f32)).astype(jnp.bfloat16)

    for which in range(groups):
        packed[which] = sum(lax.dot_general(halves, third, (((1,), (1,)), ((), ())),
                                            preferred_element_type=f32)
                            for third in thirds(overlap[which]))
    for step in range(1, groups):
        overlap_copy(step).start()
    for step in range(1, groups):
        for copy in sum_copies(own_planes - 1, step):
            copy.start()
    total = packed[group]
    overlap_all().wait_recv()
    for step in range(1, groups):
        total = total + packed_in[step - 1]
    merged[...] = total
    for step in range(1, members):
        merged_copy(step).start()
    merged_all().wait_recv()
    for step in range(1, members):
        total = total + merged_in[step - 1]
    total = total * (1.0 / (grid_len * grid_len * grid_len))
    coef[...] = sum(lax.dot_general(third, halves, (((0,), (0,)), ((), ())), preferred_element_type=f32)
                    for third in thirds(total))

    strip = grid_len // 2
    for plane in range(own_planes):
        chunk, first = plane // planes, plane % planes * grid_len
        for copy in sum_all(plane):
            copy.wait_recv()

        @pl.loop(0, grid_len // strip)
        def _(at):
            here = pl.ds(pl.multiple_of(at * strip, strip), strip)
            there = pl.ds(pl.multiple_of(first + at * strip, strip), strip)
            kept = [jnp.zeros((strip, width), f32) for _ in range(2 * shared)]
            for couple in range(couples):
                basis = held[chunk][couple, there].astype(f32)
                for k in range(2 * shared):
                    row = k * couples + couple
                    kept[k] = kept[k] + coef[row:row + 1] * basis
            for k in range(shared):
                total = parts[plane, group * shared + k, here]
                for step in range(1, groups):
                    total = total + decode(rrecv[plane, step - 1, k, here], rrunit[plane, step - 1, k])
                result[k, here] = total - kept[k] - pltpu.roll(kept[shared + k], grid_len, 1)

        for k in range(shared):
            code, level = encode(result[k])
            ysend[plane, k] = code
            yunit[plane, k] = unit_of(level)
        for hop in range(1, half):
            for copy in result_copies(plane, hop):
                copy.start()
        for copy in result_stay(plane):
            copy.start()

    for plane in range(own_planes):
        for copy in result_stay(plane):
            copy.wait()
        for copy in sum_all(plane):
            copy.wait_send()
    if half > 1:
        for copy in result_all():
            copy.wait()
    for run in range(runs):
        for copy in fwd_run_all(run):
            copy.wait_send()
    for chunk in range(chunks):
        if chunk < last:
            fwd_all(chunk).wait_send()
        for run in range(runs):
            back_all(chunk, run).wait_send()
        gather_all(chunk).wait_send()
    overlap_all().wait_send()
    merged_all().wait_send()
    tab_all().wait_send()


def local(orbitals, pair_table, n_orb, n_slab):
    own_couples, slab_len, grid_len, width = orbitals.shape
    capacity = pair_table.shape[0]
    half = max(1, cube // n_slab)
    members = n_slab * half
    groups = n_orb // half
    bands = grid_len // lines_own
    sets = members // bands
    live_total = sum(capacity * (k + 1) // n_orb for k in range(n_orb))
    quota = -(-live_total // (groups * sets * batch)) * batch
    slots = sets * quota
    couples, shared = n_orb * own_couples, half * own_couples
    planes = grid_len // members
    chunks = planes // 2
    rows, tile = 2 * grid_len, 2 * lines_own
    level_tiles = -(-quota // tile)
    overlap_rows = -(-2 * shared * couples // 128) * 128
    tab_lanes = -(-capacity // 128) * 128

    mat = hartley(grid_len)
    mat_high, mat_low = split_const(mat)
    turn_mat = jnp.asarray(np.concatenate([mat_high, mat_high, mat_low], axis=1))
    deep_high, deep_low = split_const(np.kron(np.eye(2, dtype=np.float32), mat))
    depth_mat = jnp.asarray(np.block([[deep_high, deep_low], [deep_high, np.zeros_like(deep_low)]]))

    dma, vmem, smem = pltpu.SemaphoreType.DMA, pltpu.VMEM, pltpu.SMEM
    i32, i16 = jnp.int32, jnp.int16
    bf16 = orbitals.dtype
    coded = vmem((chunks, members, quota + level_tiles, tile, width), i16)
    runs = quota // batch
    small_units = vmem((members, runs, batch, 1, width), f32)
    per_slot = vmem((chunks, members, level_tiles * tile, width), f32)
    steps = max(groups - 1, 1)
    code, unit = pl.pallas_call(
        functools.partial(action_kernel, n_orb, n_slab, half, quota, chunks, grid_len),
        out_shape=(jax.ShapeDtypeStruct((own_couples, slab_len * grid_len, width), i16),
                   jax.ShapeDtypeStruct((own_couples, slab_len, 1, width), f32)),
        in_specs=[HBM_SPEC] * 4,
        out_specs=(HBM_SPEC, HBM_SPEC),
        scratch_shapes=[vmem((couples, rows, width), orbitals.dtype)] * chunks + [
            vmem((3, capacity), i32), vmem(depth_mat.shape, bf16), vmem(turn_mat.shape, bf16),
            vmem((8, tab_lanes), i32), vmem((n_orb, 8, tab_lanes), i32), smem((n_orb, 8, tab_lanes), i32),
            smem((n_orb,), i32), smem((slots, 5), i32), smem((couples, slots), i32),
            vmem((grid_len, width), f32), vmem((grid_len, lines_own * width), f32),
            per_slot, coded, coded, small_units, small_units, per_slot,
            vmem((batch, lines_own * grid_len, width), f32), vmem((batch, lines_own * grid_len, width), f32),
            coded, coded,
            vmem((2 * slots + 1, rows, width), f32),
            vmem((planes, couples, grid_len, width), f32),
            vmem((planes, couples, grid_len, width), i16), vmem((planes, couples, 1, width), f32),
            vmem((planes, steps, shared, grid_len, width), i16), vmem((planes, steps, shared, 1, width), f32),
            vmem((groups, overlap_rows, width), f32), vmem((groups, 8, overlap_rows), f32),
            vmem((steps, 8, overlap_rows), f32), vmem((8, overlap_rows), f32),
            vmem((members - 1, 8, overlap_rows), f32), vmem((overlap_rows, width), f32),
            vmem((shared, grid_len, width), f32),
            vmem((planes, shared, grid_len, width), i16), vmem((planes, shared, 1, width), f32),
            dma((3,)), dma((2, planes)), dma, dma, dma, dma((chunks,)), dma((chunks,)), dma((chunks,)),
            dma((chunks - 1 + 2 * runs,)), dma((chunks - 1 + runs,)), dma((chunks - 1 + runs,)),
            dma((runs,)), dma((runs,)), dma((chunks,)), dma((runs * chunks,)), dma((runs * chunks,)),
            dma((2, planes)), dma((2, planes)), dma, dma, dma, dma, dma((2,)), dma((2,)),
        ],
        compiler_params=pltpu.CompilerParams(collective_id=0, has_side_effects=True,
                                             vmem_limit_bytes=56 << 20),
    )(pair_table.T, orbitals.reshape(own_couples, slab_len * grid_len, width), depth_mat, turn_mat)
    return code.reshape(orbitals.shape).astype(f32) * unit


def solution(mesh):
    placed = (P("orb", "slab", None, None), P("orb", None))
    return jax.shard_map(
        functools.partial(local, n_orb=mesh.shape["orb"], n_slab=mesh.shape["slab"]),
        mesh=mesh, in_specs=placed, out_specs=P("orb", "slab", None, None), check_vma=False
    )
```

```python
import functools
import math

import jax
import jax.numpy as jnp
import numpy as np
from jax import lax
from jax.experimental import pallas as pl
from jax.experimental.pallas import tpu as pltpu
from jax.sharding import PartitionSpec as P

exchange_fraction = 0.25
cell_ratio = 8.0
lines_own = 8
cube = 16
batch = 3
code_peak = 32700.0
MESH = pl.DeviceIdType.MESH
HBM_SPEC = pl.BlockSpec(memory_space=pltpu.HBM)
f32 = jnp.float32


def hartley(grid_len):
    rows_idx = np.arange(grid_len)
    angles = 2.0 * math.pi / grid_len * (rows_idx[:, None] * rows_idx[None, :] % grid_len)
    return ((np.cos(angles) + np.sin(angles)) / math.sqrt(grid_len)).astype(np.float32)


def split_const(values):
    high = values.astype(jnp.bfloat16)
    return high, (values - high.astype(np.float32)).astype(jnp.bfloat16)


def split(values):
    high = values.astype(jnp.bfloat16)
    low = (values - high.astype(f32)).astype(jnp.bfloat16)
    return high, low


def depth_turn(rows, depth_ref):
    width = rows.shape[1]
    high, low = split(rows)
    both = jnp.dot(jnp.concatenate([high, low], axis=1), depth_ref[...],
                   preferred_element_type=f32)
    return both[:, :width] + both[:, width:]


def left_turn(fields, left_ref):
    high, low = split(jnp.concatenate(fields, axis=1))
    return jnp.dot(left_ref[...], jnp.concatenate([high, low, high], axis=0),
                   preferred_element_type=f32)


def unit_of(level):
    return jnp.exp2(level * (1.0 / 64.0))


def encode(block):
    peak = jnp.max(jnp.abs(block), axis=0, keepdims=True)
    level = jnp.ceil(jnp.log2(jnp.maximum(peak, 1e-30) * (1.0 / code_peak)) * 64.0)
    return whole(block * unit_of(-level)), level


def whole(values):
    return jnp.round(values).astype(jnp.int32).astype(jnp.int16)


def plain(code):
    return code.astype(jnp.int32).astype(f32)


def decode(code, unit):
    return plain(code) * unit


def remote(src, dst, send_sem, recv_sem, device):
    return pltpu.make_async_remote_copy(src_ref=src, dst_ref=dst, send_sem=send_sem, recv_sem=recv_sem,
                                        device_id=device, device_id_type=MESH)


def flipped(index, bits):
    turned, bit = index, 1
    while bit <= bits:
        if bits & bit:
            turned = turned + bit - 2 * bit * (index // bit % 2)
        bit *= 2
    return turned


def spread_order(members, half):
    core = half
    plain = sorted((b for b in range(1, members) if not b & core), key=lambda b: (bin(b).count("1"), b))
    order, left = [], list(plain)
    while left:
        first = left.pop(0)
        order.append(first)
        rest = (max(members - 1 - core, 0)) ^ first
        if rest in left:
            left.remove(rest)
            order.append(rest)
    return order + [b | core for b in order] + [core] if members > core else order


def action_kernel(n_orb, n_slab, half, quota, chunks, grid_len, table_hbm, own_ref, depth_hbm,
                  turn_hbm, out_ref, unit_ref, *scratch):
    held = scratch[:chunks]
    (table_ref, depth_ref, turn_ref, tab_own, tables, tab_s, starts, ids, chosen, gain, kern, levels, fsend, frecv, funit, funit_in, units, work,
     turned, bsend, brecv, terms, parts, rsend, runit, rrecv, rrunit, overlap, packed,
     packed_in, merged, merged_in, coef, result, ysend, yunit,
     load_sem, out_sem, tab_sem, tab_send, tab_recv, own_sem, g_send, g_recv, stay_sem, f_send, f_recv, s_send, s_recv, keep_sem, b_send,
     b_recv, r_send, r_recv, o_send, o_recv, p_send, p_recv, y_send, y_recv) = scratch[chunks:]
    me, me_slab = lax.axis_index("orb"), lax.axis_index("slab")
    group, part = me // half, me % half
    groups, members = n_orb // half, n_slab * half
    place = me_slab * half + part
    own_couples, _, width = own_ref.shape
    couples = n_orb * own_couples
    shared = half * own_couples
    capacity = table_ref.shape[1]
    lines = lines_own
    bands = grid_len // lines
    sets = members // bands
    slots = sets * quota
    runs = quota // batch
    own_planes = grid_len // members
    planes = own_planes // chunks
    rows = planes * grid_len
    tile = planes * lines
    slot_tiles = fsend.shape[2]

    def taker(which, band):
        return (band // half * sets + which) * half + band % half

    my_band = me_slab // sets * half + part

    near = spread_order(members, half)

    def line_to(step):
        return flipped(me, n_orb - step)

    def line_peer(step):
        return {"orb": line_to(step)}

    def member(step):
        to = flipped(place, near[step - 1])
        return to, {"orb": group * half + to % half, "slab": to // half}

    loads = [pltpu.make_async_copy(src, dst, load_sem.at[k]) for k, (src, dst) in enumerate(
        ((table_hbm, table_ref), (depth_hbm, depth_ref), (turn_hbm, turn_ref)))]

    barrier = pltpu.get_barrier_semaphore()
    for step in range(1, n_orb):
        pl.semaphore_signal(barrier, inc=1, device_id=line_peer(step), device_id_type=MESH)
    for slab_step in range(1, n_slab):
        for other in range(half):
            pl.semaphore_signal(
                barrier, inc=1, device_id={"orb": group * half + other,
                                           "slab": lax.rem(me_slab + slab_step, n_slab)},
                device_id_type=MESH)

    def plane_rows(which, chunk):
        return pl.ds(pl.multiple_of((which * chunks + chunk) * rows, rows), rows)

    def tab_copy(step):
        return remote(tab_own, tables.at[me], tab_send, tab_recv, line_peer(step))

    def tab_all():
        every = tables.at[pl.ds(0, n_orb - 1)]
        return remote(every, every, tab_send, tab_recv, line_peer(1))

    def plane_row(which, plane):
        return pl.ds(pl.multiple_of((which * own_planes + plane) * grid_len, grid_len), grid_len)

    def gather_copy(chunk, step):
        to = line_to(step)
        return remote(own_ref.at[:, plane_rows(to % half, chunk)],
                      held[chunk].at[pl.ds(me * own_couples, own_couples)],
                      g_send.at[chunk], g_recv.at[chunk], line_peer(step))

    def gather_all(chunk):
        every = held[chunk].at[pl.ds(0, couples - own_couples)]
        return remote(every, every, g_send.at[chunk], g_recv.at[chunk], line_peer(1))

    def own_copy(chunk):
        return pltpu.make_async_copy(own_ref.at[:, plane_rows(part, chunk)],
                                     held[chunk].at[pl.ds(me * own_couples, own_couples)],
                                     own_sem.at[chunk])

    last = chunks - 1

    def fwd_copy(chunk, step):
        to, device = member(step)
        return remote(fsend.at[chunk, to], frecv.at[chunk, place], f_send.at[chunk], f_recv.at[chunk], device)

    others = pl.ds(0, members - 1)

    def fwd_all(chunk):
        return remote(fsend.at[chunk, others], frecv.at[chunk, others], f_send.at[chunk], f_recv.at[chunk],
                      member(1)[1])

    def fwd_stay(chunk):
        return pltpu.make_async_copy(fsend.at[chunk, place], frecv.at[chunk, place], stay_sem.at[chunk])

    def fwd_run(step, run):
        to, device = member(step)
        some = pl.ds(run * batch, batch)
        at = last + run
        return (remote(fsend.at[last, to, some], frecv.at[last, place, some], f_send.at[at], f_recv.at[at],
                       device),
                remote(funit.at[to, run], funit_in.at[place, run], s_send.at[run], s_recv.at[run], device))

    def fwd_run_all(run):
        some = pl.ds(run * batch, batch)
        at = last + run
        return (remote(fsend.at[last, others, some], frecv.at[last, others, some], f_send.at[at],
                       f_recv.at[at], member(1)[1]),
                remote(funit.at[others, run], funit_in.at[others, run], s_send.at[run], s_recv.at[run],
                       member(1)[1]))

    def fwd_stay_run(run):
        some = pl.ds(run * batch, batch)
        return (pltpu.make_async_copy(fsend.at[last, place, some], frecv.at[last, place, some],
                                      stay_sem.at[last + run]),
                pltpu.make_async_copy(funit.at[place, run], funit_in.at[place, run],
                                      stay_sem.at[last + runs + run]))

    def slot_at(chunk, slot):
        return slot + (slot_tiles - quota if chunk == last else 0)

    def back_run(chunk, run):
        some, at = pl.ds(slot_at(chunk, run * batch), batch), chunk * runs + run
        if isinstance(run, int):
            if chunk == last and run == 0:
                some = pl.ds(0, slot_tiles - quota + batch)
            elif chunk < last and run == runs - 1:
                some = pl.ds(run * batch, slot_tiles - run * batch)
        return some, at

    def back_copy(chunk, step, run):
        to, device = member(step)
        some, at = back_run(chunk, run)
        return remote(bsend.at[chunk, to, some], brecv.at[chunk, place, some], b_send.at[at], b_recv.at[at],
                      device)

    def back_all(chunk, run):
        some, at = back_run(chunk, run)
        return remote(bsend.at[chunk, others, some], brecv.at[chunk, others, some], b_send.at[at],
                      b_recv.at[at], member(1)[1])

    def back_stay(chunk):
        return pltpu.make_async_copy(bsend.at[chunk, place], brecv.at[chunk, place], keep_sem.at[chunk])

    def sum_copies(plane, step):
        to = lax.rem(group + step, groups)
        theirs = pl.ds(to * shared, shared)
        device = {"orb": to * half + part}
        return (remote(rsend.at[plane, theirs], rrecv.at[plane, step - 1], r_send.at[0, plane],
                       r_recv.at[0, plane], device),
                remote(runit.at[plane, theirs], rrunit.at[plane, step - 1], r_send.at[1, plane],
                       r_recv.at[1, plane], device))

    def sum_all(plane):
        device = {"orb": lax.rem(group + 1, groups) * half + part}
        return [remote(ref.at[plane], ref.at[plane], r_send.at[k, plane], r_recv.at[k, plane], device)
                for k, ref in enumerate((rrecv, rrunit))]

    def overlap_copy(step):
        to = lax.rem(group + step, groups)
        return remote(packed.at[to], packed_in.at[step - 1], o_send, o_recv,
                      {"orb": to * half + part})

    def overlap_all():
        return remote(packed_in, packed_in, o_send, o_recv, {"orb": lax.rem(group + 1, groups) * half + part})

    def merged_copy(step):
        return remote(merged, merged_in.at[step - 1], p_send, p_recv, member(step)[1])

    def merged_all():
        return remote(merged_in, merged_in, p_send, p_recv, member(1)[1])

    def result_stay(plane):
        mine = pl.ds(part * own_couples, own_couples)
        return (pltpu.make_async_copy(ysend.at[plane, mine], out_ref.at[:, plane_row(part, plane)],
                                      out_sem.at[0, plane]),
                pltpu.make_async_copy(yunit.at[plane, mine], unit_ref.at[:, part * own_planes + plane],
                                      out_sem.at[1, plane]))

    def result_copies(plane, hop):
        to = flipped(part, hop)
        theirs, device = pl.ds(to * own_couples, own_couples), {"orb": group * half + to}
        return (remote(ysend.at[plane, theirs], out_ref.at[:, plane_row(part, plane)],
                       y_send.at[0], y_recv.at[0], device),
                remote(yunit.at[plane, theirs], unit_ref.at[:, part * own_planes + plane],
                       y_send.at[1], y_recv.at[1], device))

    def result_all():
        theirs = pl.ds(0, shared - own_couples)
        device = {"orb": group * half + flipped(part, 1)}
        return [remote(ref.at[:, theirs], ref.at[:, theirs], y_send.at[k], y_recv.at[k], device)
                for k, ref in enumerate((ysend, yunit))]

    for load in loads:
        load.start()
    tab_own[...] = jnp.full(tab_own.shape, -1, jnp.int32)
    loads[0].wait()
    tab_own[0:3, 0:capacity] = table_ref[...]
    kz = lax.broadcasted_iota(jnp.int32, (grid_len, width), 1) % grid_len
    fz = jnp.minimum(kz, grid_len - kz).astype(f32)
    ky = lax.broadcasted_iota(jnp.int32, (grid_len, width), 0)
    fy = jnp.minimum(ky, grid_len - ky).astype(f32)
    plane_sq = fy * fy + fz * fz
    deep = cell_ratio * cell_ratio
    gain[...] = 1.0 / jnp.where(plane_sq > 0, plane_sq, deep)
    fx = cell_ratio * fy
    scale_k = (2.0 * math.pi / grid_len) * (2.0 * math.pi / grid_len)
    for line in range(lines):
        at = my_band * lines + line
        fl = jnp.minimum(at, grid_len - at).astype(f32)
        plane = fl * fl + fz * fz
        full = fx * fx + plane
        level = jnp.where(plane > 0, plane, deep)
        kern[:, line * width:(line + 1) * width] = jnp.where(
            full > 0, (-exchange_fraction / scale_k) * level / jnp.where(full > 0, full, 1.0), 0.0)
    terms[2 * slots] = jnp.zeros(terms.shape[1:], f32)
    overlap[...] = jnp.zeros(overlap.shape, f32)
    levels[...] = jnp.zeros(levels.shape, f32)

    pl.semaphore_wait(barrier, n_orb - 1 + (n_slab - 1) * half)
    for step in range(1, n_orb):
        tab_copy(step).start()
    for chunk in range(chunks):
        for step in range(1, n_orb):
            gather_copy(chunk, step).start()
        own_copy(chunk).start()
    tables[me] = tab_own[...]

    tab_all().wait_recv()
    to_scalars = pltpu.make_async_copy(tables, tab_s, tab_sem)
    to_scalars.start()
    to_scalars.wait()

    def count_block(block, total):
        starts[block] = total
        return lax.fori_loop(
            0, capacity, lambda k, sum_in: sum_in + (tab_s[block, 0, k] >= 0).astype(jnp.int32), total)

    live = lax.fori_loop(0, n_orb, count_block, jnp.int32(0))

    @pl.loop(0, slots)
    def _(slot):
        wanted = slot * groups + group
        used = wanted < live
        block = lax.fori_loop(
            1, n_orb, lambda b, sum_in: sum_in + (starts[b] <= wanted).astype(jnp.int32), jnp.int32(0))
        column = jnp.clip(wanted - starts[block], 0, capacity - 1)
        for k in range(3):
            ids[slot, k] = jnp.maximum(tab_s[block, k, column], 0)
        for k in range(2):
            ids[slot, 3 + k] = jnp.where(used, tab_s[block, k, column], -1)

    def pair_of(chunk, slot, span):
        left = held[chunk][ids[slot, 0], span].astype(f32)
        right = held[chunk][ids[slot, 1], span].astype(f32)
        crossed = ids[slot, 2] == 1
        return left, jnp.where(crossed, pltpu.roll(right, grid_len, 1), right), crossed

    def put_levels(ref, chunk, to, first):
        for k in range(slot_tiles - quota):
            ref[chunk, to, first + k] = whole(levels[chunk, to, k * tile:(k + 1) * tile])

    def take_units(ref, chunk, first):
        for src in range(members):
            for k in range(slot_tiles - quota):
                units[chunk, src, k * tile:(k + 1) * tile] = unit_of(plain(ref[chunk, src, first + k]))

    def advance(chunk):
        own_copy(chunk).wait()
        gather_all(chunk).wait_recv()

        def densities(which, base, keep):
            pairs = [pair_of(chunk, which * quota + base + k, slice(None)) for k in range(batch)]
            flat = depth_turn(jnp.concatenate([left * partner for left, partner, _ in pairs], axis=0),
                              depth_ref)
            done = left_turn([flat[k * grid_len:(k + 1) * grid_len] for k in range(2 * batch)], turn_ref)
            for k in range(batch):
                one = done[:, 2 * k * width:(2 * k + 1) * width] * gain[...]
                two = done[:, (2 * k + 1) * width:(2 * k + 2) * width] * gain[...]
                for band in range(bands):
                    to = taker(which, band)
                    span = slice(band * lines, (band + 1) * lines)
                    code, level = encode(jnp.concatenate([one[span], two[span]], axis=0))
                    fsend[chunk, to, base + k] = code
                    keep(to, base, k, level)

        def keep_level(to, base, k, level):
            levels[chunk, to, pl.ds(base + k, 1)] = level

        def keep_unit(to, base, k, level):
            funit[to, base // batch, k] = unit_of(level)

        if chunk < last:
            for which in range(sets):
                @pl.loop(0, quota, step=batch)
                def _(base):
                    densities(which, base, keep_level)

                for band in range(bands):
                    put_levels(fsend, chunk, taker(which, band), quota)
                for step in range(1, members):
                    to = member(step)[0]

                    @pl.when(to // half % sets == which)
                    def _():
                        fwd_copy(chunk, step).start()

            fwd_stay(chunk).start()
        else:
            for run in range(runs):
                for which in range(sets):
                    densities(which, run * batch, keep_unit)
                for step in range(1, members):
                    for copy in fwd_run(step, run):
                        copy.start()
                for copy in fwd_stay_run(run):
                    copy.start()

    for load in loads[1:]:
        load.wait()
    for chunk in range(chunks):
        advance(chunk)

    @pl.loop(0, slots)
    def _(slot):
        @pl.loop(0, couples)
        def _(couple):
            chosen[couple, slot] = jnp.where(
                ids[slot, 3] == couple, 2 * slot, jnp.where(ids[slot, 4] == couple, 2 * slot + 1, 2 * slots))

    for chunk in range(last):
        fwd_stay(chunk).wait()
        fwd_all(chunk).wait_recv()
        take_units(frecv, chunk, quota)

    for run in range(runs):
        base = run * batch
        for copy in fwd_stay_run(run):
            copy.wait()
        for copy in fwd_run_all(run):
            copy.wait_recv()
        for k in range(batch):
            for src in range(members):
                for chunk in range(chunks):
                    at = (src * chunks + chunk) * tile
                    unit = (units[chunk, src, pl.ds(base + k, 1)] if chunk < last
                            else funit_in[src, run, k])
                    work[k, at:at + tile] = decode(frecv[chunk, src, base + k], unit)
            done = left_turn([work[k, pl.ds(line, grid_len, stride=lines), :] for line in range(lines)],
                             turn_ref)
            done = done * kern[...]
            back = left_turn([done[:, line * width:(line + 1) * width] for line in range(lines)], turn_ref)
            for line in range(lines):
                turned[k, pl.ds(line, grid_len, stride=lines), :] = back[:, line * width:(line + 1) * width]
            for to in range(members):
                for chunk in range(chunks):
                    at = (to * chunks + chunk) * tile
                    code, level = encode(turned[k, at:at + tile])
                    bsend[chunk, to, slot_at(chunk, base + k)] = code
                    levels[chunk, to, pl.ds(base + k, 1)] = level

        if run < runs - 1:
            for chunk in range(last):
                for step in range(1, members):
                    back_copy(chunk, step, run).start()

    for chunk in range(chunks):
        for to in range(members):
            put_levels(bsend, chunk, to, 0 if chunk == last else quota)
        for run in range(0 if chunk == last else runs - 1, runs):
            for step in range(1, members):
                back_copy(chunk, step, run).start()
        back_stay(chunk).start()

    def retreat(chunk):
        def potentials_of(base):
            slots_at = [(which, base + k) for which in range(sets) for k in range(batch)]
            fields = []
            for which, slot in slots_at:
                blocks = [decode(brecv[chunk, taker(which, band), slot_at(chunk, slot)],
                                 units[chunk, taker(which, band), pl.ds(slot, 1)])
                          for band in range(bands)]
                for k in range(planes):
                    fields.append(jnp.concatenate([block[k * lines:(k + 1) * lines] for block in blocks],
                                                  axis=0))
            done = left_turn(fields, turn_ref)
            deep = depth_turn(jnp.concatenate(
                [done[:, k * width:(k + 1) * width] for k in range(len(fields))], axis=0), depth_ref)
            for k, (which, place_in) in enumerate(slots_at):
                slot = which * quota + place_in
                potential = deep[k * rows:(k + 1) * rows]
                left, partner, crossed = pair_of(chunk, slot, slice(None))
                terms[2 * slot] = potential * partner
                second = potential * left
                terms[2 * slot + 1] = jnp.where(crossed, pltpu.roll(second, grid_len, 1), second)

        back_stay(chunk).wait()
        if chunk < last:
            for run in range(runs):
                back_all(chunk, run).wait_recv()
            take_units(brecv, chunk, quota)

            @pl.loop(0, quota, step=batch)
            def _(base):
                potentials_of(base)
        else:
            back_all(chunk, 0).wait_recv()
            take_units(brecv, chunk, 0)
            potentials_of(0)

            for run in range(1, runs):
                back_all(chunk, run).wait_recv()
                potentials_of(run * batch)

    def finish(plane):
        chunk = plane // planes
        span = slice(plane % planes * grid_len, (plane % planes + 1) * grid_len)

        @pl.loop(0, couples)
        def _(couple):
            total = terms[chosen[couple, 0], span]
            for slot in range(1, slots):
                total = total + terms[chosen[couple, slot], span]
            parts[plane, couple] = total
            code, level = encode(total)
            rsend[plane, couple] = code
            runit[plane, couple] = unit_of(level)

    def send_sums(plane):
        for step in range(1, groups):
            for copy in sum_copies(plane, step):
                copy.start()

    def project(plane):
        chunk = plane // planes
        span = slice(plane % planes * grid_len, (plane % planes + 1) * grid_len)

        @pl.loop(0, couples)
        def _(couple):
            total = parts[plane, couple]
            across = pltpu.roll(total, grid_len, 1)
            at = couple % shared * couples
            for other in range(couples):
                basis = held[chunk][other, span].astype(f32)
                for kind, field in enumerate((total, across)):
                    row = pl.ds(at + kind * shared * couples + other, 1)
                    overlap[couple // shared, row] += jnp.sum(basis * field, axis=0, keepdims=True)

    for plane in range(own_planes):
        if plane % planes == 0:
            retreat(plane // planes)
        finish(plane)
        if plane < own_planes - 1:
            send_sums(plane)
        if plane < own_planes - planes:
            project(plane)
    for plane in range(own_planes - planes, own_planes):
        project(plane)

    lane = lax.broadcasted_iota(jnp.int32, (8, width), 1)
    halves = ((lane // grid_len) == lax.broadcasted_iota(jnp.int32, (8, width), 0)).astype(jnp.bfloat16)

    def thirds(values):
        high = values.astype(jnp.bfloat16)
        rest = values - high.astype(f32)
        mid = rest.astype(jnp.bfloat16)
        return high, mid, (rest - mid.astype(f32)).astype(jnp.bfloat16)

    for which in range(groups):
        packed[which] = sum(lax.dot_general(halves, third, (((1,), (1,)), ((), ())),
                                            preferred_element_type=f32)
                            for third in thirds(overlap[which]))
    for step in range(1, groups):
        overlap_copy(step).start()
    total = packed[group]
    overlap_all().wait_recv()
    for step in range(1, groups):
        total = total + packed_in[step - 1]
    merged[...] = total
    for step in range(1, members):
        merged_copy(step).start()
    for step in range(1, groups):
        for copy in sum_copies(own_planes - 1, step):
            copy.start()
    merged_all().wait_recv()
    for step in range(1, members):
        total = total + merged_in[step - 1]
    total = total * (1.0 / (grid_len * grid_len * grid_len))
    coef[...] = sum(lax.dot_general(third, halves, (((0,), (0,)), ((), ())), preferred_element_type=f32)
                    for third in thirds(total))

    strip = grid_len // 2
    for plane in range(own_planes):
        chunk, first = plane // planes, plane % planes * grid_len
        for copy in sum_all(plane):
            copy.wait_recv()

        @pl.loop(0, grid_len // strip)
        def _(at):
            here = pl.ds(pl.multiple_of(at * strip, strip), strip)
            there = pl.ds(pl.multiple_of(first + at * strip, strip), strip)
            kept = [jnp.zeros((strip, width), f32) for _ in range(2 * shared)]
            for couple in range(couples):
                basis = held[chunk][couple, there].astype(f32)
                for k in range(2 * shared):
                    row = k * couples + couple
                    kept[k] = kept[k] + coef[row:row + 1] * basis
            for k in range(shared):
                total = parts[plane, group * shared + k, here]
                for step in range(1, groups):
                    total = total + decode(rrecv[plane, step - 1, k, here], rrunit[plane, step - 1, k])
                result[k, here] = total - kept[k] - pltpu.roll(kept[shared + k], grid_len, 1)

        for k in range(shared):
            code, level = encode(result[k])
            ysend[plane, k] = code
            yunit[plane, k] = unit_of(level)
        for hop in range(1, half):
            for copy in result_copies(plane, hop):
                copy.start()
        for copy in result_stay(plane):
            copy.start()

    for plane in range(own_planes):
        for copy in result_stay(plane):
            copy.wait()
        for copy in sum_all(plane):
            copy.wait_send()
    if half > 1:
        for copy in result_all():
            copy.wait()
    for run in range(runs):
        for copy in fwd_run_all(run):
            copy.wait_send()
    for chunk in range(chunks):
        if chunk < last:
            fwd_all(chunk).wait_send()
        for run in range(runs):
            back_all(chunk, run).wait_send()
        gather_all(chunk).wait_send()
    overlap_all().wait_send()
    merged_all().wait_send()
    tab_all().wait_send()


def local(orbitals, pair_table, n_orb, n_slab):
    own_couples, slab_len, grid_len, width = orbitals.shape
    capacity = pair_table.shape[0]
    half = max(1, cube // n_slab)
    members = n_slab * half
    groups = n_orb // half
    bands = grid_len // lines_own
    sets = members // bands
    live_total = sum(capacity * (k + 1) // n_orb for k in range(n_orb))
    quota = -(-live_total // (groups * sets * batch)) * batch
    slots = sets * quota
    couples, shared = n_orb * own_couples, half * own_couples
    planes = grid_len // members
    chunks = planes // 2
    rows, tile = 2 * grid_len, 2 * lines_own
    level_tiles = -(-quota // tile)
    overlap_rows = -(-2 * shared * couples // 128) * 128
    tab_lanes = -(-capacity // 128) * 128

    mat = hartley(grid_len)
    mat_high, mat_low = split_const(mat)
    turn_mat = jnp.asarray(np.concatenate([mat_high, mat_high, mat_low], axis=1))
    deep_high, deep_low = split_const(np.kron(np.eye(2, dtype=np.float32), mat))
    depth_mat = jnp.asarray(np.block([[deep_high, deep_low], [deep_high, np.zeros_like(deep_low)]]))

    dma, vmem, smem = pltpu.SemaphoreType.DMA, pltpu.VMEM, pltpu.SMEM
    i32, i16 = jnp.int32, jnp.int16
    bf16 = orbitals.dtype
    coded = vmem((chunks, members, quota + level_tiles, tile, width), i16)
    runs = quota // batch
    small_units = vmem((members, runs, batch, 1, width), f32)
    per_slot = vmem((chunks, members, level_tiles * tile, width), f32)
    steps = max(groups - 1, 1)
    code, unit = pl.pallas_call(
        functools.partial(action_kernel, n_orb, n_slab, half, quota, chunks, grid_len),
        out_shape=(jax.ShapeDtypeStruct((own_couples, slab_len * grid_len, width), i16),
                   jax.ShapeDtypeStruct((own_couples, slab_len, 1, width), f32)),
        in_specs=[HBM_SPEC] * 4,
        out_specs=(HBM_SPEC, HBM_SPEC),
        scratch_shapes=[vmem((couples, rows, width), orbitals.dtype)] * chunks + [
            vmem((3, capacity), i32), vmem(depth_mat.shape, bf16), vmem(turn_mat.shape, bf16),
            vmem((8, tab_lanes), i32), vmem((n_orb, 8, tab_lanes), i32), smem((n_orb, 8, tab_lanes), i32),
            smem((n_orb,), i32), smem((slots, 5), i32), smem((couples, slots), i32),
            vmem((grid_len, width), f32), vmem((grid_len, lines_own * width), f32),
            per_slot, coded, coded, small_units, small_units, per_slot,
            vmem((batch, lines_own * grid_len, width), f32), vmem((batch, lines_own * grid_len, width), f32),
            coded, coded,
            vmem((2 * slots + 1, rows, width), f32),
            vmem((planes, couples, grid_len, width), f32),
            vmem((planes, couples, grid_len, width), i16), vmem((planes, couples, 1, width), f32),
            vmem((planes, steps, shared, grid_len, width), i16), vmem((planes, steps, shared, 1, width), f32),
            vmem((groups, overlap_rows, width), f32), vmem((groups, 8, overlap_rows), f32),
            vmem((steps, 8, overlap_rows), f32), vmem((8, overlap_rows), f32),
            vmem((members - 1, 8, overlap_rows), f32), vmem((overlap_rows, width), f32),
            vmem((shared, grid_len, width), f32),
            vmem((planes, shared, grid_len, width), i16), vmem((planes, shared, 1, width), f32),
            dma((3,)), dma((2, planes)), dma, dma, dma, dma((chunks,)), dma((chunks,)), dma((chunks,)),
            dma((chunks - 1 + 2 * runs,)), dma((chunks - 1 + runs,)), dma((chunks - 1 + runs,)),
            dma((runs,)), dma((runs,)), dma((chunks,)), dma((runs * chunks,)), dma((runs * chunks,)),
            dma((2, planes)), dma((2, planes)), dma, dma, dma, dma, dma((2,)), dma((2,)),
        ],
        compiler_params=pltpu.CompilerParams(collective_id=0, has_side_effects=True,
                                             vmem_limit_bytes=56 << 20),
    )(pair_table.T, orbitals.reshape(own_couples, slab_len * grid_len, width), depth_mat, turn_mat)
    return code.reshape(orbitals.shape).astype(f32) * unit


def solution(mesh):
    placed = (P("orb", "slab", None, None), P("orb", None))
    return jax.shard_map(
        functools.partial(local, n_orb=mesh.shape["orb"], n_slab=mesh.shape["slab"]),
        mesh=mesh, in_specs=placed, out_specs=P("orb", "slab", None, None), check_vma=False
    )
```

```python
import functools
import math

import jax
import jax.numpy as jnp
import numpy as np
from jax import lax
from jax.experimental import pallas as pl
from jax.experimental.pallas import tpu as pltpu
from jax.sharding import PartitionSpec as P

exchange_fraction = 0.25
cell_ratio = 8.0
lines_own = 8
cube = 16
batch = 3
code_peak = 32700.0
MESH = pl.DeviceIdType.MESH
HBM_SPEC = pl.BlockSpec(memory_space=pltpu.HBM)
f32 = jnp.float32


def hartley(grid_len):
    rows_idx = np.arange(grid_len)
    angles = 2.0 * math.pi / grid_len * (rows_idx[:, None] * rows_idx[None, :] % grid_len)
    return ((np.cos(angles) + np.sin(angles)) / math.sqrt(grid_len)).astype(np.float32)


def split_const(values):
    high = values.astype(jnp.bfloat16)
    return high, (values - high.astype(np.float32)).astype(jnp.bfloat16)


def split(values):
    high = values.astype(jnp.bfloat16)
    low = (values - high.astype(f32)).astype(jnp.bfloat16)
    return high, low


def depth_turn(rows, depth_ref):
    width = rows.shape[1]
    high, low = split(rows)
    both = jnp.dot(jnp.concatenate([high, low], axis=1), depth_ref[...],
                   preferred_element_type=f32)
    return both[:, :width] + both[:, width:]


def left_turn(fields, left_ref):
    high, low = split(jnp.concatenate(fields, axis=1))
    return jnp.dot(left_ref[...], jnp.concatenate([high, low, high], axis=0),
                   preferred_element_type=f32)


def unit_of(level):
    return jnp.exp2(level * (1.0 / 64.0))


def encode(block):
    peak = jnp.max(jnp.abs(block), axis=0, keepdims=True)
    level = jnp.ceil(jnp.log2(jnp.maximum(peak, 1e-33) * (1.0 / code_peak)) * 64.0)
    return whole(block * unit_of(-level)), level


def whole(values):
    return jnp.round(values).astype(jnp.int32).astype(jnp.int16)


def plain(code):
    return code.astype(jnp.int32).astype(f32)


def decode(code, unit):
    return plain(code) * unit


def remote(src, dst, send_sem, recv_sem, device):
    return pltpu.make_async_remote_copy(src_ref=src, dst_ref=dst, send_sem=send_sem, recv_sem=recv_sem,
                                        device_id=device, device_id_type=MESH)


def flipped(index, bits):
    turned, bit = index, 1
    while bit <= bits:
        if bits & bit:
            turned = turned + bit - 2 * bit * (index // bit % 2)
        bit *= 2
    return turned


def spread_order(members, half):
    core = half
    plain = sorted((b for b in range(1, members) if not b & core), key=lambda b: (bin(b).count("1"), b))
    order, left = [], list(plain)
    while left:
        first = left.pop(0)
        order.append(first)
        rest = (max(members - 1 - core, 0)) ^ first
        if rest in left:
            left.remove(rest)
            order.append(rest)
    return order + [b | core for b in order] + [core] if members > core else order


def action_kernel(n_orb, n_slab, half, quota, chunks, grid_len, table_hbm, own_ref, depth_hbm,
                  turn_hbm, out_ref, unit_ref, *scratch):
    held = scratch[:chunks]
    (table_ref, depth_ref, turn_ref, tab_own, tables, tab_s, starts, ids, chosen, gain, kern, levels, fsend, frecv, funit, funit_in, units, work,
     turned, bsend, brecv, terms, parts, rsend, runit, rrecv, rrunit, overlap, packed,
     packed_in, merged, merged_in, coef, result, ysend, yunit,
     load_sem, out_sem, tab_sem, tab_send, tab_recv, own_sem, g_send, g_recv, stay_sem, f_send, f_recv, s_send, s_recv, keep_sem, b_send,
     b_recv, r_send, r_recv, o_send, o_recv, p_send, p_recv, y_send, y_recv) = scratch[chunks:]
    me, me_slab = lax.axis_index("orb"), lax.axis_index("slab")
    group, part = me // half, me % half
    groups, members = n_orb // half, n_slab * half
    place = me_slab * half + part
    own_couples, _, width = own_ref.shape
    couples = n_orb * own_couples
    shared = half * own_couples
    capacity = table_ref.shape[1]
    lines = lines_own
    bands = grid_len // lines
    sets = members // bands
    slots = sets * quota
    runs = quota // batch
    own_planes = grid_len // members
    planes = own_planes // chunks
    rows = planes * grid_len
    tile = planes * lines
    slot_tiles = fsend.shape[2]

    def taker(which, band):
        return (band // half * sets + which) * half + band % half

    my_band = me_slab // sets * half + part

    near = spread_order(members, half)

    def line_to(step):
        return flipped(me, n_orb - step)

    def line_peer(step):
        return {"orb": line_to(step)}

    def member(step):
        to = flipped(place, near[step - 1])
        return to, {"orb": group * half + to % half, "slab": to // half}

    loads = [pltpu.make_async_copy(src, dst, load_sem.at[k]) for k, (src, dst) in enumerate(
        ((table_hbm, table_ref), (depth_hbm, depth_ref), (turn_hbm, turn_ref)))]

    barrier = pltpu.get_barrier_semaphore()
    for step in range(1, n_orb):
        pl.semaphore_signal(barrier, inc=1, device_id=line_peer(step), device_id_type=MESH)
    for slab_step in range(1, n_slab):
        for other in range(half):
            pl.semaphore_signal(
                barrier, inc=1, device_id={"orb": group * half + other,
                                           "slab": lax.rem(me_slab + slab_step, n_slab)},
                device_id_type=MESH)

    def plane_rows(which, chunk):
        return pl.ds(pl.multiple_of((which * chunks + chunk) * rows, rows), rows)

    def tab_copy(step):
        return remote(tab_own, tables.at[me], tab_send, tab_recv, line_peer(step))

    def tab_all():
        every = tables.at[pl.ds(0, n_orb - 1)]
        return remote(every, every, tab_send, tab_recv, line_peer(1))

    def plane_row(which, plane):
        return pl.ds(pl.multiple_of((which * own_planes + plane) * grid_len, grid_len), grid_len)

    def gather_copy(chunk, step):
        to = line_to(step)
        return remote(own_ref.at[:, plane_rows(to % half, chunk)],
                      held[chunk].at[pl.ds(me * own_couples, own_couples)],
                      g_send.at[chunk], g_recv.at[chunk], line_peer(step))

    def gather_all(chunk):
        every = held[chunk].at[pl.ds(0, couples - own_couples)]
        return remote(every, every, g_send.at[chunk], g_recv.at[chunk], line_peer(1))

    def own_copy(chunk):
        return pltpu.make_async_copy(own_ref.at[:, plane_rows(part, chunk)],
                                     held[chunk].at[pl.ds(me * own_couples, own_couples)],
                                     own_sem.at[chunk])

    last = chunks - 1

    def fwd_copy(chunk, step):
        to, device = member(step)
        return remote(fsend.at[chunk, to], frecv.at[chunk, place], f_send.at[chunk], f_recv.at[chunk], device)

    others = pl.ds(0, members - 1)

    def fwd_all(chunk):
        return remote(fsend.at[chunk, others], frecv.at[chunk, others], f_send.at[chunk], f_recv.at[chunk],
                      member(1)[1])

    def fwd_stay(chunk):
        return pltpu.make_async_copy(fsend.at[chunk, place], frecv.at[chunk, place], stay_sem.at[chunk])

    def fwd_run(step, run):
        to, device = member(step)
        some = pl.ds(run * batch, batch)
        at = last + run
        return (remote(fsend.at[last, to, some], frecv.at[last, place, some], f_send.at[at], f_recv.at[at],
                       device),
                remote(funit.at[to, run], funit_in.at[place, run], s_send.at[run], s_recv.at[run], device))

    def fwd_run_all(run):
        some = pl.ds(run * batch, batch)
        at = last + run
        return (remote(fsend.at[last, others, some], frecv.at[last, others, some], f_send.at[at],
                       f_recv.at[at], member(1)[1]),
                remote(funit.at[others, run], funit_in.at[others, run], s_send.at[run], s_recv.at[run],
                       member(1)[1]))

    def fwd_stay_run(run):
        some = pl.ds(run * batch, batch)
        return (pltpu.make_async_copy(fsend.at[last, place, some], frecv.at[last, place, some],
                                      stay_sem.at[last + run]),
                pltpu.make_async_copy(funit.at[place, run], funit_in.at[place, run],
                                      stay_sem.at[last + runs + run]))

    def slot_at(chunk, slot):
        return slot + (slot_tiles - quota if chunk == last else 0)

    def back_run(chunk, run):
        some, at = pl.ds(slot_at(chunk, run * batch), batch), chunk * runs + run
        if isinstance(run, int):
            if chunk == last and run == 0:
                some = pl.ds(0, slot_tiles - quota + batch)
            elif chunk < last and run == runs - 1:
                some = pl.ds(run * batch, slot_tiles - run * batch)
        return some, at

    def back_copy(chunk, step, run):
        to, device = member(step)
        some, at = back_run(chunk, run)
        return remote(bsend.at[chunk, to, some], brecv.at[chunk, place, some], b_send.at[at], b_recv.at[at],
                      device)

    def back_all(chunk, run):
        some, at = back_run(chunk, run)
        return remote(bsend.at[chunk, others, some], brecv.at[chunk, others, some], b_send.at[at],
                      b_recv.at[at], member(1)[1])

    def back_stay(chunk):
        return pltpu.make_async_copy(bsend.at[chunk, place], brecv.at[chunk, place], keep_sem.at[chunk])

    def sum_copies(plane, step):
        to = lax.rem(group + step, groups)
        theirs = pl.ds(to * shared, shared)
        device = {"orb": to * half + part}
        return (remote(rsend.at[plane, theirs], rrecv.at[plane, step - 1], r_send.at[0, plane],
                       r_recv.at[0, plane], device),
                remote(runit.at[plane, theirs], rrunit.at[plane, step - 1], r_send.at[1, plane],
                       r_recv.at[1, plane], device))

    def sum_all(plane):
        device = {"orb": lax.rem(group + 1, groups) * half + part}
        return [remote(ref.at[plane], ref.at[plane], r_send.at[k, plane], r_recv.at[k, plane], device)
                for k, ref in enumerate((rrecv, rrunit))]

    def overlap_copy(step):
        to = lax.rem(group + step, groups)
        return remote(packed.at[to], packed_in.at[step - 1], o_send, o_recv,
                      {"orb": to * half + part})

    def overlap_all():
        return remote(packed_in, packed_in, o_send, o_recv, {"orb": lax.rem(group + 1, groups) * half + part})

    def merged_copy(step):
        return remote(merged, merged_in.at[step - 1], p_send, p_recv, member(step)[1])

    def merged_all():
        return remote(merged_in, merged_in, p_send, p_recv, member(1)[1])

    def result_stay(plane):
        mine = pl.ds(part * own_couples, own_couples)
        return (pltpu.make_async_copy(ysend.at[plane, mine], out_ref.at[:, plane_row(part, plane)],
                                      out_sem.at[0, plane]),
                pltpu.make_async_copy(yunit.at[plane, mine], unit_ref.at[:, part * own_planes + plane],
                                      out_sem.at[1, plane]))

    def result_copies(plane, hop):
        to = flipped(part, hop)
        theirs, device = pl.ds(to * own_couples, own_couples), {"orb": group * half + to}
        return (remote(ysend.at[plane, theirs], out_ref.at[:, plane_row(part, plane)],
                       y_send.at[0], y_recv.at[0], device),
                remote(yunit.at[plane, theirs], unit_ref.at[:, part * own_planes + plane],
                       y_send.at[1], y_recv.at[1], device))

    def result_all():
        theirs = pl.ds(0, shared - own_couples)
        device = {"orb": group * half + flipped(part, 1)}
        return [remote(ref.at[:, theirs], ref.at[:, theirs], y_send.at[k], y_recv.at[k], device)
                for k, ref in enumerate((ysend, yunit))]

    for load in loads:
        load.start()
    tab_own[...] = jnp.full(tab_own.shape, -1, jnp.int32)
    loads[0].wait()
    tab_own[0:3, 0:capacity] = table_ref[...]
    kz = lax.broadcasted_iota(jnp.int32, (grid_len, width), 1) % grid_len
    fz = jnp.minimum(kz, grid_len - kz).astype(f32)
    ky = lax.broadcasted_iota(jnp.int32, (grid_len, width), 0)
    fy = jnp.minimum(ky, grid_len - ky).astype(f32)
    plane_sq = fy * fy + fz * fz
    deep = cell_ratio * cell_ratio
    gain[...] = 1.0 / jnp.where(plane_sq > 0, plane_sq, deep)
    fx = cell_ratio * fy
    scale_k = (2.0 * math.pi / grid_len) * (2.0 * math.pi / grid_len)
    for line in range(lines):
        at = my_band * lines + line
        fl = jnp.minimum(at, grid_len - at).astype(f32)
        plane = fl * fl + fz * fz
        full = fx * fx + plane
        level = jnp.where(plane > 0, plane, deep)
        kern[:, line * width:(line + 1) * width] = jnp.where(
            full > 0, (-exchange_fraction / scale_k) * level / jnp.where(full > 0, full, 1.0), 0.0)
    terms[2 * slots] = jnp.zeros(terms.shape[1:], f32)
    overlap[...] = jnp.zeros(overlap.shape, f32)
    levels[...] = jnp.zeros(levels.shape, f32)

    pl.semaphore_wait(barrier, n_orb - 1 + (n_slab - 1) * half)
    for step in range(1, n_orb):
        tab_copy(step).start()
    for chunk in range(chunks):
        for step in range(1, n_orb):
            gather_copy(chunk, step).start()
        own_copy(chunk).start()
    tables[me] = tab_own[...]

    tab_all().wait_recv()
    to_scalars = pltpu.make_async_copy(tables, tab_s, tab_sem)
    to_scalars.start()
    to_scalars.wait()

    def count_block(block, total):
        starts[block] = total
        return lax.fori_loop(
            0, capacity, lambda k, sum_in: sum_in + (tab_s[block, 0, k] >= 0).astype(jnp.int32), total)

    live = lax.fori_loop(0, n_orb, count_block, jnp.int32(0))

    @pl.loop(0, slots)
    def _(slot):
        wanted = slot * groups + group
        used = wanted < live
        block = lax.fori_loop(
            1, n_orb, lambda b, sum_in: sum_in + (starts[b] <= wanted).astype(jnp.int32), jnp.int32(0))
        column = jnp.clip(wanted - starts[block], 0, capacity - 1)
        for k in range(3):
            ids[slot, k] = jnp.maximum(tab_s[block, k, column], 0)
        for k in range(2):
            ids[slot, 3 + k] = jnp.where(used, tab_s[block, k, column], -1)

    def pair_of(chunk, slot, span):
        left = held[chunk][ids[slot, 0], span].astype(f32)
        right = held[chunk][ids[slot, 1], span].astype(f32)
        crossed = ids[slot, 2] == 1
        return left, jnp.where(crossed, pltpu.roll(right, grid_len, 1), right), crossed

    def put_levels(ref, chunk, to, first):
        for k in range(slot_tiles - quota):
            ref[chunk, to, first + k] = whole(levels[chunk, to, k * tile:(k + 1) * tile])

    def take_units(ref, chunk, first):
        for src in range(members):
            for k in range(slot_tiles - quota):
                units[chunk, src, k * tile:(k + 1) * tile] = unit_of(plain(ref[chunk, src, first + k]))

    def advance(chunk):
        own_copy(chunk).wait()
        gather_all(chunk).wait_recv()

        def densities(which, base, keep):
            pairs = [pair_of(chunk, which * quota + base + k, slice(None)) for k in range(batch)]
            flat = depth_turn(jnp.concatenate([left * partner for left, partner, _ in pairs], axis=0),
                              depth_ref)
            done = left_turn([flat[k * grid_len:(k + 1) * grid_len] for k in range(2 * batch)], turn_ref)
            for k in range(batch):
                one = done[:, 2 * k * width:(2 * k + 1) * width] * gain[...]
                two = done[:, (2 * k + 1) * width:(2 * k + 2) * width] * gain[...]
                for band in range(bands):
                    to = taker(which, band)
                    span = slice(band * lines, (band + 1) * lines)
                    code, level = encode(jnp.concatenate([one[span], two[span]], axis=0))
                    fsend[chunk, to, base + k] = code
                    keep(to, base, k, level)

        def keep_level(to, base, k, level):
            levels[chunk, to, pl.ds(base + k, 1)] = level

        def keep_unit(to, base, k, level):
            funit[to, base // batch, k] = unit_of(level)

        if chunk < last:
            for which in range(sets):
                @pl.loop(0, quota, step=batch)
                def _(base):
                    densities(which, base, keep_level)

                for band in range(bands):
                    put_levels(fsend, chunk, taker(which, band), quota)
                for step in range(1, members):
                    to = member(step)[0]

                    @pl.when(to // half % sets == which)
                    def _():
                        fwd_copy(chunk, step).start()

            fwd_stay(chunk).start()
        else:
            for run in range(runs):
                for which in range(sets):
                    densities(which, run * batch, keep_unit)
                for step in range(1, members):
                    for copy in fwd_run(step, run):
                        copy.start()
                for copy in fwd_stay_run(run):
                    copy.start()

    for load in loads[1:]:
        load.wait()
    for chunk in range(chunks):
        advance(chunk)

    @pl.loop(0, slots)
    def _(slot):
        @pl.loop(0, couples)
        def _(couple):
            chosen[couple, slot] = jnp.where(
                ids[slot, 3] == couple, 2 * slot, jnp.where(ids[slot, 4] == couple, 2 * slot + 1, 2 * slots))

    for chunk in range(last):
        fwd_stay(chunk).wait()
        fwd_all(chunk).wait_recv()
        take_units(frecv, chunk, quota)

    for run in range(runs):
        base = run * batch
        for copy in fwd_stay_run(run):
            copy.wait()
        for copy in fwd_run_all(run):
            copy.wait_recv()
        for k in range(batch):
            for src in range(members):
                for chunk in range(chunks):
                    at = (src * chunks + chunk) * tile
                    unit = (units[chunk, src, pl.ds(base + k, 1)] if chunk < last
                            else funit_in[src, run, k])
                    work[k, at:at + tile] = decode(frecv[chunk, src, base + k], unit)
            done = left_turn([work[k, pl.ds(line, grid_len, stride=lines), :] for line in range(lines)],
                             turn_ref)
            done = done * kern[...]
            back = left_turn([done[:, line * width:(line + 1) * width] for line in range(lines)], turn_ref)
            for line in range(lines):
                turned[k, pl.ds(line, grid_len, stride=lines), :] = back[:, line * width:(line + 1) * width]
            for to in range(members):
                for chunk in range(chunks):
                    at = (to * chunks + chunk) * tile
                    code, level = encode(turned[k, at:at + tile])
                    bsend[chunk, to, slot_at(chunk, base + k)] = code
                    levels[chunk, to, pl.ds(base + k, 1)] = level

        if run < runs - 1:
            for chunk in range(last):
                for step in range(1, members):
                    back_copy(chunk, step, run).start()

    for chunk in range(chunks):
        for to in range(members):
            put_levels(bsend, chunk, to, 0 if chunk == last else quota)
        for run in range(0 if chunk == last else runs - 1, runs):
            for step in range(1, members):
                back_copy(chunk, step, run).start()
        back_stay(chunk).start()

    def retreat(chunk):
        def potentials_of(base):
            slots_at = [(which, base + k) for which in range(sets) for k in range(batch)]
            fields = []
            for which, slot in slots_at:
                blocks = [decode(brecv[chunk, taker(which, band), slot_at(chunk, slot)],
                                 units[chunk, taker(which, band), pl.ds(slot, 1)])
                          for band in range(bands)]
                for k in range(planes):
                    fields.append(jnp.concatenate([block[k * lines:(k + 1) * lines] for block in blocks],
                                                  axis=0))
            done = left_turn(fields, turn_ref)
            deep = depth_turn(jnp.concatenate(
                [done[:, k * width:(k + 1) * width] for k in range(len(fields))], axis=0), depth_ref)
            for k, (which, place_in) in enumerate(slots_at):
                slot = which * quota + place_in
                potential = deep[k * rows:(k + 1) * rows]
                left, partner, crossed = pair_of(chunk, slot, slice(None))
                terms[2 * slot] = potential * partner
                second = potential * left
                terms[2 * slot + 1] = jnp.where(crossed, pltpu.roll(second, grid_len, 1), second)

        back_stay(chunk).wait()
        if chunk < last:
            for run in range(runs):
                back_all(chunk, run).wait_recv()
            take_units(brecv, chunk, quota)

            @pl.loop(0, quota, step=batch)
            def _(base):
                potentials_of(base)
        else:
            back_all(chunk, 0).wait_recv()
            take_units(brecv, chunk, 0)
            potentials_of(0)

            for run in range(1, runs):
                back_all(chunk, run).wait_recv()
                potentials_of(run * batch)

    def finish(plane):
        chunk = plane // planes
        span = slice(plane % planes * grid_len, (plane % planes + 1) * grid_len)

        @pl.loop(0, couples)
        def _(couple):
            total = terms[chosen[couple, 0], span]
            for slot in range(1, slots):
                total = total + terms[chosen[couple, slot], span]
            parts[plane, couple] = total
            code, level = encode(total)
            rsend[plane, couple] = code
            runit[plane, couple] = unit_of(level)

    def send_sums(plane):
        for step in range(1, groups):
            for copy in sum_copies(plane, step):
                copy.start()

    def project(plane):
        chunk = plane // planes
        span = slice(plane % planes * grid_len, (plane % planes + 1) * grid_len)

        @pl.loop(0, couples)
        def _(couple):
            total = parts[plane, couple]
            across = pltpu.roll(total, grid_len, 1)
            at = couple % shared * couples
            for other in range(couples):
                basis = held[chunk][other, span].astype(f32)
                for kind, field in enumerate((total, across)):
                    row = pl.ds(at + kind * shared * couples + other, 1)
                    overlap[couple // shared, row] += jnp.sum(basis * field, axis=0, keepdims=True)

    for plane in range(own_planes):
        if plane % planes == 0:
            retreat(plane // planes)
        finish(plane)
        if plane < own_planes - 1:
            send_sums(plane)
        if plane < own_planes - planes:
            project(plane)
    for plane in range(own_planes - planes, own_planes):
        project(plane)

    lane = lax.broadcasted_iota(jnp.int32, (8, width), 1)
    halves = ((lane // grid_len) == lax.broadcasted_iota(jnp.int32, (8, width), 0)).astype(jnp.bfloat16)

    def thirds(values):
        high = values.astype(jnp.bfloat16)
        rest = values - high.astype(f32)
        mid = rest.astype(jnp.bfloat16)
        return high, mid, (rest - mid.astype(f32)).astype(jnp.bfloat16)

    for which in range(groups):
        packed[which] = sum(lax.dot_general(halves, third, (((1,), (1,)), ((), ())),
                                            preferred_element_type=f32)
                            for third in thirds(overlap[which]))
    for step in range(1, groups):
        overlap_copy(step).start()
    total = packed[group]
    overlap_all().wait_recv()
    for step in range(1, groups):
        total = total + packed_in[step - 1]
    merged[...] = total
    for step in range(1, members):
        merged_copy(step).start()
    for step in range(1, groups):
        for copy in sum_copies(own_planes - 1, step):
            copy.start()
    merged_all().wait_recv()
    for step in range(1, members):
        total = total + merged_in[step - 1]
    total = total * (1.0 / (grid_len * grid_len * grid_len))
    coef[...] = sum(lax.dot_general(third, halves, (((0,), (0,)), ((), ())), preferred_element_type=f32)
                    for third in thirds(total))

    strip = grid_len // 2
    for plane in range(own_planes):
        chunk, first = plane // planes, plane % planes * grid_len
        for copy in sum_all(plane):
            copy.wait_recv()

        @pl.loop(0, grid_len // strip)
        def _(at):
            here = pl.ds(pl.multiple_of(at * strip, strip), strip)
            there = pl.ds(pl.multiple_of(first + at * strip, strip), strip)
            kept = [jnp.zeros((strip, width), f32) for _ in range(2 * shared)]
            for couple in range(couples):
                basis = held[chunk][couple, there].astype(f32)
                for k in range(2 * shared):
                    row = k * couples + couple
                    kept[k] = kept[k] + coef[row:row + 1] * basis
            for k in range(shared):
                total = parts[plane, group * shared + k, here]
                for step in range(1, groups):
                    total = total + decode(rrecv[plane, step - 1, k, here], rrunit[plane, step - 1, k])
                result[k, here] = total - kept[k] - pltpu.roll(kept[shared + k], grid_len, 1)

        for k in range(shared):
            code, level = encode(result[k])
            ysend[plane, k] = code
            yunit[plane, k] = unit_of(level)
        for hop in range(1, half):
            for copy in result_copies(plane, hop):
                copy.start()
        for copy in result_stay(plane):
            copy.start()

    for plane in range(own_planes):
        for copy in result_stay(plane):
            copy.wait()
        for copy in sum_all(plane):
            copy.wait_send()
    if half > 1:
        for copy in result_all():
            copy.wait()
    for run in range(runs):
        for copy in fwd_run_all(run):
            copy.wait_send()
    for chunk in range(chunks):
        if chunk < last:
            fwd_all(chunk).wait_send()
        for run in range(runs):
            back_all(chunk, run).wait_send()
        gather_all(chunk).wait_send()
    overlap_all().wait_send()
    merged_all().wait_send()
    tab_all().wait_send()


def local(orbitals, pair_table, n_orb, n_slab):
    own_couples, slab_len, grid_len, width = orbitals.shape
    capacity = pair_table.shape[0]
    half = max(1, cube // n_slab)
    members = n_slab * half
    groups = n_orb // half
    bands = grid_len // lines_own
    sets = members // bands
    live_total = sum(capacity * (k + 1) // n_orb for k in range(n_orb))
    quota = -(-live_total // (groups * sets * batch)) * batch
    slots = sets * quota
    couples, shared = n_orb * own_couples, half * own_couples
    planes = grid_len // members
    chunks = planes // 2
    rows, tile = 2 * grid_len, 2 * lines_own
    level_tiles = -(-quota // tile)
    overlap_rows = -(-2 * shared * couples // 128) * 128
    tab_lanes = -(-capacity // 128) * 128

    mat = hartley(grid_len)
    mat_high, mat_low = split_const(mat)
    turn_mat = jnp.asarray(np.concatenate([mat_high, mat_high, mat_low], axis=1))
    deep_high, deep_low = split_const(np.kron(np.eye(2, dtype=np.float32), mat))
    depth_mat = jnp.asarray(np.block([[deep_high, deep_low], [deep_high, np.zeros_like(deep_low)]]))

    dma, vmem, smem = pltpu.SemaphoreType.DMA, pltpu.VMEM, pltpu.SMEM
    i32, i16 = jnp.int32, jnp.int16
    bf16 = orbitals.dtype
    coded = vmem((chunks, members, quota + level_tiles, tile, width), i16)
    runs = quota // batch
    small_units = vmem((members, runs, batch, 1, width), f32)
    per_slot = vmem((chunks, members, level_tiles * tile, width), f32)
    steps = max(groups - 1, 1)
    code, unit = pl.pallas_call(
        functools.partial(action_kernel, n_orb, n_slab, half, quota, chunks, grid_len),
        out_shape=(jax.ShapeDtypeStruct((own_couples, slab_len * grid_len, width), i16),
                   jax.ShapeDtypeStruct((own_couples, slab_len, 1, width), f32)),
        in_specs=[HBM_SPEC] * 4,
        out_specs=(HBM_SPEC, HBM_SPEC),
        scratch_shapes=[vmem((couples, rows, width), orbitals.dtype)] * chunks + [
            vmem((3, capacity), i32), vmem(depth_mat.shape, bf16), vmem(turn_mat.shape, bf16),
            vmem((8, tab_lanes), i32), vmem((n_orb, 8, tab_lanes), i32), smem((n_orb, 8, tab_lanes), i32),
            smem((n_orb,), i32), smem((slots, 5), i32), smem((couples, slots), i32),
            vmem((grid_len, width), f32), vmem((grid_len, lines_own * width), f32),
            per_slot, coded, coded, small_units, small_units, per_slot,
            vmem((batch, lines_own * grid_len, width), f32), vmem((batch, lines_own * grid_len, width), f32),
            coded, coded,
            vmem((2 * slots + 1, rows, width), f32),
            vmem((planes, couples, grid_len, width), f32),
            vmem((planes, couples, grid_len, width), i16), vmem((planes, couples, 1, width), f32),
            vmem((planes, steps, shared, grid_len, width), i16), vmem((planes, steps, shared, 1, width), f32),
            vmem((groups, overlap_rows, width), f32), vmem((groups, 8, overlap_rows), f32),
            vmem((steps, 8, overlap_rows), f32), vmem((8, overlap_rows), f32),
            vmem((members - 1, 8, overlap_rows), f32), vmem((overlap_rows, width), f32),
            vmem((shared, grid_len, width), f32),
            vmem((planes, shared, grid_len, width), i16), vmem((planes, shared, 1, width), f32),
            dma((3,)), dma((2, planes)), dma, dma, dma, dma((chunks,)), dma((chunks,)), dma((chunks,)),
            dma((chunks - 1 + 2 * runs,)), dma((chunks - 1 + runs,)), dma((chunks - 1 + runs,)),
            dma((runs,)), dma((runs,)), dma((chunks,)), dma((runs * chunks,)), dma((runs * chunks,)),
            dma((2, planes)), dma((2, planes)), dma, dma, dma, dma, dma((2,)), dma((2,)),
        ],
        compiler_params=pltpu.CompilerParams(collective_id=0, has_side_effects=True,
                                             vmem_limit_bytes=56 << 20),
    )(pair_table.T, orbitals.reshape(own_couples, slab_len * grid_len, width), depth_mat, turn_mat)
    return code.reshape(orbitals.shape).astype(f32) * unit


def solution(mesh):
    placed = (P("orb", "slab", None, None), P("orb", None))
    return jax.shard_map(
        functools.partial(local, n_orb=mesh.shape["orb"], n_slab=mesh.shape["slab"]),
        mesh=mesh, in_specs=placed, out_specs=P("orb", "slab", None, None), check_vma=False
    )
```
